256 devices in a mesh: depth: 64 (over x, y, z_hi), comp: 4 (over z_lo, core).
Axes of the slice: x: 4, y: 4, z: 8 (z_hi: 4, z_lo: 2; z = z_hi * 2 + z_lo), core: 2. Of those that a mesh axis runs over, the one named last changes fastest.
Arguments:
- density: float32 [64, 512, 256], P('depth', 'comp'), may hold values from -4 to 4
- observed: float32 [4, 512, 256], P('comp', 'depth'), may hold values from -6 to 6
- data_weight: float32 [4, 512, 256], P('comp', 'depth'), may hold values from 0.3 to 7.5
- layer_top: float32 [64], P('depth'), may hold values from 0.5 to 8
Outputs:
- density_new: float32 [64, 512, 256], P('depth', 'comp')
- weighted_error: float32 [4, 512, 256], P('comp', 'depth')
The draws below stay inside these ranges and needn't reach their ends.
All inputs are finite; a program needn't handle non-finite values.
Results may differ from the reference program's by a relative error of at most 0.0001.
Values sent between devices are 32-bit elements; how exact they have to be, the bound alone decides.
No kernel may reach another device: no remote copies, remote signals or barrier semaphores. Data moves between devices by JAX's collectives and lax.ppermute only.
A program may use at most 64 MiB of HBM per device.

```python
import math
import jax
import jax.numpy as jnp
from jax import lax

NX = 512
NY = 256
COMP = 4
ITERS = 2
LAYERS = 64


def draw_data_weight(key, part):
    rows = jnp.arange(NX, dtype=jnp.float32)[None, :, None] / NX
    comps = jnp.arange(COMP, dtype=jnp.float32)[:, None, None] / COMP
    place = 0.8 * rows + 0.2 * comps
    rise = jnp.exp(math.log(4.0) * place)
    rough = jnp.exp(jax.random.uniform(key, (COMP, NX, NY), jnp.float32, math.log(0.7), math.log(1.4)))
    return (0.5 * rise * rough).astype(jnp.float32)


def steps_of(key, shape, shards, low, largest):
    loudness = 1.0
    for position, shards_of in shards:
        steps = jax.random.uniform(jax.random.fold_in(jax.random.fold_in(key, 6), position), (shards_of,), jnp.float32, low / len(shards), largest / len(shards))
        loudness = loudness * jnp.repeat(jnp.exp(steps), shape[position] // shards_of).reshape((-1,) + (1,) * (len(shape) - 1 - position))
    return loudness


def gaussian(own_key, shape, width, most, shards=(), kind=jnp.bfloat16):
    values = jax.random.normal(own_key, shape, jnp.float32) * width
    if len(shards) > 0:
        values = steps_of(own_key, shape, shards, -0.22, 0.18) * values
    return jnp.clip(values, min=-most, max=most).astype(kind)


def setup_inputs(seed: int = 0) -> dict:
    arg_keys = jax.random.split(jax.random.key(seed), 5)
    density = gaussian(arg_keys[0], (LAYERS, NX, NY), 0.5, 4.0, ((0, 64), (1, 4)), jnp.float32)
    observed = gaussian(arg_keys[1], (COMP, NX, NY), 1.0, 6.0, ((0, 4), (1, 64)), jnp.float32)
    data_weight = draw_data_weight(jax.random.fold_in(arg_keys[4], 71), 0)
    layer_top = jnp.clip(jnp.exp(math.log(8.0) - 2.7725887 * jax.random.uniform(arg_keys[3], (LAYERS,), jnp.float32) ** steps_of(arg_keys[3], (LAYERS,), ((0, 64),), -0.2, 0.2)), 0.5, 8.0)
    return dict(density=density, observed=observed, data_weight=data_weight, layer_top=layer_top)


TWO_PI = 2.0 * math.pi

def kernel_parts(top, comp_index):
    kx = (jnp.fft.fftfreq(NX) * TWO_PI).astype(jnp.float32)[:, None]
    ky = (jnp.fft.fftfreq(NY) * TWO_PI).astype(jnp.float32)[None, :]
    kabs = jnp.sqrt(kx * kx + ky * ky)
    floor_k = jnp.maximum(kabs, TWO_PI / max(NX, NY))
    decay = 4.0 * jnp.exp(-kabs * top) * (1.0 - jnp.exp(-kabs))
    zeros = jnp.zeros_like(kabs)
    if comp_index == 0:
        return (decay, zeros)
    if comp_index == 1:
        return (zeros, decay * (kx / floor_k))
    if comp_index == 2:
        return (zeros, decay * (ky / floor_k))
    return (decay * (-(kx * kx) / (floor_k * floor_k)), zeros)

def forward(layers, tops):

    def step(carry, item):
        layer, top = item
        spec = jnp.fft.fft2(layer)
        outs = []
        for comp in range(COMP):
            kre, kim = kernel_parts(top, comp)
            outs.append(jnp.real(jnp.fft.ifft2(lax.complex(kre, kim) * spec)))
        return (carry + jnp.stack(outs).astype(carry.dtype), None)
    start = jnp.zeros((COMP, NX, NY), jnp.float32)
    total, unused = lax.scan(step, start, (layers, tops))
    return total

def adjoint(planes, tops):
    specs = jnp.fft.fft2(planes, axes=(1, 2))

    def one(top):
        total = jnp.zeros((NX, NY), jnp.float32)
        for comp in range(COMP):
            kre, kim = kernel_parts(top, comp)
            term = jnp.real(jnp.fft.ifft2(lax.complex(kre, -kim) * specs[comp]))
            total = total + term.astype(total.dtype)
        return total
    return lax.map(one, tops)

def reference(density, observed, data_weight, layer_top):
    dens = density
    predicted = forward(dens, layer_top)
    weighted_error = data_weight * (predicted - observed)
    for step in range(ITERS):
        quad = 1.0 / (dens * dens + 0.25)
        grad = adjoint(data_weight * weighted_error, layer_top) + 0.5 * (quad * dens)
        image = forward(grad, layer_top)
        grad_sq = jnp.sum(grad * grad)
        quad_sq = jnp.sum(quad * grad * grad)
        weighted_image = data_weight * image
        curv = jnp.sum(weighted_image * weighted_image)
        alpha = grad_sq / (curv + 0.5 * quad_sq)
        dens = dens - alpha * grad
        predicted = predicted - alpha * image
        weighted_error = data_weight * (predicted - observed)
    return (dens, weighted_error)
```

```python
import functools
import math

import jax
import jax.numpy as jnp
import numpy as np
from jax import lax
from jax.experimental import pallas as pl
from jax.experimental.pallas import tpu as pltpu
from jax.sharding import Mesh
from jax.sharding import PartitionSpec as P

TWO_PI = 2.0 * math.pi
F32 = jnp.float32
BF16 = jnp.bfloat16
XY = ("x", "y")
DEPTH = ("x", "y", "h")
COMP = ("l", "k")
ALL = ("x", "y", "h", "l", "k")

NX = 512
NY = 256
HX = NX // 2
QX = NX // 4
HY = NY // 2


def split_table(table):
    high = table.astype(jnp.bfloat16)
    low = (table - high.astype(np.float64)).astype(jnp.bfloat16)
    return np.stack([high, low])


def basis(count, waves):
    place = np.arange(count)
    rows = []
    for wave in waves:
        norm = math.sqrt((1.0 if wave == 0 else 2.0) / count)
        rows.append(norm * np.cos(TWO_PI * (wave * place % count) / count))
    for wave in waves:
        if wave == 0:
            rows.append(math.sqrt(1.0 / count) * (1.0 - 2.0 * (place % 2)))
        else:
            rows.append(math.sqrt(2.0 / count) * np.sin(TWO_PI * (wave * place % count) / count))
    return np.stack(rows)


def make_tables():
    even = basis(NX, range(0, HX, 2))[:, :HX]
    odd = basis(NX, range(1, HX, 2))[:, :HX]
    col = basis(NY, range(HY))
    return (
        np.concatenate([split_table(even), split_table(odd)]),
        np.concatenate([split_table(even.T), split_table(odd.T)]),
        np.concatenate([split_table(col.T), split_table(col)]),
    )


def split(value):
    high = value.astype(BF16)
    low = (value - high.astype(F32)).astype(BF16)
    return high, low


def dot(left, right):
    return jnp.dot(left, right, preferred_element_type=F32)


def times_table(value, high, low):
    vh, vl = split(value)
    return dot(vh, high) + (dot(vl, high) + dot(vh, low))


def table_times(high, low, value):
    vh, vl = split(value)
    return dot(high, vh) + (dot(high, vl) + dot(low, vh))


def to_waves(field, fx, ty):
    cols = times_table(field, ty[0], ty[1])
    upper, lower = cols[:HX], cols[HX:]
    return (
        table_times(fx[0], fx[1], upper + lower),
        table_times(fx[2], fx[3], upper - lower),
    )


def from_waves(even, odd, bx, ty):
    first = table_times(bx[0], bx[1], even)
    second = table_times(bx[2], bx[3], odd)
    rows = jnp.concatenate([first + second, first - second], axis=0)
    return times_table(rows, ty[2], ty[3])


def swap_x(half):
    return jnp.concatenate([half[HX // 2 :], half[: HX // 2]], axis=0)


def swap_y(half):
    return jnp.concatenate([half[:, HY:], half[:, :HY]], axis=1)


def component(even, odd, own, comp):
    def one(half, coefficients):
        met = jnp.where(comp == 1, swap_x(half), jnp.where(comp == 2, swap_y(half), half))
        return met * coefficients

    return one(even, own[:HX]), one(odd, own[HX:])


def comp_index():
    return lax.axis_index("l") * 2 + lax.axis_index("k")


def wave_grid(rows):
    shape = (rows, NY)
    row = lax.broadcasted_iota(jnp.int32, shape, 0)
    col = lax.broadcasted_iota(jnp.int32, shape, 1)
    odd = (row >= HX).astype(jnp.int32)
    slot = row % QX
    wave_x = 2 * slot + odd
    sine_x = (row % HX) >= QX
    nyquist_x = sine_x & (wave_x == 0)
    wave_x = jnp.where(nyquist_x, HX, wave_x)
    wave_y = col % HY
    sine_y = col >= HY
    nyquist_y = sine_y & (wave_y == 0)
    wave_y = jnp.where(nyquist_y, HY, wave_y)
    kx = wave_x.astype(F32) * (TWO_PI / NX)
    ky = wave_y.astype(F32) * (TWO_PI / NY)
    return kx, ky, sine_x, sine_y, nyquist_x, nyquist_y


def prepare_kernel(top_ref, decay_ref, own_ref, factors_ref):
    comp = comp_index()
    kx, ky, sine_x, sine_y, nyquist_x, nyquist_y = wave_grid(NX)
    kabs = jnp.sqrt(kx * kx + ky * ky)
    inverse = 1.0 / jnp.maximum(kabs, TWO_PI / max(NX, NY))
    decay_ref[...] = 4.0 * jnp.exp(-kabs * top_ref[0]) * (1.0 - jnp.exp(-kabs))
    rx = kx * inverse
    ry = ky * inverse
    first = jnp.where(nyquist_x, 0.0, jnp.where(sine_x, -rx, rx))
    second = jnp.where(nyquist_y, 0.0, jnp.where(sine_y, -ry, ry))
    third = -(rx * rx)
    factors_ref[0] = first
    factors_ref[1] = second
    factors_ref[2] = third
    own_ref[...] = jnp.where(
        comp == 0, 1.0, jnp.where(comp == 1, first, jnp.where(comp == 2, second, third))
    )


def gather_rows(pieces, full_ref):
    comp = comp_index()
    for step, piece in enumerate(pieces):
        full_ref[pl.ds(pl.multiple_of(jnp.bitwise_xor(comp, step) * QX, QX), QX), :] = piece[...]


def start_kernel(
    nxy, m0, m1, m2, m3, top_ref, decay_ref, own_ref, fx, bx, ty, out_ref, full_ref
):
    rows = NX // nxy
    comp = comp_index()
    gather_rows((m0, m1, m2, m3), full_ref)
    dens = full_ref[...]
    pull = 0.5 * (dens * (1.0 / (dens * dens + 0.25)))
    for place, field in enumerate((dens, pull)):
        even, odd = to_waves(field, fx, ty)
        even, odd = component(even * decay_ref[:HX], odd * decay_ref[HX:], own_ref, comp)
        plane = from_waves(even, odd, bx, ty)
        for target in range(nxy):
            out_ref[target, place * rows : (place + 1) * rows, :] = plane[
                target * rows : (target + 1) * rows
            ]
    for target in range(nxy):
        out_ref[target, 2 * rows : 2 * rows + 8, :] = jnp.full((8, NY), top_ref[0], F32)


def collect_kernel(nxy, got_ref, sum_ref, pull_ref):
    rows = NX // nxy
    total = got_ref[0, : 2 * rows, :]
    for source in range(1, nxy):
        total = total + got_ref[source, : 2 * rows, :]
    sum_ref[:rows] = total[:rows]
    pull_ref[...] = total[rows:]
    for source in range(nxy):
        sum_ref[rows + source : rows + source + 1, :] = got_ref[source, 2 * rows : 2 * rows + 1, :]


def residual_kernel(nxy, nh, *refs):
    rows = NX // nxy
    part = rows // nh
    sums = refs[:nh]
    data = refs[nh : 2 * nh]
    pred_ref, weight_ref, tops_ref, send_ref = refs[2 * nh : 2 * nh + 4]
    meas_ref = refs[2 * nh + 4]
    chip = lax.axis_index("h")
    total = sums[0][:rows]
    for step in range(1, nh):
        total = total + sums[step][:rows]
    for step in range(nh):
        tops_ref[step * nxy : (step + 1) * nxy] = sums[step][rows:]
        place = pl.ds(pl.multiple_of(lax.rem(chip + (nh - step), nh) * part, part), part)
        weight_ref[place, :] = data[step][:part]
        meas_ref[place, :] = data[step][part:]
    weight = weight_ref[...]
    pred_ref[...] = total
    res = weight * (weight * (total - meas_ref[...]))
    for target in range(nxy):
        send_ref[target] = res


def power_kernel(layers, tops_ref, power_ref):
    kx, ky, *_ = wave_grid(NX)
    for start in range(0, NX, 64):
        ks = jnp.sqrt(kx[start : start + 64] ** 2 + ky[start : start + 64] ** 2)
        double = -2.0 * ks

        def add(layer, total):
            return total + jnp.exp(double * tops_ref[pl.ds(layer, 1), :])

        total = lax.fori_loop(0, layers, add, jnp.zeros_like(ks))
        rise = 1.0 - jnp.exp(-ks)
        power_ref[start : start + 64] = (16.0 * (rise * rise)) * total


def adjoint_kernel(
    nxy, res_ref, decay_ref, own_ref, power_ref, factors_ref, fx, bx, ty, o0, o1, o2, o3, z_ref, i_ref
):
    rows = NX // nxy
    comp = comp_index()
    res = res_ref[...].reshape(NX, NY)
    even, odd = to_waves(res, fx, ty)
    even, odd = component(even, odd, own_ref, comp)
    sign = jnp.where((comp == 1) | (comp == 2), -1.0, 1.0)
    even = even * sign
    odd = odd * sign
    z_ref[...] = from_waves(even * decay_ref[:HX], odd * decay_ref[HX:], bx, ty)
    even = even * power_ref[:HX]
    odd = odd * power_ref[HX:]
    block = lax.axis_index("x") * lax.axis_size("y") + lax.axis_index("y")
    upper = block * rows < HX
    begin = pl.multiple_of(lax.rem(block * rows, HX), rows)
    near = pl.ds(begin, rows)
    flip = jnp.where(upper, 1.0, -1.0)
    for target in range(4):
        if target == 0:
            e, o = even, odd
        elif target == 1:
            e, o = swap_x(even) * factors_ref[0, :HX], swap_x(odd) * factors_ref[0, HX:]
        elif target == 2:
            e, o = swap_y(even) * factors_ref[1, :HX], swap_y(odd) * factors_ref[1, HX:]
        else:
            e, o = even * factors_ref[2, :HX], odd * factors_ref[2, HX:]
        line = table_times(bx[0, near, :], bx[1, near, :], e)
        line = line + flip * table_times(bx[2, near, :], bx[3, near, :], o)
        i_ref[target * rows : (target + 1) * rows, :] = line
    i_ref[...] = times_table(i_ref[...], ty[2], ty[3])
    for step, out in enumerate((o0, o1, o2, o3)):
        other = jnp.bitwise_xor(comp, step)
        out[:QX] = z_ref[pl.ds(pl.multiple_of(other * QX, QX), QX), :]
        out[QX:] = i_ref[pl.ds(pl.multiple_of(other * rows, rows), rows), :]


def share(grad, quad, image, weight, scratch, part):
    scratch[...] = weight * image
    place = pl.ds(pl.multiple_of(lax.axis_index("h") * part, part), part)
    mine = scratch[place, :]
    lane = lax.broadcasted_iota(jnp.int32, (1, 128), 1)
    square = grad * grad
    gg = jnp.sum(square)
    qgg = jnp.sum(quad * square)
    curv = jnp.sum(mine * mine)
    return jnp.where(lane == 0, gg, jnp.where(lane == 1, qgg, jnp.where(lane == 2, curv, 0.0)))


def step_length(shares):
    total = jnp.sum(shares, axis=0, keepdims=True)
    lane = lax.broadcasted_iota(jnp.int32, total.shape, 1)
    pick = lambda place: jnp.sum(jnp.where(lane == place, total, 0.0), keepdims=True)
    return pick(0) / (pick(2) + 0.5 * pick(1))


def gradient_kernel(nxy, nh, *refs):
    rows = NX // nxy
    part = rows // nh
    pieces = refs[:4]
    pulls = refs[4 : 4 + nh]
    dens_ref, weight_ref = refs[4 + nh : 6 + nh]
    share_ref, send_ref, data_ref, grad_ref, line_ref, image_ref, scratch = refs[6 + nh :]
    total = pieces[0][...] + pieces[1][...] + (pieces[2][...] + pieces[3][...])
    data = total[:QX]
    line = total[QX:]
    dens = dens_ref[0]
    quad = 1.0 / (dens * dens + 0.25)
    grad = data + 0.5 * (quad * dens)
    pulled = pulls[0][...]
    for step in range(1, nh):
        pulled = pulled + pulls[step][...]
    image = line + pulled
    weight = weight_ref[...]
    share_ref[...] = jnp.broadcast_to(
        share(grad, quad, image, weight, scratch, part), share_ref.shape
    )
    data_ref[...] = data
    grad_ref[...] = grad
    line_ref[...] = line
    image_ref[...] = image
    back = weight * (weight * image)
    for target in range(nxy):
        send_ref[target] = back


def move_kernel(shares_ref, dens_ref, grad_ref, dens_out, pull_out, alpha_ref):
    alpha = step_length(shares_ref[...])
    dens = dens_ref[0] - alpha * grad_ref[...]
    dens_out[...] = dens
    pull_out[...] = 0.5 * (dens * (1.0 / (dens * dens + 0.25)))
    alpha_ref[...] = jnp.broadcast_to(alpha, alpha_ref.shape)


def second_kernel(nxy, p0, p1, p2, p3, decay_ref, own_ref, fx, bx, ty, out_ref, full_ref):
    comp = comp_index()
    gather_rows((p0, p1, p2, p3), full_ref)
    even, odd = to_waves(full_ref[...], fx, ty)
    even, odd = component(even * decay_ref[:HX], odd * decay_ref[HX:], own_ref, comp)
    out_ref[...] = from_waves(even, odd, bx, ty).reshape(out_ref.shape)


def sum_kernel(nxy, got_ref, sum_ref):
    total = got_ref[0]
    for source in range(1, nxy):
        total = total + got_ref[source]
    sum_ref[...] = total


def second_gradient_kernel(
    u0, u1, u2, u3, alpha_ref, data_ref, pull_ref, dens_ref, line_ref, grad_ref, image_ref, share_ref
):
    alpha = alpha_ref[:1, :1]
    total = u0[...] + u1[...] + (u2[...] + u3[...])
    dens = dens_ref[...]
    grad = data_ref[...] - alpha * total[:QX] + pull_ref[...]
    quad = 1.0 / (dens * dens + 0.25)
    grad_ref[...] = grad
    image_ref[...] = line_ref[...] - alpha * total[QX:]
    square = grad * grad
    lane = lax.broadcasted_iota(jnp.int32, (8, 128), 1)
    share_ref[...] = jnp.where(
        lane == 0, jnp.sum(square), jnp.where(lane == 1, jnp.sum(quad * square), 0.0)
    )


def curvature_kernel(nxy, nh, *refs):
    rows = NX // nxy
    part = rows // nh
    pulls = refs[:nh]
    image_ref, weight_ref, part_ref, share_ref, out_ref, scratch = refs[nh:]
    image = image_ref[...]
    for step in range(nh):
        image = image + pulls[step][...]
    out_ref[...] = image
    scratch[...] = weight_ref[...] * image
    mine = scratch[pl.ds(pl.multiple_of(lax.axis_index("h") * part, part), part), :]
    lane = lax.broadcasted_iota(jnp.int32, (1, 128), 1)
    share_ref[...] = jnp.broadcast_to(
        jnp.where(lane == 2, jnp.sum(mine * mine), part_ref[:1]), share_ref.shape
    )


def finish_kernel(
    shares_ref, dens_ref, grad_ref, alpha_ref, pred_ref, first_ref, second_ref, obs_ref, w_ref, dens_out, err_out
):
    part = obs_ref.shape[1]
    alpha = step_length(shares_ref[...])
    dens_out[0] = dens_ref[...] - alpha * grad_ref[...]
    place = pl.ds(pl.multiple_of(lax.axis_index("h") * part, part), part)
    pred = pred_ref[place, :] - alpha_ref[:1, :1] * first_ref[place, :]
    pred = pred - alpha * second_ref[place, :]
    err_out[0] = w_ref[0] * (pred - obs_ref[0])


VMEM = pl.BlockSpec(memory_space=pltpu.VMEM)
SMEM = pl.BlockSpec(memory_space=pltpu.SMEM)


def call(kernel, outs, *args, scratch=(), scalars=()):
    shapes = [jax.ShapeDtypeStruct(shape, F32) for shape in outs]
    return pl.pallas_call(
        kernel,
        out_shape=shapes,
        in_specs=[SMEM if place in scalars else VMEM for place in range(len(args))],
        out_specs=[VMEM] * len(outs),
        scratch_shapes=[pltpu.VMEM(shape, F32) for shape in scratch],
    )(*args)


def from_comps(values):
    return [values[0]] + [
        lax.ppermute(values[step], COMP, [(i, i ^ step) for i in range(4)]) for step in (1, 2, 3)
    ]


def from_chips(value, nh):
    return [value] + [
        lax.ppermute(value, "h", [(i, (i + step) % nh) for i in range(nh)]) for step in range(1, nh)
    ]


def exchange(value, axes):
    return lax.all_to_all(value, axes, 0, 0, tiled=True)


def after(value, *others):
    return lax.optimization_barrier((value, *others))[0]


def body(density, observed, data_weight, layer_top):
    nxy = lax.axis_size("x") * lax.axis_size("y")
    nh = lax.axis_size("h")
    devices = nxy * nh * 4
    rows = NX // nxy
    fx, bx, ty = (jnp.asarray(table) for table in make_tables())
    bind = functools.partial

    decay, own, factors = call(
        prepare_kernel, [(NX, NY), (NX, NY), (3, NX, NY)], layer_top, scalars=(0,)
    )
    strip = density[0]
    layers = from_comps([strip] * 4)
    (message,) = call(
        bind(start_kernel, nxy),
        [(nxy, 2 * rows + 8, NY)],
        *layers, layer_top, decay, own, fx, bx, ty,
        scratch=[(NX, NY)], scalars=(4,),
    )
    data = from_chips(jnp.concatenate([data_weight[0], observed[0]], axis=0), nh)
    got = exchange(message, XY)
    sums, pulled = call(bind(collect_kernel, nxy), [(rows + nxy, NY), (rows, NY)], got)
    sums = from_chips(sums, nh)
    pred, weight, tops, message = call(
        bind(residual_kernel, nxy, nh),
        [(rows, NY), (rows, NY), (nxy * nh, NY), (nxy, rows, NY)],
        *sums, *data, scratch=[(rows, NY)],
    )
    got = exchange(message, XY)
    pulls = from_chips(after(pulled, message), nh)
    (power,) = call(bind(power_kernel, nxy * nh), [(NX, NY)], tops)
    adjoint = lambda plane: from_comps(
        call(
            bind(adjoint_kernel, nxy),
            [(QX + rows, NY)] * 4,
            plane, decay, own, power, factors, fx, bx, ty,
            scratch=[(NX, NY), (4 * rows, NY)],
        )
    )
    pieces = adjoint(got)
    shares, message, data_grad, grad, line, image = call(
        bind(gradient_kernel, nxy, nh),
        [(devices, 128), (nxy, rows, NY), (QX, NY), (QX, NY), (rows, NY), (rows, NY)],
        *pieces, *pulls, density, weight, scratch=[(rows, NY)],
    )
    shares = exchange(shares, ALL)
    dens, pull, alpha = call(
        move_kernel, [(QX, NY), (QX, NY), (8, 128)], shares, density, grad
    )
    back = exchange(after(message, pull), XY)
    pull_full = from_comps([pull] * 4)
    (message,) = call(
        bind(second_kernel, nxy), [(nxy, rows, NY)],
        *pull_full, decay, own, fx, bx, ty, scratch=[(NX, NY)],
    )
    got = exchange(message, XY)
    pieces = adjoint(back)
    grad2, image2, half = call(
        second_gradient_kernel, [(QX, NY), (rows, NY), (8, 128)],
        *pieces, alpha, data_grad, pull, dens, line,
    )
    (pulled,) = call(bind(sum_kernel, nxy), [(rows, NY)], got)
    pulls = from_chips(pulled, nh)
    shares, image2 = call(
        bind(curvature_kernel, nxy, nh), [(devices, 128), (rows, NY)],
        *pulls, image2, weight, half, scratch=[(rows, NY)],
    )
    shares = exchange(shares, ALL)
    return tuple(
        call(
            finish_kernel, [density.shape, observed.shape],
            shares, dens, grad2, alpha, pred, image, image2, observed, data_weight,
        )
    )


def solution(mesh):
    depth = mesh.shape["depth"]
    sizes = {64: (4, 4, 4), 4: (2, 1, 2)}[depth]
    fine = Mesh(mesh.devices.reshape(*sizes, 2, 2), ALL)
    data = P(COMP, DEPTH, None)
    layer = P(DEPTH, COMP, None)
    return jax.shard_map(
        body,
        mesh=fine,
        in_specs=(layer, data, data, P(DEPTH)),
        out_specs=(layer, data),
        check_vma=False,
    )
```

```python
import functools
import math

import jax
import jax.numpy as jnp
import numpy as np
from jax import lax
from jax.experimental import pallas as pl
from jax.experimental.pallas import tpu as pltpu
from jax.sharding import Mesh
from jax.sharding import PartitionSpec as P

TWO_PI = 2.0 * math.pi
F32 = jnp.float32
BF16 = jnp.bfloat16
XY = ("x", "y")
DEPTH = ("x", "y", "h")
COMP = ("l", "k")
ALL = ("x", "y", "h", "l", "k")

NX = 512
NY = 256
HX = NX // 2
QX = NX // 4
HY = NY // 2


def split_table(table):
    high = table.astype(jnp.bfloat16)
    low = (table - high.astype(np.float64)).astype(jnp.bfloat16)
    return np.stack([high, low])


def basis(count, waves):
    place = np.arange(count)
    rows = []
    for wave in waves:
        norm = math.sqrt((1.0 if wave == 0 else 2.0) / count)
        rows.append(norm * np.cos(TWO_PI * (wave * place % count) / count))
    for wave in waves:
        if wave == 0:
            rows.append(math.sqrt(1.0 / count) * (1.0 - 2.0 * (place % 2)))
        else:
            rows.append(math.sqrt(2.0 / count) * np.sin(TWO_PI * (wave * place % count) / count))
    return np.stack(rows)


def make_tables():
    even = basis(NX, range(0, HX, 2))[:, :HX]
    odd = basis(NX, range(1, HX, 2))[:, :HX]
    col = basis(NY, range(HY))
    return (
        np.concatenate([split_table(even), split_table(odd)]),
        np.concatenate([split_table(even.T), split_table(odd.T)]),
        np.concatenate([split_table(col.T), split_table(col)]),
    )


def split(value):
    high = value.astype(BF16)
    low = (value - high.astype(F32)).astype(BF16)
    return high, low


def dot(left, right):
    return jnp.dot(left, right, preferred_element_type=F32)


def times_table(value, high, low):
    vh, vl = split(value)
    return dot(vh, high) + (dot(vl, high) + dot(vh, low))


def table_times(high, low, value):
    vh, vl = split(value)
    return dot(high, vh) + (dot(high, vl) + dot(low, vh))


def to_waves(field, fx, ty):
    cols = times_table(field, ty[0], ty[1])
    upper, lower = cols[:HX], cols[HX:]
    return (
        table_times(fx[0], fx[1], upper + lower),
        table_times(fx[2], fx[3], upper - lower),
    )


def from_waves(even, odd, bx, ty):
    first = table_times(bx[0], bx[1], even)
    second = table_times(bx[2], bx[3], odd)
    rows = jnp.concatenate([first + second, first - second], axis=0)
    return times_table(rows, ty[2], ty[3])


def swap_x(half):
    return jnp.concatenate([half[HX // 2 :], half[: HX // 2]], axis=0)


def swap_y(half):
    return jnp.concatenate([half[:, HY:], half[:, :HY]], axis=1)


def component(even, odd, own, comp):
    def one(half, coefficients):
        met = jnp.where(comp == 1, swap_x(half), jnp.where(comp == 2, swap_y(half), half))
        return met * coefficients

    return one(even, own[:HX]), one(odd, own[HX:])


def comp_index():
    return lax.axis_index("l") * 2 + lax.axis_index("k")


def wave_grid(rows):
    shape = (rows, NY)
    row = lax.broadcasted_iota(jnp.int32, shape, 0)
    col = lax.broadcasted_iota(jnp.int32, shape, 1)
    odd = (row >= HX).astype(jnp.int32)
    slot = row % QX
    wave_x = 2 * slot + odd
    sine_x = (row % HX) >= QX
    nyquist_x = sine_x & (wave_x == 0)
    wave_x = jnp.where(nyquist_x, HX, wave_x)
    wave_y = col % HY
    sine_y = col >= HY
    nyquist_y = sine_y & (wave_y == 0)
    wave_y = jnp.where(nyquist_y, HY, wave_y)
    kx = wave_x.astype(F32) * (TWO_PI / NX)
    ky = wave_y.astype(F32) * (TWO_PI / NY)
    return kx, ky, sine_x, sine_y, nyquist_x, nyquist_y


def prepare_kernel(top_ref, decay_ref, own_ref, factors_ref):
    comp = comp_index()
    kx, ky, sine_x, sine_y, nyquist_x, nyquist_y = wave_grid(NX)
    kabs = jnp.sqrt(kx * kx + ky * ky)
    inverse = 1.0 / jnp.maximum(kabs, TWO_PI / max(NX, NY))
    decay_ref[...] = 4.0 * jnp.exp(-kabs * top_ref[0]) * (1.0 - jnp.exp(-kabs))
    rx = kx * inverse
    ry = ky * inverse
    first = jnp.where(nyquist_x, 0.0, jnp.where(sine_x, -rx, rx))
    second = jnp.where(nyquist_y, 0.0, jnp.where(sine_y, -ry, ry))
    third = -(rx * rx)
    factors_ref[0] = first
    factors_ref[1] = second
    factors_ref[2] = third
    own_ref[...] = jnp.where(
        comp == 0, 1.0, jnp.where(comp == 1, first, jnp.where(comp == 2, second, third))
    )


def gather_rows(pieces, full_ref):
    comp = comp_index()
    for step, piece in enumerate(pieces):
        full_ref[pl.ds(pl.multiple_of(jnp.bitwise_xor(comp, step) * QX, QX), QX), :] = piece[...]


def start_kernel(
    nxy, m0, m1, m2, m3, top_ref, decay_ref, own_ref, fx, bx, ty, out_ref, full_ref, other_ref
):
    rows = NX // nxy
    comp = comp_index()
    gather_rows((m0, m1, m2, m3), full_ref)
    dens = full_ref[...]
    pull = 0.5 * (dens * (1.0 / (dens * dens + 0.25)))
    full_ref[...] = dens
    other_ref[...] = pull

    def plane_of(field_ref, place):
        even, odd = to_waves(field_ref[...], fx, ty)
        even, odd = component(even * decay_ref[:HX], odd * decay_ref[HX:], own_ref, comp)
        plane = from_waves(even, odd, bx, ty)
        for target in range(nxy):
            out_ref[target, place * rows : (place + 1) * rows, :] = plane[
                target * rows : (target + 1) * rows
            ]

    plane_of(full_ref, 0)
    plane_of(other_ref, 1)
    for target in range(nxy):
        out_ref[target, 2 * rows : 2 * rows + 8, :] = jnp.full((8, NY), top_ref[0], F32)


def collect_kernel(nxy, got_ref, weight_ref, obs_ref, sum_ref):
    rows = NX // nxy
    total = got_ref[0, : 2 * rows, :]
    for source in range(1, nxy):
        total = total + got_ref[source, : 2 * rows, :]
    sum_ref[: 2 * rows] = total
    for source in range(nxy):
        place = 2 * rows + source
        sum_ref[place : place + 1, :] = got_ref[source, 2 * rows : 2 * rows + 1, :]
    part = weight_ref.shape[1]
    start = 2 * rows + nxy
    sum_ref[start : start + part] = weight_ref[0]
    sum_ref[start + part : start + 2 * part] = obs_ref[0]


def residual_kernel(nxy, nh, *refs):
    rows = NX // nxy
    part = rows // nh
    start = 2 * rows + nxy
    sums = refs[:nh]
    pred_ref, pull_ref, weight_ref, tops_ref, send_ref, meas_ref = refs[nh:]
    chip = lax.axis_index("h")
    total = sums[0][: 2 * rows]
    for step in range(1, nh):
        total = total + sums[step][: 2 * rows]
    for step in range(nh):
        tops_ref[step * nxy : (step + 1) * nxy] = sums[step][2 * rows : start]
        place = pl.ds(pl.multiple_of(lax.rem(chip + (nh - step), nh) * part, part), part)
        weight_ref[place, :] = sums[step][start : start + part]
        meas_ref[place, :] = sums[step][start + part :]
    weight = weight_ref[...]
    pred = total[:rows]
    pred_ref[...] = pred
    pull_ref[...] = total[rows:]
    res = weight * (weight * (pred - meas_ref[...]))
    for target in range(nxy):
        send_ref[target] = res


def power_kernel(layers, tops_ref, power_ref):
    kx, ky, *_ = wave_grid(NX)

    def block(start, count):
        ks = jnp.sqrt(kx[start : start + count] ** 2 + ky[start : start + count] ** 2)
        double = -2.0 * ks

        def add(step, total):
            for layer in range(4):
                total = total + jnp.exp(double * tops_ref[pl.ds(4 * step + layer, 1), :])
            return total

        total = lax.fori_loop(0, layers // 4, add, jnp.zeros_like(ks))
        rise = 1.0 - jnp.exp(-ks)
        return (16.0 * (rise * rise)) * total

    for half in (0, HX):
        for start in range(half, half + QX, 64):
            value = block(start, 64)
            power_ref[start : start + 64] = value
            power_ref[start + QX : start + QX + 64] = value
    value = block(QX, 8)
    row = lax.broadcasted_iota(jnp.int32, value.shape, 0)
    power_ref[QX : QX + 8] = jnp.where(row == 0, value, power_ref[QX : QX + 8])


def adjoint_kernel(
    nxy, res_ref, decay_ref, own_ref, power_ref, factors_ref, fx, bx, ty, o0, o1, o2, o3, z_ref, i_ref
):
    rows = NX // nxy
    comp = comp_index()
    res = res_ref[...].reshape(NX, NY)
    even, odd = to_waves(res, fx, ty)
    even, odd = component(even, odd, own_ref, comp)
    sign = jnp.where((comp == 1) | (comp == 2), -1.0, 1.0)
    even = even * sign
    odd = odd * sign
    z_ref[...] = from_waves(even * decay_ref[:HX], odd * decay_ref[HX:], bx, ty)
    even = even * power_ref[:HX]
    odd = odd * power_ref[HX:]
    block = lax.axis_index("x") * lax.axis_size("y") + lax.axis_index("y")
    upper = block * rows < HX
    begin = pl.multiple_of(lax.rem(block * rows, HX), rows)
    near = pl.ds(begin, rows)
    flip = jnp.where(upper, 1.0, -1.0)
    for target in range(4):
        if target == 0:
            e, o = even, odd
        elif target == 1:
            e, o = swap_x(even) * factors_ref[0, :HX], swap_x(odd) * factors_ref[0, HX:]
        elif target == 2:
            e, o = swap_y(even) * factors_ref[1, :HX], swap_y(odd) * factors_ref[1, HX:]
        else:
            e, o = even * factors_ref[2, :HX], odd * factors_ref[2, HX:]
        line = table_times(bx[0, near, :], bx[1, near, :], e)
        line = line + flip * table_times(bx[2, near, :], bx[3, near, :], o)
        i_ref[target * rows : (target + 1) * rows, :] = line
    i_ref[...] = times_table(i_ref[...], ty[2], ty[3])
    for step, out in enumerate((o0, o1, o2, o3)):
        other = jnp.bitwise_xor(comp, step)
        out[:QX] = z_ref[pl.ds(pl.multiple_of(other * QX, QX), QX), :]
        out[QX:] = i_ref[pl.ds(pl.multiple_of(other * rows, rows), rows), :]


def share(grad, quad, image, weight, scratch, part):
    scratch[...] = weight * image
    place = pl.ds(pl.multiple_of(lax.axis_index("h") * part, part), part)
    mine = scratch[place, :]
    lane = lax.broadcasted_iota(jnp.int32, (1, 128), 1)
    square = grad * grad
    gg = jnp.sum(square)
    qgg = jnp.sum(quad * square)
    curv = jnp.sum(mine * mine)
    return jnp.where(lane == 0, gg, jnp.where(lane == 1, qgg, jnp.where(lane == 2, curv, 0.0)))


def step_length(shares):
    total = jnp.sum(shares, axis=0, keepdims=True)
    lane = lax.broadcasted_iota(jnp.int32, total.shape, 1)
    pick = lambda place: jnp.sum(jnp.where(lane == place, total, 0.0), keepdims=True)
    return pick(0) / (pick(2) + 0.5 * pick(1))


def gradient_kernel(nxy, nh, *refs):
    rows = NX // nxy
    part = rows // nh
    pieces = refs[:4]
    pull_ref, dens_ref, weight_ref = refs[4:7]
    share_ref, send_ref, data_ref, grad_ref, line_ref, image_ref, scratch = refs[7:]
    total = pieces[0][...] + pieces[1][...] + (pieces[2][...] + pieces[3][...])
    data = total[:QX]
    line = total[QX:]
    dens = dens_ref[0]
    quad = 1.0 / (dens * dens + 0.25)
    grad = data + 0.5 * (quad * dens)
    image = line + pull_ref[...]
    weight = weight_ref[...]
    share_ref[...] = jnp.broadcast_to(
        share(grad, quad, image, weight, scratch, part), share_ref.shape
    )
    data_ref[...] = data
    grad_ref[...] = grad
    line_ref[...] = line
    image_ref[...] = image
    back = weight * (weight * image)
    for target in range(nxy):
        send_ref[target] = back


def move_kernel(shares_ref, dens_ref, grad_ref, dens_out, pull_out, alpha_ref):
    alpha = step_length(shares_ref[...])
    dens = dens_ref[0] - alpha * grad_ref[...]
    dens_out[...] = dens
    pull_out[...] = 0.5 * (dens * (1.0 / (dens * dens + 0.25)))
    alpha_ref[...] = jnp.broadcast_to(alpha, alpha_ref.shape)


def second_kernel(nxy, p0, p1, p2, p3, decay_ref, own_ref, fx, bx, ty, out_ref, full_ref):
    comp = comp_index()
    gather_rows((p0, p1, p2, p3), full_ref)
    even, odd = to_waves(full_ref[...], fx, ty)
    even, odd = component(even * decay_ref[:HX], odd * decay_ref[HX:], own_ref, comp)
    out_ref[...] = from_waves(even, odd, bx, ty).reshape(out_ref.shape)


def sum_kernel(nxy, got_ref, sum_ref):
    total = got_ref[0]
    for source in range(1, nxy):
        total = total + got_ref[source]
    sum_ref[...] = total


def second_gradient_kernel(
    u0, u1, u2, u3, alpha_ref, data_ref, pull_ref, dens_ref, line_ref, grad_ref, image_ref, share_ref
):
    alpha = alpha_ref[:1, :1]
    total = u0[...] + u1[...] + (u2[...] + u3[...])
    dens = dens_ref[...]
    grad = data_ref[...] - alpha * total[:QX] + pull_ref[...]
    quad = 1.0 / (dens * dens + 0.25)
    grad_ref[...] = grad
    image_ref[...] = line_ref[...] - alpha * total[QX:]
    square = grad * grad
    lane = lax.broadcasted_iota(jnp.int32, (8, 128), 1)
    share_ref[...] = jnp.where(
        lane == 0, jnp.sum(square), jnp.where(lane == 1, jnp.sum(quad * square), 0.0)
    )


def curvature_kernel(nxy, nh, *refs):
    rows = NX // nxy
    part = rows // nh
    pulls = refs[:nh]
    image_ref, weight_ref, part_ref, share_ref, out_ref, scratch = refs[nh:]
    image = image_ref[...]
    for step in range(nh):
        image = image + pulls[step][...]
    out_ref[...] = image
    scratch[...] = weight_ref[...] * image
    mine = scratch[pl.ds(pl.multiple_of(lax.axis_index("h") * part, part), part), :]
    lane = lax.broadcasted_iota(jnp.int32, (1, 128), 1)
    share_ref[...] = jnp.broadcast_to(
        jnp.where(lane == 2, jnp.sum(mine * mine), part_ref[:1]), share_ref.shape
    )


def finish_kernel(
    shares_ref, dens_ref, grad_ref, alpha_ref, pred_ref, first_ref, second_ref, obs_ref, w_ref, dens_out, err_out
):
    part = obs_ref.shape[1]
    alpha = step_length(shares_ref[...])
    dens_out[0] = dens_ref[...] - alpha * grad_ref[...]
    place = pl.ds(pl.multiple_of(lax.axis_index("h") * part, part), part)
    pred = pred_ref[place, :] - alpha_ref[:1, :1] * first_ref[place, :]
    pred = pred - alpha * second_ref[place, :]
    err_out[0] = w_ref[0] * (pred - obs_ref[0])


VMEM = pl.BlockSpec(memory_space=pltpu.VMEM)
SMEM = pl.BlockSpec(memory_space=pltpu.SMEM)


def call(kernel, outs, *args, scratch=(), scalars=(), mib=8):
    shapes = [jax.ShapeDtypeStruct(shape, F32) for shape in outs]
    return pl.pallas_call(
        kernel,
        out_shape=shapes,
        in_specs=[SMEM if place in scalars else VMEM for place in range(len(args))],
        out_specs=[VMEM] * len(outs),
        scratch_shapes=[pltpu.VMEM(shape, F32) for shape in scratch],
        compiler_params=pltpu.CompilerParams(vmem_limit_bytes=mib << 20),
    )(*args)


def from_comps(values):
    return [values[0]] + [
        lax.ppermute(values[step], COMP, [(i, i ^ step) for i in range(4)]) for step in (1, 2, 3)
    ]


def from_chips(value, nh):
    return [value] + [
        lax.ppermute(value, "h", [(i, (i + step) % nh) for i in range(nh)]) for step in range(1, nh)
    ]


def exchange(value, axes):
    return lax.all_to_all(value, axes, 0, 0, tiled=True)


def after(value, *others):
    return lax.optimization_barrier((value, *others))[0]


def body(density, observed, data_weight, layer_top):
    nxy = lax.axis_size("x") * lax.axis_size("y")
    nh = lax.axis_size("h")
    devices = nxy * nh * 4
    rows = NX // nxy
    fx, bx, ty = (jnp.asarray(table) for table in make_tables())
    bind = functools.partial

    decay, own, factors = call(
        prepare_kernel, [(NX, NY), (NX, NY), (3, NX, NY)], layer_top, scalars=(0,)
    )
    strip = density[0]
    layers = from_comps([strip] * 4)
    (message,) = call(
        bind(start_kernel, nxy),
        [(nxy, 2 * rows + 8, NY)],
        *layers, layer_top, decay, own, fx, bx, ty,
        scratch=[(NX, NY)] * 2, scalars=(4,),
    )
    got = exchange(message, XY)
    (sums,) = call(
        bind(collect_kernel, nxy), [(2 * rows + nxy + 2 * rows // nh, NY)], got, data_weight, observed
    )
    sums = from_chips(sums, nh)
    pred, pulled, weight, tops, message = call(
        bind(residual_kernel, nxy, nh),
        [(rows, NY), (rows, NY), (rows, NY), (nxy * nh, NY), (nxy, rows, NY)],
        *sums, scratch=[(rows, NY)],
    )
    got = exchange(message, XY)
    (power,) = call(bind(power_kernel, nxy * nh), [(NX, NY)], tops)
    adjoint = lambda plane: from_comps(
        call(
            bind(adjoint_kernel, nxy),
            [(QX + rows, NY)] * 4,
            plane, decay, own, power, factors, fx, bx, ty,
            scratch=[(NX, NY), (4 * rows, NY)],
        )
    )
    pieces = adjoint(got)
    shares, message, data_grad, grad, line, image = call(
        bind(gradient_kernel, nxy, nh),
        [(devices, 128), (nxy, rows, NY), (QX, NY), (QX, NY), (rows, NY), (rows, NY)],
        *pieces, pulled, density, weight, scratch=[(rows, NY)],
    )
    shares = exchange(shares, ALL)
    dens, pull, alpha = call(
        move_kernel, [(QX, NY), (QX, NY), (8, 128)], shares, density, grad
    )
    back = exchange(after(message, pull), XY)
    pull_full = from_comps([pull] * 4)
    (message,) = call(
        bind(second_kernel, nxy), [(nxy, rows, NY)],
        *pull_full, decay, own, fx, bx, ty, scratch=[(NX, NY)],
    )
    got = exchange(message, XY)
    pieces = adjoint(back)
    grad2, image2, half = call(
        second_gradient_kernel, [(QX, NY), (rows, NY), (8, 128)],
        *pieces, alpha, data_grad, pull, dens, line,
    )
    (pulled,) = call(bind(sum_kernel, nxy), [(rows, NY)], got)
    pulls = from_chips(pulled, nh)
    shares, image2 = call(
        bind(curvature_kernel, nxy, nh), [(devices, 128), (rows, NY)],
        *pulls, image2, weight, half, scratch=[(rows, NY)],
    )
    shares = exchange(shares, ALL)
    return tuple(
        call(
            finish_kernel, [density.shape, observed.shape],
            shares, dens, grad2, alpha, pred, image, image2, observed, data_weight,
        )
    )


def solution(mesh):
    depth = mesh.shape["depth"]
    sizes = {64: (4, 4, 4), 4: (2, 1, 2)}[depth]
    fine = Mesh(mesh.devices.reshape(*sizes, 2, 2), ALL)
    data = P(COMP, DEPTH, None)
    layer = P(DEPTH, COMP, None)
    return jax.shard_map(
        body,
        mesh=fine,
        in_specs=(layer, data, data, P(DEPTH)),
        out_specs=(layer, data),
        check_vma=False,
    )
```

```python
import functools
import math

import jax
import jax.numpy as jnp
import numpy as np
from jax import lax
from jax.experimental import pallas as pl
from jax.experimental.pallas import tpu as pltpu
from jax.sharding import Mesh
from jax.sharding import PartitionSpec as P

TWO_PI = 2.0 * math.pi
F32 = jnp.float32
BF16 = jnp.bfloat16
XY = ("x", "y")
DEPTH = ("x", "y", "h")
COMP = ("l", "k")
ALL = ("x", "y", "h", "l", "k")

NX = 512
NY = 256
HX = NX // 2
QX = NX // 4
HY = NY // 2


def split_table(table):
    high = table.astype(jnp.bfloat16)
    low = (table - high.astype(np.float64)).astype(jnp.bfloat16)
    return np.stack([high, low])


def basis(count, waves):
    place = np.arange(count)
    rows = []
    for wave in waves:
        norm = math.sqrt((1.0 if wave == 0 else 2.0) / count)
        rows.append(norm * np.cos(TWO_PI * (wave * place % count) / count))
    for wave in waves:
        if wave == 0:
            rows.append(math.sqrt(1.0 / count) * (1.0 - 2.0 * (place % 2)))
        else:
            rows.append(math.sqrt(2.0 / count) * np.sin(TWO_PI * (wave * place % count) / count))
    return np.stack(rows)


def make_tables():
    even = basis(NX, range(0, HX, 2))[:, :HX]
    odd = basis(NX, range(1, HX, 2))[:, :HX]
    col = basis(NY, range(HY))
    return (
        np.concatenate([split_table(even), split_table(odd)]),
        np.concatenate([split_table(even.T), split_table(odd.T)]),
        np.concatenate([split_table(col.T), split_table(col)]),
    )


def split(value):
    high = value.astype(BF16)
    low = (value - high.astype(F32)).astype(BF16)
    return high, low


def dot(left, right):
    return jnp.dot(left, right, preferred_element_type=F32)


def times_table(value, high, low):
    vh, vl = split(value)
    return dot(vh, high) + (dot(vl, high) + dot(vh, low))


def table_times(high, low, value):
    vh, vl = split(value)
    return dot(high, vh) + (dot(high, vl) + dot(low, vh))


def to_waves(field, fx, ty):
    cols = times_table(field, ty[0], ty[1])
    upper, lower = cols[:HX], cols[HX:]
    return (
        table_times(fx[0], fx[1], upper + lower),
        table_times(fx[2], fx[3], upper - lower),
    )


def from_waves(even, odd, bx, ty):
    first = table_times(bx[0], bx[1], even)
    second = table_times(bx[2], bx[3], odd)
    rows = jnp.concatenate([first + second, first - second], axis=0)
    return times_table(rows, ty[2], ty[3])


def swap_x(half):
    return jnp.concatenate([half[HX // 2 :], half[: HX // 2]], axis=0)


def swap_y(half):
    return jnp.concatenate([half[:, HY:], half[:, :HY]], axis=1)


def component(even, odd, own, comp):
    def one(half, coefficients):
        met = jnp.where(comp == 1, swap_x(half), jnp.where(comp == 2, swap_y(half), half))
        return met * coefficients

    return one(even, own[:HX]), one(odd, own[HX:])


def comp_index():
    return lax.axis_index("l") * 2 + lax.axis_index("k")


def wave_grid(rows):
    shape = (rows, NY)
    row = lax.broadcasted_iota(jnp.int32, shape, 0)
    col = lax.broadcasted_iota(jnp.int32, shape, 1)
    odd = (row >= HX).astype(jnp.int32)
    slot = row % QX
    wave_x = 2 * slot + odd
    sine_x = (row % HX) >= QX
    nyquist_x = sine_x & (wave_x == 0)
    wave_x = jnp.where(nyquist_x, HX, wave_x)
    wave_y = col % HY
    sine_y = col >= HY
    nyquist_y = sine_y & (wave_y == 0)
    wave_y = jnp.where(nyquist_y, HY, wave_y)
    kx = wave_x.astype(F32) * (TWO_PI / NX)
    ky = wave_y.astype(F32) * (TWO_PI / NY)
    return kx, ky, sine_x, sine_y, nyquist_x, nyquist_y


def prepare_kernel(top_ref, *refs):
    count = 6
    sources, outs, sems = refs[:count], refs[count : 2 * count], refs[-1]
    decay_ref, own_ref, factors_ref = refs[2 * count : 2 * count + 3]
    copies = [pltpu.make_async_copy(sources[i], outs[i], sems.at[i]) for i in range(count)]
    for copy in copies:
        copy.start()
    comp = comp_index()
    kx, ky, sine_x, sine_y, nyquist_x, nyquist_y = wave_grid(NX)
    kabs = jnp.sqrt(kx * kx + ky * ky)
    inverse = 1.0 / jnp.maximum(kabs, TWO_PI / max(NX, NY))
    decay_ref[...] = 4.0 * jnp.exp(-kabs * top_ref[0]) * (1.0 - jnp.exp(-kabs))
    rx = kx * inverse
    ry = ky * inverse
    first = jnp.where(nyquist_x, 0.0, jnp.where(sine_x, -rx, rx))
    second = jnp.where(nyquist_y, 0.0, jnp.where(sine_y, -ry, ry))
    third = -(rx * rx)
    factors_ref[0] = first
    factors_ref[1] = second
    factors_ref[2] = third
    own_ref[...] = jnp.where(
        comp == 0, 1.0, jnp.where(comp == 1, first, jnp.where(comp == 2, second, third))
    )
    for copy in copies:
        copy.wait()


def gather_rows(pieces, full_ref):
    comp = comp_index()
    for step, piece in enumerate(pieces):
        full_ref[pl.ds(pl.multiple_of(jnp.bitwise_xor(comp, step) * QX, QX), QX), :] = piece[...]


def forward_plane(field, decay_ref, own_ref, fx, bx, ty):
    even, odd = to_waves(field, fx, ty)
    even, odd = component(even * decay_ref[:HX], odd * decay_ref[HX:], own_ref, comp_index())
    return from_waves(even, odd, bx, ty)


def start_kernel(
    nxy, m0, m1, m2, m3, top_ref, decay_ref, own_ref, fx, bx, ty, out_ref, full_ref
):
    rows = NX // nxy
    gather_rows((m0, m1, m2, m3), full_ref)
    plane = forward_plane(full_ref[...], decay_ref, own_ref, fx, bx, ty)
    for target in range(nxy):
        out_ref[target, :rows, :] = plane[target * rows : (target + 1) * rows]
        out_ref[target, rows : rows + 8, :] = jnp.full((8, NY), top_ref[0], F32)


def shift_place(axis, step, rows):
    size = lax.axis_size(axis)
    return pl.ds(pl.multiple_of(lax.rem(lax.axis_index(axis) + step, size) * rows, rows), rows)


def pull_kernel(full_ref, decay_ref, own_ref, fx, bx, ty, *refs):
    outs, plane_ref = refs[:-1], refs[-1]
    dens = full_ref[...]
    pull = 0.5 * (dens * (1.0 / (dens * dens + 0.25)))
    plane_ref[...] = forward_plane(pull, decay_ref, own_ref, fx, bx, ty)
    for step, out in enumerate(outs):
        out[...] = plane_ref[shift_place("x", step, out.shape[0]), :]


def fold_kernel(count, *refs):
    parts, outs, total_ref = refs[:count], refs[count:-1], refs[-1]
    total = parts[0][...]
    for part in parts[1:]:
        total = total + part[...]
    if len(outs) == 1:
        outs[0][...] = total
    else:
        total_ref[...] = total
        for step, out in enumerate(outs):
            out[...] = total_ref[shift_place("y", step, out.shape[0]), :]


def join_kernel(*refs):
    out = refs[-1]
    rows = refs[0].shape[0]
    for place, part in enumerate(refs[:-1]):
        out[place * rows : (place + 1) * rows] = part[...]


def place_kernel(ny, nx, *refs):
    out = refs[-1]
    rows = refs[0].shape[0] // nx
    x, y = lax.axis_index("x"), lax.axis_index("y")
    for back_y in range(ny):
        for back_x in range(nx):
            block = lax.rem(x + (nx - back_x), nx) * ny + lax.rem(y + (ny - back_y), ny)
            out[pl.ds(pl.multiple_of(block * rows, rows), rows), :] = refs[back_y][
                back_x * rows : (back_x + 1) * rows
            ]


def collect_kernel(nxy, got_ref, weight_ref, obs_ref, sum_ref):
    rows = NX // nxy
    total = got_ref[0, :rows, :]
    for source in range(1, nxy):
        total = total + got_ref[source, :rows, :]
    sum_ref[:rows] = total
    for source in range(nxy):
        sum_ref[rows + source : rows + source + 1, :] = got_ref[source, rows : rows + 1, :]
    part = weight_ref.shape[1]
    start = rows + nxy
    sum_ref[start : start + part] = weight_ref[0]
    sum_ref[start + part : start + 2 * part] = obs_ref[0]


def residual_kernel(nxy, nh, *refs):
    rows = NX // nxy
    part = rows // nh
    start = rows + nxy
    sums = refs[:nh]
    pred_ref, weight_ref, tops_ref, send_ref, meas_ref = refs[nh:]
    chip = lax.axis_index("h")
    pred = sums[0][:rows]
    for step in range(1, nh):
        pred = pred + sums[step][:rows]
    for step in range(nh):
        tops_ref[step * nxy : (step + 1) * nxy] = sums[step][rows:start]
        place = pl.ds(pl.multiple_of(lax.rem(chip + (nh - step), nh) * part, part), part)
        weight_ref[place, :] = sums[step][start : start + part]
        meas_ref[place, :] = sums[step][start + part :]
    weight = weight_ref[...]
    pred_ref[...] = pred
    res = weight * (weight * (pred - meas_ref[...]))
    for target in range(nxy):
        send_ref[target] = res


def power_kernel(layers, tops_ref, power_ref):
    kx, ky, *_ = wave_grid(NX)

    def block(start, count):
        ks = jnp.sqrt(kx[start : start + count] ** 2 + ky[start : start + count] ** 2)
        double = -2.0 * ks

        def add(step, total):
            for layer in range(4):
                total = total + jnp.exp(double * tops_ref[pl.ds(4 * step + layer, 1), :])
            return total

        total = lax.fori_loop(0, layers // 4, add, jnp.zeros_like(ks))
        rise = 1.0 - jnp.exp(-ks)
        return (16.0 * (rise * rise)) * total

    for half in (0, HX):
        for start in range(half, half + QX, 64):
            value = block(start, 64)
            power_ref[start : start + 64] = value
            power_ref[start + QX : start + QX + 64] = value
    value = block(QX, 8)
    row = lax.broadcasted_iota(jnp.int32, value.shape, 0)
    power_ref[QX : QX + 8] = jnp.where(row == 0, value, power_ref[QX : QX + 8])


def adjoint_kernel(
    nxy, res_ref, decay_ref, own_ref, power_ref, factors_ref, fx, bx, ty, o0, o1, o2, o3, z_ref, i_ref
):
    rows = NX // nxy
    comp = comp_index()
    even, odd = to_waves(res_ref[...], fx, ty)
    even, odd = component(even, odd, own_ref, comp)
    sign = jnp.where((comp == 1) | (comp == 2), -1.0, 1.0)
    even = even * sign
    odd = odd * sign
    z_ref[...] = from_waves(even * decay_ref[:HX], odd * decay_ref[HX:], bx, ty)
    even = even * power_ref[:HX]
    odd = odd * power_ref[HX:]
    block = lax.axis_index("x") * lax.axis_size("y") + lax.axis_index("y")
    upper = block * rows < HX
    begin = pl.multiple_of(lax.rem(block * rows, HX), rows)
    near = pl.ds(begin, rows)
    flip = jnp.where(upper, 1.0, -1.0)
    for target in range(4):
        if target == 0:
            e, o = even, odd
        elif target == 1:
            e, o = swap_x(even) * factors_ref[0, :HX], swap_x(odd) * factors_ref[0, HX:]
        elif target == 2:
            e, o = swap_y(even) * factors_ref[1, :HX], swap_y(odd) * factors_ref[1, HX:]
        else:
            e, o = even * factors_ref[2, :HX], odd * factors_ref[2, HX:]
        line = table_times(bx[0, near, :], bx[1, near, :], e)
        line = line + flip * table_times(bx[2, near, :], bx[3, near, :], o)
        i_ref[target * rows : (target + 1) * rows, :] = line
    i_ref[...] = times_table(i_ref[...], ty[2], ty[3])
    for step, out in enumerate((o0, o1, o2, o3)):
        other = jnp.bitwise_xor(comp, step)
        out[:QX] = z_ref[pl.ds(pl.multiple_of(other * QX, QX), QX), :]
        out[QX:] = i_ref[pl.ds(pl.multiple_of(other * rows, rows), rows), :]


def share(grad, quad, image, weight, scratch, part):
    scratch[...] = weight * image
    place = pl.ds(pl.multiple_of(lax.axis_index("h") * part, part), part)
    mine = scratch[place, :]
    lane = lax.broadcasted_iota(jnp.int32, (1, 128), 1)
    square = grad * grad
    gg = jnp.sum(square)
    qgg = jnp.sum(quad * square)
    curv = jnp.sum(mine * mine)
    return jnp.where(lane == 0, gg, jnp.where(lane == 1, qgg, jnp.where(lane == 2, curv, 0.0)))


def step_length(shares):
    total = jnp.sum(shares, axis=0, keepdims=True)
    lane = lax.broadcasted_iota(jnp.int32, total.shape, 1)
    pick = lambda place: jnp.sum(jnp.where(lane == place, total, 0.0), keepdims=True)
    return pick(0) / (pick(2) + 0.5 * pick(1))


def gradient_kernel(nxy, nh, *refs):
    rows = NX // nxy
    part = rows // nh
    pieces, pulls = refs[:4], refs[4 : 4 + nh]
    dens_ref, weight_ref = refs[4 + nh : 6 + nh]
    share_ref, back_ref, data_ref, grad_ref, line_ref, image_ref, scratch = refs[6 + nh :]
    total = pieces[0][...] + pieces[1][...] + (pieces[2][...] + pieces[3][...])
    data = total[:QX]
    line = total[QX:]
    dens = dens_ref[0]
    quad = 1.0 / (dens * dens + 0.25)
    grad = data + 0.5 * (quad * dens)
    pulled = pulls[0][...]
    for step in range(1, nh):
        pulled = pulled + pulls[step][...]
    image = line + pulled
    weight = weight_ref[...]
    share_ref[...] = jnp.broadcast_to(
        share(grad, quad, image, weight, scratch, part), share_ref.shape
    )
    data_ref[...] = data
    grad_ref[...] = grad
    line_ref[...] = line
    image_ref[...] = image
    back_ref[...] = weight * (weight * image)


def move_kernel(shares_ref, dens_ref, grad_ref, dens_out, pull_out, alpha_ref):
    alpha = step_length(shares_ref[...])
    dens = dens_ref[0] - alpha * grad_ref[...]
    dens_out[...] = dens
    pull_out[...] = 0.5 * (dens * (1.0 / (dens * dens + 0.25)))
    alpha_ref[...] = jnp.broadcast_to(alpha, alpha_ref.shape)


def second_kernel(p0, p1, p2, p3, decay_ref, own_ref, fx, bx, ty, out_ref, full_ref):
    gather_rows((p0, p1, p2, p3), full_ref)
    plane = forward_plane(full_ref[...], decay_ref, own_ref, fx, bx, ty)
    out_ref[...] = plane.reshape(out_ref.shape)


def second_gradient_kernel(
    u0, u1, u2, u3, alpha_ref, data_ref, pull_ref, dens_ref, line_ref, grad_ref, image_ref, share_ref
):
    alpha = alpha_ref[:1, :1]
    total = u0[...] + u1[...] + (u2[...] + u3[...])
    dens = dens_ref[...]
    grad = data_ref[...] - alpha * total[:QX] + pull_ref[...]
    quad = 1.0 / (dens * dens + 0.25)
    grad_ref[...] = grad
    image_ref[...] = line_ref[...] - alpha * total[QX:]
    square = grad * grad
    lane = lax.broadcasted_iota(jnp.int32, (8, 128), 1)
    share_ref[...] = jnp.where(
        lane == 0, jnp.sum(square), jnp.where(lane == 1, jnp.sum(quad * square), 0.0)
    )


def curvature_kernel(got_ref, image_ref, weight_ref, part_ref, share_ref, out_ref):
    part = weight_ref.shape[1]
    image = image_ref[pl.ds(pl.multiple_of(lax.axis_index("h") * part, part), part), :]
    total = got_ref[0]
    for source in range(1, got_ref.shape[0]):
        total = total + got_ref[source]
    image = image + total
    out_ref[...] = image
    mine = weight_ref[0] * image
    lane = lax.broadcasted_iota(jnp.int32, (1, 128), 1)
    share_ref[...] = jnp.broadcast_to(
        jnp.where(lane == 2, jnp.sum(mine * mine), part_ref[:1]), share_ref.shape
    )


def finish_kernel(
    shares_ref, dens_ref, grad_ref, alpha_ref, pred_ref, first_ref, second_ref, obs_ref, w_ref, dens_out, err_out
):
    part = obs_ref.shape[1]
    alpha = step_length(shares_ref[...])
    dens_out[0] = dens_ref[...] - alpha * grad_ref[...]
    place = pl.ds(pl.multiple_of(lax.axis_index("h") * part, part), part)
    pred = pred_ref[place, :] - alpha_ref[:1, :1] * first_ref[place, :]
    pred = pred - alpha * second_ref[...]
    err_out[0] = w_ref[0] * (pred - obs_ref[0])


VMEM = pl.BlockSpec(memory_space=pltpu.VMEM)
SMEM = pl.BlockSpec(memory_space=pltpu.SMEM)
ANY = pl.BlockSpec(memory_space=pl.ANY)


def call(kernel, outs, *args, scratch=(), places=(), out=pltpu.VMEM, mib=8):
    places = dict(places)
    kinds = [(item, F32) if isinstance(item, tuple) else (item.shape, item.dtype) for item in outs]
    return pl.pallas_call(
        kernel,
        out_shape=[out(shape, dtype) for shape, dtype in kinds],
        in_specs=[places.get(place, VMEM) for place in range(len(args))],
        out_specs=[VMEM] * len(outs),
        scratch_shapes=[
            pltpu.VMEM(item, F32) if isinstance(item, tuple) else item for item in scratch
        ],
        compiler_params=pltpu.CompilerParams(vmem_limit_bytes=mib << 20),
    )(*args)


def from_comps(values):
    return [values[0]] + [
        lax.ppermute(values[step], COMP, [(i, i ^ step) for i in range(4)]) for step in (1, 2, 3)
    ]


def from_axis(values, axis):
    size = len(values)
    return [values[0]] + [
        lax.ppermute(values[step], axis, [(i, (i + step) % size) for i in range(size)])
        for step in range(1, size)
    ]


def exchange(value, axes):
    return lax.all_to_all(value, axes, 0, 0, tiled=True)


def after(values, *others):
    if isinstance(values, (list, tuple)):
        return list(lax.optimization_barrier((tuple(values), others))[0])
    return lax.optimization_barrier((values, others))[0]


def body(density, observed, data_weight, layer_top):
    nx, ny, nh = (lax.axis_size(axis) for axis in DEPTH)
    nxy = nx * ny
    devices = nxy * nh * 4
    rows = NX // nxy
    part = rows // nh
    tables = [jnp.asarray(table) for table in make_tables()]
    bind = functools.partial

    layers = from_comps([density[0]] * 4)
    kept = [*tables, density, data_weight, observed]
    *tables, density, data_weight, observed, decay, own, factors = call(
        prepare_kernel, [*kept, (NX, NY), (NX, NY), (3, NX, NY)], layer_top, *kept,
        scratch=[pltpu.SemaphoreType.DMA((6,))],
        places=[(0, SMEM), *((place, ANY) for place in range(1, 7))],
    )
    message, full = call(
        bind(start_kernel, nxy), [(nxy, rows + 8, NY), (NX, NY)],
        density[0], *layers[1:], layer_top, decay, own, *tables, places=[(4, SMEM)],
    )
    got = exchange(message, XY)
    parts = call(
        pull_kernel, [(NX // nx, NY)] * nx, after(full, message), decay, own, *tables,
        scratch=[(NX, NY)],
    )
    parts = call(
        bind(fold_kernel, nx), [(rows, NY)] * ny, *from_axis(parts, "x"), scratch=[(NX // nx, NY)]
    )
    got = after(got, *parts)
    (sums,) = call(
        bind(collect_kernel, nxy), [(rows + nxy + 2 * part, NY)], got, data_weight, observed
    )
    sums = from_axis([sums] * nh, "h")
    pred, weight, tops, message = call(
        bind(residual_kernel, nxy, nh),
        [(rows, NY), (rows, NY), (nxy * nh, NY), (nxy, rows, NY)],
        *sums, scratch=[(rows, NY)],
    )
    got = exchange(message, XY)
    parts = from_axis(after(parts, message), "y")
    (pulled,) = call(bind(fold_kernel, ny), [(rows, NY)], *parts, scratch=[(rows, NY)])
    pulls = from_axis([pulled] * nh, "h")
    (power,) = call(bind(power_kernel, nxy * nh), [(NX, NY)], tops)
    adjoint = lambda plane: call(
        bind(adjoint_kernel, nxy), [(QX + rows, NY)] * 4,
        plane, decay, own, power, factors, *tables, scratch=[(NX, NY), (4 * rows, NY)],
    )
    got = after(got, *pulls)
    pieces = from_comps(adjoint(got.reshape(NX, NY)))
    shares, back, data_grad, grad, line, image = call(
        bind(gradient_kernel, nxy, nh),
        [(devices, 128), (rows, NY), (QX, NY), (QX, NY), (rows, NY), (rows, NY)],
        *pieces, *pulls, density, weight, scratch=[(rows, NY)],
    )
    shares = exchange(shares, ALL)
    (joined,) = call(join_kernel, [(nx * rows, NY)], *from_axis([back] * nx, "x"))
    (plane,) = call(bind(place_kernel, ny, nx), [(NX, NY)], *from_axis([joined] * ny, "y"))
    shares = after(shares, plane)
    dens, pull, alpha = call(
        move_kernel, [(QX, NY), (QX, NY), (8, 128)], shares, density, grad
    )
    pull_full = from_comps([pull] * 4)
    pieces = adjoint(after(plane, pull))
    pull_full = after(pull_full, *pieces)
    (message,) = call(
        second_kernel, [(nxy * nh, part, NY)], *pull_full, decay, own, *tables, scratch=[(NX, NY)]
    )
    got = exchange(message, DEPTH)
    pieces = from_comps(after(pieces, message))
    grad2, image2, half = call(
        second_gradient_kernel, [(QX, NY), (rows, NY), (8, 128)],
        *pieces, alpha, data_grad, pull, dens, line,
    )
    got = after(got, half)
    shares, image2 = call(
        curvature_kernel, [(devices, 128), (part, NY)], got, image2, data_weight, half
    )
    shares = exchange(shares, ALL)
    return tuple(
        call(
            finish_kernel, [density.shape, observed.shape],
            shares, dens, grad2, alpha, pred, image, image2, observed, data_weight,
            out=jax.ShapeDtypeStruct,
        )
    )


def solution(mesh):
    depth = mesh.shape["depth"]
    sizes = {64: (4, 4, 4), 4: (2, 1, 2)}[depth]
    fine = Mesh(mesh.devices.reshape(*sizes, 2, 2), ALL)
    data = P(COMP, DEPTH, None)
    layer = P(DEPTH, COMP, None)
    return jax.shard_map(
        body,
        mesh=fine,
        in_specs=(layer, data, data, P(DEPTH)),
        out_specs=(layer, data),
        check_vma=False,
    )
```

```python
import functools
import math

import jax
import jax.numpy as jnp
import numpy as np
from jax import lax
from jax.experimental import pallas as pl
from jax.experimental.pallas import tpu as pltpu
from jax.sharding import Mesh
from jax.sharding import PartitionSpec as P

TWO_PI = 2.0 * math.pi
F32 = jnp.float32
BF16 = jnp.bfloat16
XY = ("x", "y")
DEPTH = ("x", "y", "h")
COMP = ("l", "k")
ALL = ("x", "y", "h", "l", "k")

NX = 512
NY = 256
HX = NX // 2
QX = NX // 4
HY = NY // 2


def split_table(table):
    high = table.astype(jnp.bfloat16)
    low = (table - high.astype(np.float64)).astype(jnp.bfloat16)
    return np.stack([high, low])


def basis(count, waves):
    place = np.arange(count)
    rows = []
    for wave in waves:
        norm = math.sqrt((1.0 if wave == 0 else 2.0) / count)
        rows.append(norm * np.cos(TWO_PI * (wave * place % count) / count))
    for wave in waves:
        if wave == 0:
            rows.append(math.sqrt(1.0 / count) * (1.0 - 2.0 * (place % 2)))
        else:
            rows.append(math.sqrt(2.0 / count) * np.sin(TWO_PI * (wave * place % count) / count))
    return np.stack(rows)


def make_tables():
    even = basis(NX, range(0, HX, 2))[:, :HX]
    odd = basis(NX, range(1, HX, 2))[:, :HX]
    col = basis(NY, range(HY))
    return (
        np.concatenate([split_table(even), split_table(odd)]),
        split_table(col.T),
    )


def split(value):
    high = value.astype(BF16)
    low = (value - high.astype(F32)).astype(BF16)
    return high, low


def dot(left, right):
    return jnp.dot(left, right, preferred_element_type=F32)


def dot_turned(left, right):
    return lax.dot_general(left, right, (((1,), (1,)), ((), ())), preferred_element_type=F32)


def times_table(value, high, low):
    vh, vl = split(value)
    return dot(vh, high) + (dot(vl, high) + dot(vh, low))


def times_turned(value, high, low):
    vh, vl = split(value)
    return dot_turned(vh, high) + (dot_turned(vl, high) + dot_turned(vh, low))


def table_times(high, low, value):
    vh, vl = split(value)
    return dot(high, vh) + (dot(high, vl) + dot(low, vh))


def to_waves(field, fx, ty):
    cols = times_table(field, ty[0], ty[1])
    upper, lower = cols[:HX], cols[HX:]
    return (
        table_times(fx[0], fx[1], upper + lower),
        table_times(fx[2], fx[3], upper - lower),
    )


def from_waves(even, odd, bx, ty):
    first = table_times(bx[0], bx[1], even)
    second = table_times(bx[2], bx[3], odd)
    rows = jnp.concatenate([first + second, first - second], axis=0)
    return times_turned(rows, ty[0], ty[1])


def swap_x(half):
    return jnp.concatenate([half[HX // 2 :], half[: HX // 2]], axis=0)


def swap_y(half):
    return jnp.concatenate([half[:, HY:], half[:, :HY]], axis=1)


def sines(cosines, nyquist):
    row = lax.broadcasted_iota(jnp.int32, cosines.shape, 0)
    return jnp.where(row == 0, nyquist, cosines)


def spread(ref):
    even, odd = ref[:QX], ref[QX:HX]
    return (
        jnp.concatenate([even, sines(even, ref[HX : HX + 1])], axis=0),
        jnp.concatenate([odd, odd], axis=0),
    )


def x_factors(gx_ref):
    even, odd = gx_ref[:QX], gx_ref[QX:HX]
    return jnp.concatenate([even, -even], axis=0), jnp.concatenate([odd, -odd], axis=0)


def xx_factors(gx_ref):
    even, odd = spread(gx_ref)
    return -(even * even), -(odd * odd)


def component(even, odd, gx_ref, gy_ref, comp):
    halves = []
    for half, first, second, third in zip(
        (even, odd), x_factors(gx_ref), spread(gy_ref), xx_factors(gx_ref)
    ):
        met = jnp.where(comp == 1, swap_x(half), jnp.where(comp == 2, swap_y(half), half))
        factor = jnp.where(comp == 1, first, jnp.where(comp == 2, second, third))
        halves.append(met * jnp.where(comp == 0, 1.0, factor))
    return halves


def comp_index():
    return lax.axis_index("l") * 2 + lax.axis_index("k")


KEPT = HX + 8


def wave_grid():
    row = lax.broadcasted_iota(jnp.int32, (KEPT, NY), 0)
    col = lax.broadcasted_iota(jnp.int32, (KEPT, NY), 1)
    wave_x = jnp.where(row >= HX, HX, 2 * (row % QX) + (row >= QX).astype(jnp.int32))
    nyquist_y = col == HY
    wave_y = jnp.where(nyquist_y, HY, col % HY)
    kx = wave_x.astype(F32) * (TWO_PI / NX)
    ky = wave_y.astype(F32) * (TWO_PI / NY)
    return kx, ky, col >= HY, nyquist_y


def prepare_kernel(
    top_ref, fx_in, ty_in, dens_in, weight_in, obs_in,
    fx, bx, ty, dens_ref, weight_ref, obs_ref, decay_ref, gx_ref, gy_ref,
):
    dens_ref[...] = dens_in[0]
    weight_ref[...] = weight_in[0]
    obs_ref[...] = obs_in[0]
    for place in range(4):
        table = fx_in[place]
        fx[place] = table
        bx[place] = table.astype(F32).T.astype(BF16)
    for place in range(2):
        ty[place] = ty_in[place]
    kx, ky, sine_y, nyquist_y = wave_grid()
    kabs = jnp.sqrt(kx * kx + ky * ky)
    inverse = 1.0 / jnp.maximum(kabs, TWO_PI / max(NX, NY))
    decay_ref[...] = 4.0 * jnp.exp(-kabs * top_ref[0]) * (1.0 - jnp.exp(-kabs))
    gx_ref[...] = kx * inverse
    ry = ky * inverse
    gy_ref[...] = jnp.where(nyquist_y, 0.0, jnp.where(sine_y, -ry, ry))


def gather_rows(pieces, full_ref):
    comp = comp_index()
    for step, piece in enumerate(pieces):
        full_ref[pl.ds(pl.multiple_of(jnp.bitwise_xor(comp, step) * QX, QX), QX), :] = piece[...]


def forward_plane(field, decay_ref, gx_ref, gy_ref, fx, bx, ty):
    even, odd = to_waves(field, fx, ty)
    decay = spread(decay_ref)
    even, odd = component(even * decay[0], odd * decay[1], gx_ref, gy_ref, comp_index())
    return from_waves(even, odd, bx, ty)


def start_kernel(
    nxy, m0, m1, m2, m3, top_ref, decay_ref, gx_ref, gy_ref, fx, bx, ty, out_ref, full_ref, pull_ref
):
    rows = NX // nxy
    gather_rows((m0, m1, m2, m3), full_ref)
    dens = full_ref[...]
    pull_ref[...] = 0.5 * (dens * (1.0 / (dens * dens + 0.25)))
    for place, field in enumerate((full_ref, pull_ref)):
        plane = forward_plane(field[...], decay_ref, gx_ref, gy_ref, fx, bx, ty)
        for target in range(nxy):
            out_ref[target, place * rows : (place + 1) * rows, :] = plane[
                target * rows : (target + 1) * rows
            ]
    for target in range(nxy):
        out_ref[target, 2 * rows : 2 * rows + 8, :] = jnp.full((8, NY), top_ref[0], F32)


def collect_kernel(nxy, got_ref, weight_ref, obs_ref, sum_ref):
    rows = NX // nxy
    total = got_ref[0, : 2 * rows, :]
    for source in range(1, nxy):
        total = total + got_ref[source, : 2 * rows, :]
    sum_ref[: 2 * rows] = total
    for source in range(nxy):
        place = 2 * rows + source
        sum_ref[place : place + 1, :] = got_ref[source, 2 * rows : 2 * rows + 1, :]
    part = weight_ref.shape[0]
    start = 2 * rows + nxy
    sum_ref[start : start + part] = weight_ref[...]
    sum_ref[start + part : start + 2 * part] = obs_ref[...]


def residual_kernel(nxy, nh, *refs):
    rows = NX // nxy
    part = rows // nh
    start = 2 * rows + nxy
    sums = refs[:nh]
    pred_ref, pull_ref, weight_ref, tops_ref, send_ref, meas_ref = refs[nh:]
    chip = lax.axis_index("h")
    total = sums[0][: 2 * rows]
    for step in range(1, nh):
        total = total + sums[step][: 2 * rows]
    for step in range(nh):
        tops_ref[step * nxy : (step + 1) * nxy] = sums[step][2 * rows : start]
        place = pl.ds(pl.multiple_of(lax.rem(chip + (nh - step), nh) * part, part), part)
        weight_ref[place, :] = sums[step][start : start + part]
        meas_ref[place, :] = sums[step][start + part :]
    weight = weight_ref[...]
    pred = total[:rows]
    pred_ref[...] = pred
    pull_ref[...] = total[rows:]
    res = weight * (weight * (pred - meas_ref[...]))
    for target in range(nxy):
        send_ref[target] = res


def power_kernel(layers, tops_ref, power_ref):
    kx, ky, *_ = wave_grid()
    for start in range(0, KEPT, 64):
        stop = min(start + 64, KEPT)
        ks = jnp.sqrt(kx[start:stop] ** 2 + ky[start:stop] ** 2)
        double = -2.0 * ks

        def add(step, total):
            for layer in range(4):
                total = total + jnp.exp(double * tops_ref[pl.ds(4 * step + layer, 1), :])
            return total

        total = lax.fori_loop(0, layers // 4, add, jnp.zeros_like(ks))
        rise = 1.0 - jnp.exp(-ks)
        power_ref[start:stop] = (16.0 * (rise * rise)) * total


def adjoint_kernel(
    nxy, res_ref, decay_ref, gx_ref, gy_ref, power_ref, fx, bx, ty, o0, o1, o2, o3, z_ref, i_ref
):
    rows = NX // nxy
    comp = comp_index()
    even, odd = to_waves(res_ref[...], fx, ty)
    even, odd = component(even, odd, gx_ref, gy_ref, comp)
    sign = jnp.where((comp == 1) | (comp == 2), -1.0, 1.0)
    even = even * sign
    odd = odd * sign
    decay = spread(decay_ref)
    z_ref[...] = from_waves(even * decay[0], odd * decay[1], bx, ty)
    power = spread(power_ref)
    even = even * power[0]
    odd = odd * power[1]
    block = lax.axis_index("x") * lax.axis_size("y") + lax.axis_index("y")
    upper = block * rows < HX
    near = pl.ds(pl.multiple_of(lax.rem(block * rows, HX), rows), rows)
    flip = jnp.where(upper, 1.0, -1.0)
    for target in range(4):
        if target == 0:
            e, o = even, odd
        elif target == 1:
            first = x_factors(gx_ref)
            e, o = swap_x(even) * first[0], swap_x(odd) * first[1]
        elif target == 2:
            second = spread(gy_ref)
            e, o = swap_y(even) * second[0], swap_y(odd) * second[1]
        else:
            third = xx_factors(gx_ref)
            e, o = even * third[0], odd * third[1]
        line = table_times(bx[0, near, :], bx[1, near, :], e)
        line = line + flip * table_times(bx[2, near, :], bx[3, near, :], o)
        i_ref[target * rows : (target + 1) * rows, :] = line
    i_ref[...] = times_turned(i_ref[...], ty[0], ty[1])
    for step, out in enumerate((o0, o1, o2, o3)):
        other = jnp.bitwise_xor(comp, step)
        out[:QX] = z_ref[pl.ds(pl.multiple_of(other * QX, QX), QX), :]
        out[QX:] = i_ref[pl.ds(pl.multiple_of(other * rows, rows), rows), :]


def share(grad, quad, image, weight, scratch, part):
    scratch[...] = weight * image
    place = pl.ds(pl.multiple_of(lax.axis_index("h") * part, part), part)
    mine = scratch[place, :]
    lane = lax.broadcasted_iota(jnp.int32, (1, 128), 1)
    square = grad * grad
    gg = jnp.sum(square)
    qgg = jnp.sum(quad * square)
    curv = jnp.sum(mine * mine)
    return jnp.where(lane == 0, gg, jnp.where(lane == 1, qgg, jnp.where(lane == 2, curv, 0.0)))


def step_length(shares):
    total = jnp.sum(shares, axis=0, keepdims=True)
    lane = lax.broadcasted_iota(jnp.int32, total.shape, 1)
    pick = lambda place: jnp.sum(jnp.where(lane == place, total, 0.0), keepdims=True)
    return pick(0) / (pick(2) + 0.5 * pick(1))


def gradient_kernel(nxy, nh, *refs):
    rows = NX // nxy
    part = rows // nh
    pieces = refs[:4]
    pull_ref, dens_ref, weight_ref = refs[4:7]
    share_ref, send_ref, grad_ref, line_ref, image_ref, scratch = refs[7:]
    total = pieces[0][...] + pieces[1][...] + (pieces[2][...] + pieces[3][...])
    data = total[:QX]
    line = total[QX:]
    dens = dens_ref[...]
    quad = 1.0 / (dens * dens + 0.25)
    grad = data + 0.5 * (quad * dens)
    image = line + pull_ref[...]
    weight = weight_ref[...]
    share_ref[...] = jnp.broadcast_to(
        share(grad, quad, image, weight, scratch, part), share_ref.shape
    )
    grad_ref[...] = grad
    line_ref[...] = line
    image_ref[...] = image
    back = weight * (weight * image)
    for target in range(nxy):
        send_ref[target] = back


def second_kernel(
    shares_ref, dens_ref, full_ref, g0, g1, g2, g3, decay_ref, gx_ref, gy_ref, fx, bx, ty,
    out_ref, dens_out, base_out, alpha_ref, all_ref,
):
    alpha = step_length(shares_ref[...])
    alpha_ref[...] = jnp.broadcast_to(alpha, alpha_ref.shape)
    old = dens_ref[...]
    dens = old - alpha * g0[...]
    dens_out[...] = dens
    data = g0[...] - 0.5 * ((1.0 / (old * old + 0.25)) * old)
    base_out[...] = data + 0.5 * (dens * (1.0 / (dens * dens + 0.25)))
    gather_rows((g0, g1, g2, g3), all_ref)
    dens = full_ref[...] - alpha * all_ref[...]
    all_ref[...] = 0.5 * (dens * (1.0 / (dens * dens + 0.25)))
    plane = forward_plane(all_ref[...], decay_ref, gx_ref, gy_ref, fx, bx, ty)
    out_ref[...] = plane.reshape(out_ref.shape)


def second_gradient_kernel(
    u0, u1, u2, u3, alpha_ref, base_ref, dens_ref, line_ref, grad_ref, image_ref, share_ref
):
    alpha = alpha_ref[:1, :1]
    total = u0[...] + u1[...] + (u2[...] + u3[...])
    dens = dens_ref[...]
    grad = base_ref[...] - alpha * total[:QX]
    quad = 1.0 / (dens * dens + 0.25)
    grad_ref[...] = grad
    image_ref[...] = line_ref[...] - alpha * total[QX:]
    square = grad * grad
    lane = lax.broadcasted_iota(jnp.int32, (8, 128), 1)
    share_ref[...] = jnp.where(
        lane == 0, jnp.sum(square), jnp.where(lane == 1, jnp.sum(quad * square), 0.0)
    )


def curvature_kernel(got_ref, image_ref, weight_ref, part_ref, share_ref, out_ref):
    part = weight_ref.shape[0]
    image = image_ref[pl.ds(pl.multiple_of(lax.axis_index("h") * part, part), part), :]
    total = got_ref[0]
    for source in range(1, got_ref.shape[0]):
        total = total + got_ref[source]
    image = image + total
    out_ref[...] = image
    mine = weight_ref[...] * image
    lane = lax.broadcasted_iota(jnp.int32, (1, 128), 1)
    share_ref[...] = jnp.broadcast_to(
        jnp.where(lane == 2, jnp.sum(mine * mine), part_ref[:1]), share_ref.shape
    )


def finish_kernel(
    shares_ref, dens_ref, grad_ref, alpha_ref, pred_ref, first_ref, second_ref, obs_ref, w_ref, dens_out, err_out
):
    part = obs_ref.shape[0]
    alpha = step_length(shares_ref[...])
    dens_out[0] = dens_ref[...] - alpha * grad_ref[...]
    place = pl.ds(pl.multiple_of(lax.axis_index("h") * part, part), part)
    pred = pred_ref[place, :] - alpha_ref[:1, :1] * first_ref[place, :]
    pred = pred - alpha * second_ref[...]
    err_out[0] = w_ref[...] * (pred - obs_ref[...])


VMEM = pl.BlockSpec(memory_space=pltpu.VMEM)
SMEM = pl.BlockSpec(memory_space=pltpu.SMEM)
ANY = pl.BlockSpec(memory_space=pl.ANY)


class Program:
    def __init__(self):
        self.alive = []

    def hold(self, *values):
        self.alive += values

    def drop(self, *values):
        self.alive = [item for item in self.alive if all(item is not value for value in values)]

    def call(self, kernel, outs, *args, scratch=(), scalars=(), mib=8):
        used = len(args)
        keep = [item for item in self.alive if all(item is not value for value in args)]
        kept = len(keep)

        def inner(*refs):
            kernel(*refs[:used], *refs[used + kept :])

        kinds = [(item, F32) if isinstance(item, tuple) else (item.shape, item.dtype) for item in outs]
        return pl.pallas_call(
            inner,
            out_shape=[jax.ShapeDtypeStruct(shape, dtype) for shape, dtype in kinds],
            in_specs=[SMEM if place in scalars else VMEM for place in range(used)] + [ANY] * kept,
            out_specs=[VMEM] * len(outs),
            scratch_shapes=[pltpu.VMEM(shape, F32) for shape in scratch],
            compiler_params=pltpu.CompilerParams(vmem_limit_bytes=mib << 20),
        )(*args, *keep)


def from_comps(values):
    return [values[0]] + [
        lax.ppermute(values[step], COMP, [(i, i ^ step) for i in range(4)]) for step in (1, 2, 3)
    ]


def from_axis(values, axis):
    size = len(values)
    return [values[0]] + [
        lax.ppermute(values[step], axis, [(i, (i + step) % size) for i in range(size)])
        for step in range(1, size)
    ]


def exchange(value, axes):
    return lax.all_to_all(value, axes, 0, 0, tiled=True)


def after(values, *others):
    if isinstance(values, (list, tuple)):
        return list(lax.optimization_barrier((tuple(values), others))[0])
    return lax.optimization_barrier((values, others))[0]


def body(density, observed, data_weight, layer_top):
    nx, ny, nh = (lax.axis_size(axis) for axis in DEPTH)
    nxy = nx * ny
    devices = nxy * nh * 4
    rows = NX // nxy
    part = rows // nh
    fx, ty = (jnp.asarray(table) for table in make_tables())
    bind = functools.partial
    program = Program()
    call = program.call

    layers = from_comps([density[0]] * 4)
    *tables, dens, weight_own, obs_own, decay, gx, gy = call(
        prepare_kernel,
        [
            fx, fx, ty, (QX, NY), (part, NY), (part, NY), (KEPT, NY), (KEPT, NY), (KEPT, NY),
        ],
        layer_top, fx, ty, density, data_weight, observed, scalars=(0,),
    )
    factors = (decay, gx, gy)
    program.hold(*tables, *factors, dens, weight_own, obs_own)
    message, full = call(
        bind(start_kernel, nxy), [(nxy, 2 * rows + 8, NY), (NX, NY)],
        dens, *layers[1:], layer_top, *factors, *tables, scratch=[(NX, NY)], scalars=(4,),
    )
    got = exchange(message, XY)
    (sums,) = call(
        bind(collect_kernel, nxy), [(2 * rows + nxy + 2 * part, NY)], got, weight_own, obs_own
    )
    sums = from_axis([sums] * nh, "h")
    pred, pulled, weight, tops, message = call(
        bind(residual_kernel, nxy, nh),
        [(rows, NY), (rows, NY), (rows, NY), (nxy * nh, NY), (nxy, rows, NY)],
        *sums, scratch=[(rows, NY)],
    )
    program.hold(pred, pulled, weight)
    got = exchange(message, XY)
    (power,) = call(bind(power_kernel, nxy * nh), [(KEPT, NY)], tops)
    program.hold(power)
    adjoint = lambda plane: call(
        bind(adjoint_kernel, nxy), [(QX + rows, NY)] * 4,
        plane.reshape(NX, NY), *factors, power, *tables,
        scratch=[(NX, NY), (4 * rows, NY)],
    )
    pieces = from_comps(adjoint(got))
    shares, message, grad, line, image = call(
        bind(gradient_kernel, nxy, nh),
        [(devices, 128), (nxy, rows, NY), (QX, NY), (rows, NY), (rows, NY)],
        *pieces, pulled, dens, weight, scratch=[(rows, NY)],
    )
    program.drop(pulled, weight)
    program.hold(line, image)
    grads = from_comps([grad] * 4)
    shares = after(exchange(shares, ALL), *grads)
    back = exchange(after(message, shares), XY)
    message, dens, base, alpha = call(
        second_kernel, [(nxy * nh, part, NY), (QX, NY), (QX, NY), (8, 128)],
        shares, dens, full, *grads, *factors, *tables, scratch=[(NX, NY)],
    )
    program.alive = [*tables, *factors, power, weight_own, obs_own, pred, line, image]
    program.hold(dens, base, alpha)
    got = exchange(after(message, back), DEPTH)
    pieces = from_comps(adjoint(after(back, message)))
    program.alive = [weight_own, obs_own, pred, image, dens, alpha]
    grad2, image2, half = call(
        second_gradient_kernel, [(QX, NY), (rows, NY), (8, 128)],
        *pieces, alpha, base, dens, line,
    )
    program.hold(grad2)
    got = after(got, half)
    shares, image2 = call(
        curvature_kernel, [(devices, 128), (part, NY)], got, image2, weight_own, half
    )
    shares = exchange(shares, ALL)
    program.alive = []
    return tuple(
        call(
            finish_kernel, [density.shape, observed.shape],
            shares, dens, grad2, alpha, pred, image, image2, obs_own, weight_own,
        )
    )


def solution(mesh):
    depth = mesh.shape["depth"]
    sizes = {64: (4, 4, 4), 4: (2, 1, 2)}[depth]
    fine = Mesh(mesh.devices.reshape(*sizes, 2, 2), ALL)
    data = P(COMP, DEPTH, None)
    layer = P(DEPTH, COMP, None)
    return jax.shard_map(
        body,
        mesh=fine,
        in_specs=(layer, data, data, P(DEPTH)),
        out_specs=(layer, data),
        check_vma=False,
    )
```

```python
import functools
import math

import jax
import jax.numpy as jnp
import numpy as np
from jax import lax
from jax.experimental import pallas as pl
from jax.experimental.pallas import tpu as pltpu
from jax.sharding import Mesh
from jax.sharding import PartitionSpec as P

TWO_PI = 2.0 * math.pi
F32 = jnp.float32
BF16 = jnp.bfloat16
XY = ("x", "y")
DEPTH = ("x", "y", "h")
COMP = ("l", "k")
ALL = ("x", "y", "h", "l", "k")

NX = 512
NY = 256
HX = NX // 2
QX = NX // 4
HY = NY // 2


def split_table(table):
    high = table.astype(jnp.bfloat16)
    low = (table - high.astype(np.float64)).astype(jnp.bfloat16)
    return np.stack([high, low])


def basis(count, waves):
    place = np.arange(count)
    rows = []
    for wave in waves:
        norm = math.sqrt((1.0 if wave == 0 else 2.0) / count)
        rows.append(norm * np.cos(TWO_PI * (wave * place % count) / count))
    for wave in waves:
        if wave == 0:
            rows.append(math.sqrt(1.0 / count) * (1.0 - 2.0 * (place % 2)))
        else:
            rows.append(math.sqrt(2.0 / count) * np.sin(TWO_PI * (wave * place % count) / count))
    return np.stack(rows)


def make_tables():
    even = basis(NX, range(0, HX, 2))[:, :HX]
    odd = basis(NX, range(1, HX, 2))[:, :HX]
    col = basis(NY, range(HY))
    return (
        np.concatenate([split_table(even), split_table(odd)]),
        split_table(col.T),
    )


def split(value):
    high = value.astype(BF16)
    low = (value - high.astype(F32)).astype(BF16)
    return high, low


def dot(left, right):
    return jnp.dot(left, right, preferred_element_type=F32)


def dot_turned(left, right):
    return lax.dot_general(left, right, (((1,), (1,)), ((), ())), preferred_element_type=F32)


def times_table(value, high, low):
    vh, vl = split(value)
    return dot(vh, high) + (dot(vl, high) + dot(vh, low))


def times_turned(value, high, low):
    vh, vl = split(value)
    return dot_turned(vh, high) + (dot_turned(vl, high) + dot_turned(vh, low))


def table_times(high, low, value):
    vh, vl = split(value)
    return dot(high, vh) + (dot(high, vl) + dot(low, vh))


def to_waves(field, fx, ty):
    cols = times_table(field, ty[0], ty[1])
    upper, lower = cols[:HX], cols[HX:]
    return (
        table_times(fx[0], fx[1], upper + lower),
        table_times(fx[2], fx[3], upper - lower),
    )


def from_waves(even, odd, bx, ty):
    first = table_times(bx[0], bx[1], even)
    second = table_times(bx[2], bx[3], odd)
    rows = jnp.concatenate([first + second, first - second], axis=0)
    return times_turned(rows, ty[0], ty[1])


def swap_x(half):
    return jnp.concatenate([half[HX // 2 :], half[: HX // 2]], axis=0)


def swap_y(half):
    return jnp.concatenate([half[:, HY:], half[:, :HY]], axis=1)


def sines(cosines, nyquist):
    row = lax.broadcasted_iota(jnp.int32, cosines.shape, 0)
    return jnp.where(row == 0, nyquist, cosines)


def spread(ref):
    even, odd = ref[:QX], ref[QX:HX]
    return (
        jnp.concatenate([even, sines(even, ref[HX : HX + 1])], axis=0),
        jnp.concatenate([odd, odd], axis=0),
    )


def x_factors(gx_ref):
    even, odd = gx_ref[:QX], gx_ref[QX:HX]
    return jnp.concatenate([even, -even], axis=0), jnp.concatenate([odd, -odd], axis=0)


def xx_factors(gx_ref):
    even, odd = spread(gx_ref)
    return -(even * even), -(odd * odd)


def component(even, odd, gx_ref, gy_ref, comp):
    halves = []
    for half, first, second, third in zip(
        (even, odd), x_factors(gx_ref), spread(gy_ref), xx_factors(gx_ref)
    ):
        met = jnp.where(comp == 1, swap_x(half), jnp.where(comp == 2, swap_y(half), half))
        factor = jnp.where(comp == 1, first, jnp.where(comp == 2, second, third))
        halves.append(met * jnp.where(comp == 0, 1.0, factor))
    return halves


def comp_index():
    return lax.axis_index("l") * 2 + lax.axis_index("k")


KEPT = HX + 8


def wave_grid():
    row = lax.broadcasted_iota(jnp.int32, (KEPT, NY), 0)
    col = lax.broadcasted_iota(jnp.int32, (KEPT, NY), 1)
    wave_x = jnp.where(row >= HX, HX, 2 * (row % QX) + (row >= QX).astype(jnp.int32))
    nyquist_y = col == HY
    wave_y = jnp.where(nyquist_y, HY, col % HY)
    kx = wave_x.astype(F32) * (TWO_PI / NX)
    ky = wave_y.astype(F32) * (TWO_PI / NY)
    return kx, ky, col >= HY, nyquist_y


def prepare_kernel(
    top_ref, fx_in, ty_in, dens_in, weight_in, obs_in,
    fx, bx, ty, dens_ref, weight_ref, obs_ref, decay_ref, gx_ref, gy_ref,
):
    dens_ref[...] = dens_in[0]
    weight_ref[...] = weight_in[0]
    obs_ref[...] = obs_in[0]
    for place in range(4):
        table = fx_in[place]
        fx[place] = table
        bx[place] = table.astype(F32).T.astype(BF16)
    for place in range(2):
        ty[place] = ty_in[place]
    kx, ky, sine_y, nyquist_y = wave_grid()
    kabs = jnp.sqrt(kx * kx + ky * ky)
    inverse = 1.0 / jnp.maximum(kabs, TWO_PI / max(NX, NY))
    decay_ref[...] = 4.0 * jnp.exp(-kabs * top_ref[0]) * (1.0 - jnp.exp(-kabs))
    gx_ref[...] = kx * inverse
    ry = ky * inverse
    gy_ref[...] = jnp.where(nyquist_y, 0.0, jnp.where(sine_y, -ry, ry))


def gather_rows(pieces, full_ref):
    comp = comp_index()
    for step, piece in enumerate(pieces):
        full_ref[pl.ds(pl.multiple_of(jnp.bitwise_xor(comp, step) * QX, QX), QX), :] = piece[...]


def forward_plane(field, decay_ref, gx_ref, gy_ref, fx, bx, ty):
    even, odd = to_waves(field, fx, ty)
    decay = spread(decay_ref)
    even, odd = component(even * decay[0], odd * decay[1], gx_ref, gy_ref, comp_index())
    return from_waves(even, odd, bx, ty)


def start_kernel(
    nxy, m0, m1, m2, m3, top_ref, decay_ref, gx_ref, gy_ref, fx, bx, ty, out_ref, far_ref, full_ref, pull_ref, sem
):
    rows = NX // nxy
    gather_rows((m0, m1, m2, m3), full_ref)
    copy = pltpu.make_async_copy(full_ref, far_ref, sem)
    copy.start()
    dens = full_ref[...]
    pull_ref[...] = 0.5 * (dens * (1.0 / (dens * dens + 0.25)))
    for place, field in enumerate((full_ref, pull_ref)):
        plane = forward_plane(field[...], decay_ref, gx_ref, gy_ref, fx, bx, ty)
        for target in range(nxy):
            out_ref[target, place * rows : (place + 1) * rows, :] = plane[
                target * rows : (target + 1) * rows
            ]
    for target in range(nxy):
        out_ref[target, 2 * rows : 2 * rows + 8, :] = jnp.full((8, NY), top_ref[0], F32)
    copy.wait()


def collect_kernel(nxy, got_ref, weight_ref, obs_ref, sum_ref):
    rows = NX // nxy
    total = got_ref[0, : 2 * rows, :]
    for source in range(1, nxy):
        total = total + got_ref[source, : 2 * rows, :]
    sum_ref[: 2 * rows] = total
    for source in range(nxy):
        place = 2 * rows + source
        sum_ref[place : place + 1, :] = got_ref[source, 2 * rows : 2 * rows + 1, :]
    part = weight_ref.shape[0]
    start = 2 * rows + nxy
    sum_ref[start : start + part] = weight_ref[...]
    sum_ref[start + part : start + 2 * part] = obs_ref[...]


def residual_kernel(nxy, nh, *refs):
    rows = NX // nxy
    part = rows // nh
    start = 2 * rows + nxy
    sums = refs[:nh]
    pred_ref, pull_ref, weight_ref, tops_ref, send_ref, meas_ref = refs[nh:]
    chip = lax.axis_index("h")
    total = sums[0][: 2 * rows]
    for step in range(1, nh):
        total = total + sums[step][: 2 * rows]
    for step in range(nh):
        tops_ref[step * nxy : (step + 1) * nxy] = sums[step][2 * rows : start]
        place = pl.ds(pl.multiple_of(lax.rem(chip + (nh - step), nh) * part, part), part)
        weight_ref[place, :] = sums[step][start : start + part]
        meas_ref[place, :] = sums[step][start + part :]
    weight = weight_ref[...]
    pred = total[:rows]
    pred_ref[...] = pred
    pull_ref[...] = total[rows:]
    res = weight * (weight * (pred - meas_ref[...]))
    for target in range(nxy):
        send_ref[target] = res


def power_kernel(layers, tops_ref, power_ref):
    kx, ky, *_ = wave_grid()
    for start in range(0, KEPT, 64):
        stop = min(start + 64, KEPT)
        ks = jnp.sqrt(kx[start:stop] ** 2 + ky[start:stop] ** 2)
        double = -2.0 * ks

        def add(step, total):
            for layer in range(4):
                total = total + jnp.exp(double * tops_ref[pl.ds(4 * step + layer, 1), :])
            return total

        total = lax.fori_loop(0, layers // 4, add, jnp.zeros_like(ks))
        rise = 1.0 - jnp.exp(-ks)
        power_ref[start:stop] = (16.0 * (rise * rise)) * total


def adjoint_kernel(
    nxy, res_ref, decay_ref, gx_ref, gy_ref, power_ref, fx, bx, ty, o0, o1, o2, o3, z_ref, i_ref
):
    rows = NX // nxy
    comp = comp_index()
    even, odd = to_waves(res_ref[...], fx, ty)
    even, odd = component(even, odd, gx_ref, gy_ref, comp)
    sign = jnp.where((comp == 1) | (comp == 2), -1.0, 1.0)
    even = even * sign
    odd = odd * sign
    decay = spread(decay_ref)
    z_ref[...] = from_waves(even * decay[0], odd * decay[1], bx, ty)
    power = spread(power_ref)
    even = even * power[0]
    odd = odd * power[1]
    block = lax.axis_index("x") * lax.axis_size("y") + lax.axis_index("y")
    upper = block * rows < HX
    near = pl.ds(pl.multiple_of(lax.rem(block * rows, HX), rows), rows)
    flip = jnp.where(upper, 1.0, -1.0)
    for target in range(4):
        if target == 0:
            e, o = even, odd
        elif target == 1:
            first = x_factors(gx_ref)
            e, o = swap_x(even) * first[0], swap_x(odd) * first[1]
        elif target == 2:
            second = spread(gy_ref)
            e, o = swap_y(even) * second[0], swap_y(odd) * second[1]
        else:
            third = xx_factors(gx_ref)
            e, o = even * third[0], odd * third[1]
        line = table_times(bx[0, near, :], bx[1, near, :], e)
        line = line + flip * table_times(bx[2, near, :], bx[3, near, :], o)
        i_ref[target * rows : (target + 1) * rows, :] = line
    i_ref[...] = times_turned(i_ref[...], ty[0], ty[1])
    for step, out in enumerate((o0, o1, o2, o3)):
        other = jnp.bitwise_xor(comp, step)
        out[:QX] = z_ref[pl.ds(pl.multiple_of(other * QX, QX), QX), :]
        out[QX:] = i_ref[pl.ds(pl.multiple_of(other * rows, rows), rows), :]


def share(grad, quad, image, weight, scratch, part):
    scratch[...] = weight * image
    place = pl.ds(pl.multiple_of(lax.axis_index("h") * part, part), part)
    mine = scratch[place, :]
    lane = lax.broadcasted_iota(jnp.int32, (1, NY), 1)
    square = grad * grad
    gg = jnp.sum(square)
    qgg = jnp.sum(quad * square)
    curv = jnp.sum(mine * mine)
    return jnp.where(lane == 0, gg, jnp.where(lane == 1, qgg, jnp.where(lane == 2, curv, 0.0)))


def step_length(shares):
    total = jnp.sum(shares, axis=0, keepdims=True)
    lane = lax.broadcasted_iota(jnp.int32, total.shape, 1)
    pick = lambda place: jnp.sum(jnp.where(lane == place, total, 0.0), keepdims=True)
    return pick(0) / (pick(2) + 0.5 * pick(1))


def gradient_kernel(nxy, nh, *refs):
    rows = NX // nxy
    part = rows // nh
    pieces = refs[:4]
    pull_ref, dens_ref, weight_ref = refs[4:7]
    send_ref, grad_ref, line_ref, image_ref, scratch = refs[7:]
    total = pieces[0][...] + pieces[1][...] + (pieces[2][...] + pieces[3][...])
    data = total[:QX]
    line = total[QX:]
    dens = dens_ref[...]
    quad = 1.0 / (dens * dens + 0.25)
    grad = data + 0.5 * (quad * dens)
    image = line + pull_ref[...]
    weight = weight_ref[...]
    mine = jnp.broadcast_to(share(grad, quad, image, weight, scratch, part), (8, NY))
    grad_ref[...] = grad
    line_ref[...] = line
    image_ref[...] = image
    back = weight * (weight * image)
    for target in range(nxy):
        send_ref[target, :rows] = back
        send_ref[target, rows:] = mine


def part_kernel(nxy, got_ref, plane_ref, share_ref):
    rows = NX // nxy
    total = got_ref[0, rows:, :]
    for source in range(1, nxy):
        total = total + got_ref[source, rows:, :]
    share_ref[...] = total
    for source in range(nxy):
        plane_ref[source * rows : (source + 1) * rows] = got_ref[source, :rows, :]


def add_kernel(*refs):
    total = refs[0][...]
    for part in refs[1:-1]:
        total = total + part[...]
    refs[-1][...] = total


def second_kernel(
    s0, s1, s2, s3, dens_ref, full_ref, g0, g1, g2, g3, decay_ref, gx_ref, gy_ref, fx, bx, ty,
    out_ref, dens_out, base_out, alpha_ref, all_ref, near_ref, sems,
):
    comp = comp_index()
    copies = [pltpu.make_async_copy(full_ref, near_ref, sems.at[4])]
    for step, piece in enumerate((g0, g1, g2, g3)):
        place = pl.ds(pl.multiple_of(jnp.bitwise_xor(comp, step) * QX, QX), QX)
        copies.append(pltpu.make_async_copy(piece, all_ref.at[place, :], sems.at[step]))
    for copy in copies:
        copy.start()
    alpha = step_length(s0[:1] + s1[:1] + (s2[:1] + s3[:1]))
    alpha_ref[...] = jnp.broadcast_to(alpha, alpha_ref.shape)
    old = dens_ref[...]
    for copy in copies:
        copy.wait()
    grad = all_ref[pl.ds(pl.multiple_of(comp * QX, QX), QX), :]
    dens = old - alpha * grad
    dens_out[...] = dens
    data = grad - 0.5 * ((1.0 / (old * old + 0.25)) * old)
    base_out[...] = data + 0.5 * (dens * (1.0 / (dens * dens + 0.25)))
    dens = near_ref[...] - alpha * all_ref[...]
    all_ref[...] = 0.5 * (dens * (1.0 / (dens * dens + 0.25)))
    plane = forward_plane(all_ref[...], decay_ref, gx_ref, gy_ref, fx, bx, ty)
    out_ref[...] = plane.reshape(out_ref.shape)


def sum_kernel(nxy, got_ref, sum_ref):
    total = got_ref[0]
    for source in range(1, nxy):
        total = total + got_ref[source]
    sum_ref[...] = total


def second_gradient_kernel(
    u0, u1, u2, u3, alpha_ref, base_ref, dens_ref, line_ref, grad_ref, image_ref, share_ref
):
    alpha = alpha_ref[:1, :1]
    total = u0[...] + u1[...] + (u2[...] + u3[...])
    dens = dens_ref[...]
    grad = base_ref[...] - alpha * total[:QX]
    quad = 1.0 / (dens * dens + 0.25)
    grad_ref[...] = grad
    image_ref[...] = line_ref[...] - alpha * total[QX:]
    square = grad * grad
    lane = lax.broadcasted_iota(jnp.int32, (8, 128), 1)
    share_ref[...] = jnp.where(
        lane == 0, jnp.sum(square), jnp.where(lane == 1, jnp.sum(quad * square), 0.0)
    )


def curvature_kernel(nh, *refs):
    parts = refs[:nh]
    image_ref, weight_ref, part_ref, share_ref, out_ref = refs[nh:]
    part = weight_ref.shape[0]
    place = pl.ds(pl.multiple_of(lax.axis_index("h") * part, part), part)
    image = image_ref[place, :]
    for piece in parts:
        image = image + piece[place, :]
    out_ref[...] = image
    mine = weight_ref[...] * image
    lane = lax.broadcasted_iota(jnp.int32, (1, 128), 1)
    share_ref[...] = jnp.broadcast_to(
        jnp.where(lane == 2, jnp.sum(mine * mine), part_ref[:1]), share_ref.shape
    )


def finish_kernel(
    shares_ref, dens_ref, grad_ref, alpha_ref, pred_ref, first_ref, second_ref, obs_ref, w_ref, dens_out, err_out
):
    part = obs_ref.shape[0]
    alpha = step_length(shares_ref[...])
    dens_out[0] = dens_ref[...] - alpha * grad_ref[...]
    place = pl.ds(pl.multiple_of(lax.axis_index("h") * part, part), part)
    pred = pred_ref[place, :] - alpha_ref[:1, :1] * first_ref[place, :]
    pred = pred - alpha * second_ref[...]
    err_out[0] = w_ref[...] * (pred - obs_ref[...])


VMEM = pl.BlockSpec(memory_space=pltpu.VMEM)
SMEM = pl.BlockSpec(memory_space=pltpu.SMEM)
ANY = pl.BlockSpec(memory_space=pl.ANY)


class Program:
    def __init__(self):
        self.alive = []

    def hold(self, *values):
        self.alive += values

    def drop(self, *values):
        self.alive = [item for item in self.alive if all(item is not value for value in values)]

    def call(self, kernel, outs, *args, scratch=(), scalars=(), far=(), far_out=(), sems=0, mib=8):
        used = len(args)
        keep = [item for item in self.alive if all(item is not value for value in args)]
        kept = len(keep)

        def inner(*refs):
            kernel(*refs[:used], *refs[used + kept :])

        kinds = [(item, F32) if isinstance(item, tuple) else (item.shape, item.dtype) for item in outs]
        return pl.pallas_call(
            inner,
            out_shape=[jax.ShapeDtypeStruct(shape, dtype) for shape, dtype in kinds],
            in_specs=[
                SMEM if place in scalars else ANY if place in far else VMEM for place in range(used)
            ]
            + [ANY] * kept,
            out_specs=[ANY if place in far_out else VMEM for place in range(len(outs))],
            scratch_shapes=[pltpu.VMEM(shape, F32) for shape in scratch]
            + [pltpu.SemaphoreType.DMA((sems,) if sems > 1 else ())] * (sems > 0),
            compiler_params=pltpu.CompilerParams(vmem_limit_bytes=mib << 20),
        )(*args, *keep)


def from_comps(values):
    return [values[0]] + [
        lax.ppermute(values[step], COMP, [(i, i ^ step) for i in range(4)]) for step in (1, 2, 3)
    ]


def from_axis(values, axis):
    size = len(values)
    return [values[0]] + [
        lax.ppermute(values[step], axis, [(i, (i + step) % size) for i in range(size)])
        for step in range(1, size)
    ]


def exchange(value, axes):
    return lax.all_to_all(value, axes, 0, 0, tiled=True)


def after(values, *others):
    if isinstance(values, (list, tuple)):
        return list(lax.optimization_barrier((tuple(values), others))[0])
    return lax.optimization_barrier((values, others))[0]


def body(density, observed, data_weight, layer_top):
    nx, ny, nh = (lax.axis_size(axis) for axis in DEPTH)
    nxy = nx * ny
    devices = nxy * nh * 4
    rows = NX // nxy
    part = rows // nh
    fx, ty = (jnp.asarray(table) for table in make_tables())
    bind = functools.partial
    program = Program()
    call = program.call

    layers = from_comps([density[0]] * 4)
    *tables, dens, weight_own, obs_own, decay, gx, gy = call(
        prepare_kernel,
        [
            fx, fx, ty, (QX, NY), (part, NY), (part, NY), (KEPT, NY), (KEPT, NY), (KEPT, NY),
        ],
        layer_top, fx, ty, density, data_weight, observed, scalars=(0,),
    )
    factors = (decay, gx, gy)
    program.hold(*tables, *factors, dens, weight_own, obs_own)
    message, full = call(
        bind(start_kernel, nxy), [(nxy, 2 * rows + 8, NY), (NX, NY)],
        dens, *layers[1:], layer_top, *factors, *tables,
        scratch=[(NX, NY)] * 2, scalars=(4,), far_out=(1,), sems=1,
    )
    got = exchange(message, XY)
    (sums,) = call(
        bind(collect_kernel, nxy), [(2 * rows + nxy + 2 * part, NY)], got, weight_own, obs_own
    )
    sums = from_axis([sums] * nh, "h")
    pred, pulled, weight, tops, message = call(
        bind(residual_kernel, nxy, nh),
        [(rows, NY), (rows, NY), (rows, NY), (nxy * nh, NY), (nxy, rows, NY)],
        *sums, scratch=[(rows, NY)],
    )
    program.hold(pred, pulled, weight)
    got = exchange(message, XY)
    (power,) = call(bind(power_kernel, nxy * nh), [(KEPT, NY)], tops)
    program.hold(power)
    adjoint = lambda plane: call(
        bind(adjoint_kernel, nxy), [(QX + rows, NY)] * 4,
        plane.reshape(NX, NY), *factors, power, *tables,
        scratch=[(NX, NY), (4 * rows, NY)],
    )
    pieces = from_comps(adjoint(got))
    message, grad, line, image = call(
        bind(gradient_kernel, nxy, nh),
        [(nxy, rows + 8, NY), (QX, NY), (rows, NY), (rows, NY)],
        *pieces, pulled, dens, weight, scratch=[(rows, NY)],
    )
    program.drop(pulled, weight)
    program.hold(line, image)
    grads = from_comps([grad] * 4)
    got = after(exchange(message, XY), *grads)
    plane, shares = call(bind(part_kernel, nxy), [(NX, NY), (8, NY)], got)
    pieces = adjoint(plane)
    shares = after(from_axis([shares] * nh, "h"), *pieces)
    (shares,) = call(add_kernel, [(8, NY)], *shares)
    shares = from_comps([shares] * 4)
    message, dens, base, alpha = call(
        second_kernel, [(nxy, rows, NY), (QX, NY), (QX, NY), (8, 128)],
        *shares, dens, full, *grads, *factors, *tables,
        scratch=[(NX, NY)] * 2, far=(5, 6, 7, 8, 9), sems=5,
    )
    program.alive = [weight_own, obs_own, pred, line, image, dens, base, alpha]
    got = exchange(message, XY)
    pieces = from_comps(after(pieces, message))
    grad2, image2, half = call(
        second_gradient_kernel, [(QX, NY), (rows, NY), (8, 128)],
        *pieces, alpha, base, dens, line,
    )
    (parts,) = call(bind(sum_kernel, nxy), [(rows, NY)], got)
    parts = after(from_axis([parts] * nh, "h"), half)
    program.alive = [obs_own, pred, image, dens, alpha, grad2]
    shares, image2 = call(
        bind(curvature_kernel, nh), [(devices, 128), (part, NY)], *parts, image2, weight_own, half
    )
    shares = exchange(shares, ALL)
    program.alive = []
    return tuple(
        call(
            finish_kernel, [density.shape, observed.shape],
            shares, dens, grad2, alpha, pred, image, image2, obs_own, weight_own,
        )
    )


def solution(mesh):
    depth = mesh.shape["depth"]
    sizes = {64: (4, 4, 4), 4: (2, 1, 2)}[depth]
    fine = Mesh(mesh.devices.reshape(*sizes, 2, 2), ALL)
    data = P(COMP, DEPTH, None)
    layer = P(DEPTH, COMP, None)
    return jax.shard_map(
        body,
        mesh=fine,
        in_specs=(layer, data, data, P(DEPTH)),
        out_specs=(layer, data),
        check_vma=False,
    )
```

```python
import functools
import math

import jax
import jax.numpy as jnp
import numpy as np
from jax import lax
from jax.experimental import pallas as pl
from jax.experimental.pallas import tpu as pltpu
from jax.sharding import Mesh
from jax.sharding import PartitionSpec as P

TWO_PI = 2.0 * math.pi
F32 = jnp.float32
BF16 = jnp.bfloat16
XY = ("x", "y")
DEPTH = ("x", "y", "h")
COMP = ("l", "k")
ALL = ("x", "y", "h", "l", "k")

NX = 512
NY = 256
HX = NX // 2
QX = NX // 4
HY = NY // 2


def split_table(table):
    high = table.astype(jnp.bfloat16)
    low = (table - high.astype(np.float64)).astype(jnp.bfloat16)
    return np.stack([high, low])


def basis(count, waves):
    place = np.arange(count)
    rows = []
    for wave in waves:
        norm = math.sqrt((1.0 if wave == 0 else 2.0) / count)
        rows.append(norm * np.cos(TWO_PI * (wave * place % count) / count))
    for wave in waves:
        if wave == 0:
            rows.append(math.sqrt(1.0 / count) * (1.0 - 2.0 * (place % 2)))
        else:
            rows.append(math.sqrt(2.0 / count) * np.sin(TWO_PI * (wave * place % count) / count))
    return np.stack(rows)


def make_tables():
    even = basis(NX, range(0, HX, 2))[:, :HX]
    odd = basis(NX, range(1, HX, 2))[:, :HX]
    col = basis(NY, range(HY))
    return (
        np.concatenate([split_table(even), split_table(odd)]),
        split_table(col.T),
    )


def split(value):
    high = value.astype(BF16)
    low = (value - high.astype(F32)).astype(BF16)
    return high, low


def dot(left, right):
    return jnp.dot(left, right, preferred_element_type=F32)


def dot_turned(left, right):
    return lax.dot_general(left, right, (((1,), (1,)), ((), ())), preferred_element_type=F32)


def times_table(value, high, low):
    vh, vl = split(value)
    return dot(vh, high) + (dot(vl, high) + dot(vh, low))


def times_turned(value, high, low):
    vh, vl = split(value)
    return dot_turned(vh, high) + (dot_turned(vl, high) + dot_turned(vh, low))


def table_times(high, low, value):
    vh, vl = split(value)
    return dot(high, vh) + (dot(high, vl) + dot(low, vh))


def to_waves(field, fx, ty):
    cols = times_table(field, ty[0], ty[1])
    upper, lower = cols[:HX], cols[HX:]
    return (
        table_times(fx[0], fx[1], upper + lower),
        table_times(fx[2], fx[3], upper - lower),
    )


def from_waves(even, odd, bx, ty):
    first = table_times(bx[0], bx[1], even)
    second = table_times(bx[2], bx[3], odd)
    rows = jnp.concatenate([first + second, first - second], axis=0)
    return times_turned(rows, ty[0], ty[1])


def swap_x(half):
    return jnp.concatenate([half[HX // 2 :], half[: HX // 2]], axis=0)


def swap_y(half):
    return jnp.concatenate([half[:, HY:], half[:, :HY]], axis=1)


def sines(cosines, nyquist):
    row = lax.broadcasted_iota(jnp.int32, cosines.shape, 0)
    return jnp.where(row == 0, nyquist, cosines)


def spread(ref):
    even, odd = ref[:QX], ref[QX:HX]
    return (
        jnp.concatenate([even, sines(even, ref[HX : HX + 1])], axis=0),
        jnp.concatenate([odd, odd], axis=0),
    )


def x_factors(gx_ref):
    even, odd = gx_ref[:QX], gx_ref[QX:HX]
    return jnp.concatenate([even, -even], axis=0), jnp.concatenate([odd, -odd], axis=0)


def xx_factors(gx_ref):
    even, odd = spread(gx_ref)
    return -(even * even), -(odd * odd)


def component(even, odd, gx_ref, gy_ref, comp):
    halves = []
    for half, first, second, third in zip(
        (even, odd), x_factors(gx_ref), spread(gy_ref), xx_factors(gx_ref)
    ):
        met = jnp.where(comp == 1, swap_x(half), jnp.where(comp == 2, swap_y(half), half))
        factor = jnp.where(comp == 1, first, jnp.where(comp == 2, second, third))
        halves.append(met * jnp.where(comp == 0, 1.0, factor))
    return halves


def comp_index():
    return lax.axis_index("l") * 2 + lax.axis_index("k")


KEPT = HX + 8


def wave_grid():
    row = lax.broadcasted_iota(jnp.int32, (KEPT, NY), 0)
    col = lax.broadcasted_iota(jnp.int32, (KEPT, NY), 1)
    wave_x = jnp.where(row >= HX, HX, 2 * (row % QX) + (row >= QX).astype(jnp.int32))
    nyquist_y = col == HY
    wave_y = jnp.where(nyquist_y, HY, col % HY)
    kx = wave_x.astype(F32) * (TWO_PI / NX)
    ky = wave_y.astype(F32) * (TWO_PI / NY)
    return kx, ky, col >= HY, nyquist_y


def prepare_kernel(
    top_ref, fx_in, ty_in, dens_in, weight_in, obs_in,
    fx, bx, ty, dens_ref, weight_ref, obs_ref, decay_ref, gx_ref, gy_ref,
):
    dens_ref[...] = dens_in[0]
    weight_ref[...] = weight_in[0]
    obs_ref[...] = obs_in[0]
    for place in range(4):
        table = fx_in[place]
        fx[place] = table
        bx[place] = table.astype(F32).T.astype(BF16)
    for place in range(2):
        ty[place] = ty_in[place]
    kx, ky, sine_y, nyquist_y = wave_grid()
    kabs = jnp.sqrt(kx * kx + ky * ky)
    inverse = 1.0 / jnp.maximum(kabs, TWO_PI / max(NX, NY))
    decay_ref[...] = 4.0 * jnp.exp(-kabs * top_ref[0]) * (1.0 - jnp.exp(-kabs))
    gx_ref[...] = kx * inverse
    ry = ky * inverse
    gy_ref[...] = jnp.where(nyquist_y, 0.0, jnp.where(sine_y, -ry, ry))


def gather_rows(pieces, full_ref):
    comp = comp_index()
    for step, piece in enumerate(pieces):
        full_ref[pl.ds(pl.multiple_of(jnp.bitwise_xor(comp, step) * QX, QX), QX), :] = piece[...]


def forward_plane(field, decay_ref, gx_ref, gy_ref, fx, bx, ty):
    even, odd = to_waves(field, fx, ty)
    decay = spread(decay_ref)
    even, odd = component(even * decay[0], odd * decay[1], gx_ref, gy_ref, comp_index())
    return from_waves(even, odd, bx, ty)


def start_kernel(
    nxy, m0, m1, m2, m3, top_ref, decay_ref, gx_ref, gy_ref, fx, bx, ty, out_ref, full_ref
):
    rows = NX // nxy
    gather_rows((m0, m1, m2, m3), full_ref)
    plane = forward_plane(full_ref[...], decay_ref, gx_ref, gy_ref, fx, bx, ty)
    for target in range(nxy):
        out_ref[target, :rows, :] = plane[target * rows : (target + 1) * rows]
        out_ref[target, rows:, :] = jnp.full((8, NY), top_ref[0], F32)


def pull_kernel(full_ref, decay_ref, gx_ref, gy_ref, fx, bx, ty, out_ref):
    dens = full_ref[...]
    pull = 0.5 * (dens * (1.0 / (dens * dens + 0.25)))
    plane = forward_plane(pull, decay_ref, gx_ref, gy_ref, fx, bx, ty)
    out_ref[...] = plane.reshape(out_ref.shape)


def collect_kernel(nxy, got_ref, weight_ref, obs_ref, sum_ref):
    rows = NX // nxy
    total = got_ref[0, :rows, :]
    for source in range(1, nxy):
        total = total + got_ref[source, :rows, :]
    sum_ref[:rows] = total
    for source in range(nxy):
        sum_ref[rows + source : rows + source + 1, :] = got_ref[source, rows : rows + 1, :]
    part = weight_ref.shape[0]
    start = rows + nxy
    sum_ref[start : start + part] = weight_ref[...]
    sum_ref[start + part : start + 2 * part] = obs_ref[...]


def residual_kernel(nxy, nh, *refs):
    rows = NX // nxy
    part = rows // nh
    start = rows + nxy
    sums = refs[:nh]
    pred_ref, weight_ref, tops_ref, send_ref, meas_ref = refs[nh:]
    chip = lax.axis_index("h")
    pred = sums[0][:rows]
    for step in range(1, nh):
        pred = pred + sums[step][:rows]
    for step in range(nh):
        tops_ref[step * nxy : (step + 1) * nxy] = sums[step][rows:start]
        place = pl.ds(pl.multiple_of(lax.rem(chip + (nh - step), nh) * part, part), part)
        weight_ref[place, :] = sums[step][start : start + part]
        meas_ref[place, :] = sums[step][start + part :]
    weight = weight_ref[...]
    pred_ref[...] = pred
    res = weight * (weight * (pred - meas_ref[...]))
    for target in range(nxy):
        send_ref[target] = res


def power_kernel(layers, tops_ref, power_ref):
    kx, ky, *_ = wave_grid()
    for start in range(0, KEPT, 64):
        stop = min(start + 64, KEPT)
        ks = jnp.sqrt(kx[start:stop] ** 2 + ky[start:stop] ** 2)
        double = -2.0 * ks

        def add(step, total):
            for layer in range(4):
                total = total + jnp.exp(double * tops_ref[pl.ds(4 * step + layer, 1), :])
            return total

        total = lax.fori_loop(0, layers // 4, add, jnp.zeros_like(ks))
        rise = 1.0 - jnp.exp(-ks)
        power_ref[start:stop] = (16.0 * (rise * rise)) * total


def adjoint_kernel(
    nxy, res_ref, decay_ref, gx_ref, gy_ref, power_ref, fx, bx, ty, o0, o1, o2, o3, z_ref, i_ref
):
    rows = NX // nxy
    comp = comp_index()
    even, odd = to_waves(res_ref[...], fx, ty)
    even, odd = component(even, odd, gx_ref, gy_ref, comp)
    sign = jnp.where((comp == 1) | (comp == 2), -1.0, 1.0)
    even = even * sign
    odd = odd * sign
    decay = spread(decay_ref)
    z_ref[...] = from_waves(even * decay[0], odd * decay[1], bx, ty)
    power = spread(power_ref)
    even = even * power[0]
    odd = odd * power[1]
    block = lax.axis_index("x") * lax.axis_size("y") + lax.axis_index("y")
    upper = block * rows < HX
    near = pl.ds(pl.multiple_of(lax.rem(block * rows, HX), rows), rows)
    flip = jnp.where(upper, 1.0, -1.0)
    for target in range(4):
        if target == 0:
            e, o = even, odd
        elif target == 1:
            first = x_factors(gx_ref)
            e, o = swap_x(even) * first[0], swap_x(odd) * first[1]
        elif target == 2:
            second = spread(gy_ref)
            e, o = swap_y(even) * second[0], swap_y(odd) * second[1]
        else:
            third = xx_factors(gx_ref)
            e, o = even * third[0], odd * third[1]
        line = table_times(bx[0, near, :], bx[1, near, :], e)
        line = line + flip * table_times(bx[2, near, :], bx[3, near, :], o)
        i_ref[target * rows : (target + 1) * rows, :] = line
    i_ref[...] = times_turned(i_ref[...], ty[0], ty[1])
    for step, out in enumerate((o0, o1, o2, o3)):
        other = jnp.bitwise_xor(comp, step)
        out[:QX] = z_ref[pl.ds(pl.multiple_of(other * QX, QX), QX), :]
        out[QX:] = i_ref[pl.ds(pl.multiple_of(other * rows, rows), rows), :]


def share(grad, quad, image, weight, scratch, part):
    scratch[...] = weight * image
    place = pl.ds(pl.multiple_of(lax.axis_index("h") * part, part), part)
    mine = scratch[place, :]
    lane = lax.broadcasted_iota(jnp.int32, (1, NY), 1)
    square = grad * grad
    gg = jnp.sum(square)
    qgg = jnp.sum(quad * square)
    curv = jnp.sum(mine * mine)
    return jnp.where(lane == 0, gg, jnp.where(lane == 1, qgg, jnp.where(lane == 2, curv, 0.0)))


def step_length(shares):
    total = jnp.sum(shares, axis=0, keepdims=True)
    lane = lax.broadcasted_iota(jnp.int32, total.shape, 1)
    pick = lambda place: jnp.sum(jnp.where(lane == place, total, 0.0), keepdims=True)
    return pick(0) / (pick(2) + 0.5 * pick(1))


def gradient_kernel(nxy, nh, *refs):
    rows = NX // nxy
    part = rows // nh
    pieces, pulls = refs[:4], refs[4 : 4 + nh]
    dens_ref, weight_ref = refs[4 + nh : 6 + nh]
    send_ref, grad_ref, line_ref, image_ref, scratch = refs[6 + nh :]
    total = pieces[0][...] + pieces[1][...] + (pieces[2][...] + pieces[3][...])
    data = total[:QX]
    line = total[QX:]
    dens = dens_ref[...]
    quad = 1.0 / (dens * dens + 0.25)
    grad = data + 0.5 * (quad * dens)
    image = line
    for pull in pulls:
        image = image + pull[...]
    weight = weight_ref[...]
    back = weight * (weight * image)
    mine = jnp.broadcast_to(share(grad, quad, image, weight, scratch, part), (8, NY))
    grad_ref[...] = grad
    line_ref[...] = line
    image_ref[...] = image
    for target in range(nxy):
        send_ref[target, :rows] = back
        send_ref[target, rows:] = mine


def part_kernel(nxy, got_ref, plane_ref, share_ref):
    rows = NX // nxy
    total = got_ref[0, rows:, :]
    for source in range(1, nxy):
        total = total + got_ref[source, rows:, :]
    share_ref[...] = total
    for source in range(nxy):
        plane_ref[source * rows : (source + 1) * rows] = got_ref[source, :rows, :]


def add_kernel(*refs):
    total = refs[0][...]
    for part in refs[1:-1]:
        total = total + part[...]
    refs[-1][...] = total


def second_kernel(
    s0, s1, s2, s3, dens_ref, full_ref, g0, g1, g2, g3, decay_ref, gx_ref, gy_ref, fx, bx, ty,
    out_ref, dens_out, base_out, alpha_ref, all_ref,
):
    gather_rows((g0, g1, g2, g3), all_ref)
    alpha = step_length(s0[:1] + s1[:1] + (s2[:1] + s3[:1]))
    alpha_ref[...] = jnp.broadcast_to(alpha, alpha_ref.shape)
    old = dens_ref[...]
    grad = g0[...]
    dens = old - alpha * grad
    dens_out[...] = dens
    data = grad - 0.5 * ((1.0 / (old * old + 0.25)) * old)
    base_out[...] = data + 0.5 * (dens * (1.0 / (dens * dens + 0.25)))
    dens = full_ref[...] - alpha * all_ref[...]
    all_ref[...] = 0.5 * (dens * (1.0 / (dens * dens + 0.25)))
    plane = forward_plane(all_ref[...], decay_ref, gx_ref, gy_ref, fx, bx, ty)
    out_ref[...] = plane.reshape(out_ref.shape)


def sum_kernel(nxy, got_ref, sum_ref):
    total = got_ref[0]
    for source in range(1, nxy):
        total = total + got_ref[source]
    sum_ref[...] = total


def second_gradient_kernel(
    u0, u1, u2, u3, alpha_ref, base_ref, dens_ref, line_ref, grad_ref, image_ref, share_ref
):
    alpha = alpha_ref[:1, :1]
    total = u0[...] + u1[...] + (u2[...] + u3[...])
    dens = dens_ref[...]
    grad = base_ref[...] - alpha * total[:QX]
    quad = 1.0 / (dens * dens + 0.25)
    grad_ref[...] = grad
    image_ref[...] = line_ref[...] - alpha * total[QX:]
    square = grad * grad
    lane = lax.broadcasted_iota(jnp.int32, (8, 128), 1)
    share_ref[...] = jnp.where(
        lane == 0, jnp.sum(square), jnp.where(lane == 1, jnp.sum(quad * square), 0.0)
    )


def curvature_kernel(nh, *refs):
    parts = refs[:nh]
    image_ref, weight_ref, part_ref, share_ref, out_ref = refs[nh:]
    part = weight_ref.shape[0]
    place = pl.ds(pl.multiple_of(lax.axis_index("h") * part, part), part)
    image = image_ref[place, :]
    for piece in parts:
        image = image + piece[place, :]
    out_ref[...] = image
    mine = weight_ref[...] * image
    lane = lax.broadcasted_iota(jnp.int32, (1, 128), 1)
    share_ref[...] = jnp.broadcast_to(
        jnp.where(lane == 2, jnp.sum(mine * mine), part_ref[:1]), share_ref.shape
    )


def finish_kernel(
    shares_ref, dens_ref, grad_ref, alpha_ref, pred_ref, first_ref, second_ref, obs_ref, w_ref, dens_out, err_out
):
    part = obs_ref.shape[0]
    alpha = step_length(shares_ref[...])
    dens_out[0] = dens_ref[...] - alpha * grad_ref[...]
    place = pl.ds(pl.multiple_of(lax.axis_index("h") * part, part), part)
    pred = pred_ref[place, :] - alpha_ref[:1, :1] * first_ref[place, :]
    pred = pred - alpha * second_ref[...]
    err_out[0] = w_ref[...] * (pred - obs_ref[...])


VMEM = pl.BlockSpec(memory_space=pltpu.VMEM)
SMEM = pl.BlockSpec(memory_space=pltpu.SMEM)
ANY = pl.BlockSpec(memory_space=pl.ANY)


class Program:
    def __init__(self):
        self.alive = []

    def hold(self, *values):
        self.alive += values

    def drop(self, *values):
        self.alive = [item for item in self.alive if all(item is not value for value in values)]

    def call(self, kernel, outs, *args, scratch=(), scalars=(), mib=8):
        used = len(args)
        keep = [item for item in self.alive if all(item is not value for value in args)]
        kept = len(keep)

        def inner(*refs):
            kernel(*refs[:used], *refs[used + kept :])

        kinds = [(item, F32) if isinstance(item, tuple) else (item.shape, item.dtype) for item in outs]
        return pl.pallas_call(
            inner,
            out_shape=[jax.ShapeDtypeStruct(shape, dtype) for shape, dtype in kinds],
            in_specs=[
                SMEM if place in scalars else VMEM for place in range(used)
            ]
            + [ANY] * kept,
            out_specs=[VMEM] * len(outs),
            scratch_shapes=[pltpu.VMEM(shape, F32) for shape in scratch],
            compiler_params=pltpu.CompilerParams(vmem_limit_bytes=mib << 20),
        )(*args, *keep)


def from_comps(values):
    return [values[0]] + [
        lax.ppermute(values[step], COMP, [(i, i ^ step) for i in range(4)]) for step in (1, 2, 3)
    ]


def from_axis(values, axis):
    size = len(values)
    return [values[0]] + [
        lax.ppermute(values[step], axis, [(i, (i + step) % size) for i in range(size)])
        for step in range(1, size)
    ]


def exchange(value, axes):
    return lax.all_to_all(value, axes, 0, 0, tiled=True)


def after(values, *others):
    if isinstance(values, (list, tuple)):
        return list(lax.optimization_barrier((tuple(values), others))[0])
    return lax.optimization_barrier((values, others))[0]


def body(density, observed, data_weight, layer_top):
    nx, ny, nh = (lax.axis_size(axis) for axis in DEPTH)
    nxy = nx * ny
    devices = nxy * nh * 4
    rows = NX // nxy
    part = rows // nh
    fx, ty = (jnp.asarray(table) for table in make_tables())
    bind = functools.partial
    program = Program()
    call = program.call

    layers = from_comps([density[0]] * 4)
    *tables, dens, weight_own, obs_own, decay, gx, gy = call(
        prepare_kernel,
        [
            fx, fx, ty, (QX, NY), (part, NY), (part, NY), (KEPT, NY), (KEPT, NY), (KEPT, NY),
        ],
        layer_top, fx, ty, density, data_weight, observed, scalars=(0,),
    )
    factors = (decay, gx, gy)
    program.hold(*tables, *factors, dens, weight_own, obs_own)
    message, full = call(
        bind(start_kernel, nxy), [(nxy, rows + 8, NY), (NX, NY)],
        dens, *layers[1:], layer_top, *factors, *tables, scalars=(4,),
    )
    got = exchange(message, XY)
    (pull_message,) = call(
        pull_kernel, [(nxy, rows, NY)], after(full, message), *factors, *tables
    )
    got = after(got, pull_message)
    (sums,) = call(
        bind(collect_kernel, nxy), [(rows + nxy + 2 * part, NY)], got, weight_own, obs_own
    )
    pulled = exchange(after(pull_message, sums), XY)
    sums = from_axis([sums] * nh, "h")
    pred, weight, tops, message = call(
        bind(residual_kernel, nxy, nh),
        [(rows, NY), (rows, NY), (nxy * nh, NY), (nxy, rows, NY)],
        *sums, scratch=[(rows, NY)],
    )
    program.hold(pred, weight)
    got = exchange(after(message, pulled), XY)
    (pulled,) = call(bind(sum_kernel, nxy), [(rows, NY)], after(pulled, message))
    pulls = from_axis([pulled] * nh, "h")
    (power,) = call(bind(power_kernel, nxy * nh), [(KEPT, NY)], tops)
    program.hold(power)
    adjoint = lambda plane: call(
        bind(adjoint_kernel, nxy), [(QX + rows, NY)] * 4,
        plane.reshape(NX, NY), *factors, power, *tables,
        scratch=[(NX, NY), (4 * rows, NY)],
    )
    got = after(got, *pulls)
    pieces = from_comps(adjoint(got))
    message, grad, line, image = call(
        bind(gradient_kernel, nxy, nh),
        [(nxy, rows + 8, NY), (QX, NY), (rows, NY), (rows, NY)],
        *pieces, *pulls, dens, weight,
        scratch=[(rows, NY)],
    )
    program.drop(weight)
    program.hold(line, image)
    grads = from_comps([grad] * 4)
    got = after(exchange(message, XY), *grads)
    plane, shares = call(bind(part_kernel, nxy), [(NX, NY), (8, NY)], got)
    (shares,) = call(add_kernel, [(8, NY)], *from_axis([shares] * nh, "h"))
    shares = from_comps([shares] * 4)
    message, dens, base, alpha = call(
        second_kernel, [(nxy, rows, NY), (QX, NY), (QX, NY), (8, 128)],
        *shares, dens, full, *grads, *factors, *tables,
        scratch=[(NX, NY)],
    )
    program.alive = [weight_own, obs_own, pred, line, image, dens, base, alpha]
    got = exchange(message, XY)
    pieces = from_comps(adjoint(after(plane, message)))
    grad2, image2, half = call(
        second_gradient_kernel, [(QX, NY), (rows, NY), (8, 128)],
        *pieces, alpha, base, dens, line,
    )
    (parts,) = call(bind(sum_kernel, nxy), [(rows, NY)], after(got, *pieces))
    parts = after(from_axis([parts] * nh, "h"), half)
    program.alive = [obs_own, pred, image, dens, alpha, grad2]
    shares, image2 = call(
        bind(curvature_kernel, nh), [(devices, 128), (part, NY)], *parts, image2, weight_own, half
    )
    shares = exchange(shares, ALL)
    program.alive = []
    return tuple(
        call(
            finish_kernel, [density.shape, observed.shape],
            shares, dens, grad2, alpha, pred, image, image2, obs_own, weight_own,
        )
    )


def solution(mesh):
    depth = mesh.shape["depth"]
    sizes = {64: (4, 4, 4), 4: (2, 1, 2)}[depth]
    fine = Mesh(mesh.devices.reshape(*sizes, 2, 2), ALL)
    data = P(COMP, DEPTH, None)
    layer = P(DEPTH, COMP, None)
    return jax.shard_map(
        body,
        mesh=fine,
        in_specs=(layer, data, data, P(DEPTH)),
        out_specs=(layer, data),
        check_vma=False,
    )
```

```python
import functools
import math

import jax
import jax.numpy as jnp
import numpy as np
from jax import lax
from jax.experimental import pallas as pl
from jax.experimental.pallas import tpu as pltpu
from jax.sharding import Mesh
from jax.sharding import PartitionSpec as P

TWO_PI = 2.0 * math.pi
F32 = jnp.float32
BF16 = jnp.bfloat16
XY = ("x", "y")
DEPTH = ("x", "y", "h")
COMP = ("l", "k")
ALL = ("x", "y", "h", "l", "k")

NX = 512
NY = 256
HX = NX // 2
QX = NX // 4
HY = NY // 2


def split_table(table):
    high = table.astype(jnp.bfloat16)
    low = (table - high.astype(np.float64)).astype(jnp.bfloat16)
    return np.stack([high, low])


def basis(count, waves):
    place = np.arange(count)
    rows = []
    for wave in waves:
        norm = math.sqrt((1.0 if wave == 0 else 2.0) / count)
        rows.append(norm * np.cos(TWO_PI * (wave * place % count) / count))
    for wave in waves:
        if wave == 0:
            rows.append(math.sqrt(1.0 / count) * (1.0 - 2.0 * (place % 2)))
        else:
            rows.append(math.sqrt(2.0 / count) * np.sin(TWO_PI * (wave * place % count) / count))
    return np.stack(rows)


def make_tables():
    even = basis(NX, range(0, HX, 2))[:, :HX]
    odd = basis(NX, range(1, HX, 2))[:, :HX]
    col = basis(NY, range(HY))
    return (
        np.concatenate([split_table(even), split_table(odd)]),
        split_table(col.T),
    )


def split(value):
    high = value.astype(BF16)
    low = (value - high.astype(F32)).astype(BF16)
    return high, low


def dot(left, right):
    return jnp.dot(left, right, preferred_element_type=F32)


def dot_turned(left, right):
    return lax.dot_general(left, right, (((1,), (1,)), ((), ())), preferred_element_type=F32)


def times_table(value, high, low):
    vh, vl = split(value)
    return dot(vh, high) + (dot(vl, high) + dot(vh, low))


def times_turned(value, high, low):
    vh, vl = split(value)
    return dot_turned(vh, high) + (dot_turned(vl, high) + dot_turned(vh, low))


def table_times(high, low, value):
    vh, vl = split(value)
    return dot(high, vh) + (dot(high, vl) + dot(low, vh))


def to_waves(field, fx, ty):
    cols = times_table(field, ty[0], ty[1])
    upper, lower = cols[:HX], cols[HX:]
    return (
        table_times(fx[0], fx[1], upper + lower),
        table_times(fx[2], fx[3], upper - lower),
    )


def from_waves(even, odd, bx, ty):
    first = table_times(bx[0], bx[1], even)
    second = table_times(bx[2], bx[3], odd)
    rows = jnp.concatenate([first + second, first - second], axis=0)
    return times_turned(rows, ty[0], ty[1])


def swap_x(half):
    return jnp.concatenate([half[HX // 2 :], half[: HX // 2]], axis=0)


def swap_y(half):
    return jnp.concatenate([half[:, HY:], half[:, :HY]], axis=1)


def sines(cosines, nyquist):
    row = lax.broadcasted_iota(jnp.int32, cosines.shape, 0)
    return jnp.where(row == 0, nyquist, cosines)


def spread(ref):
    even, odd = ref[:QX], ref[QX:HX]
    return (
        jnp.concatenate([even, sines(even, ref[HX : HX + 1])], axis=0),
        jnp.concatenate([odd, odd], axis=0),
    )


def x_factors(gx_ref):
    even, odd = gx_ref[:QX], gx_ref[QX:HX]
    return jnp.concatenate([even, -even], axis=0), jnp.concatenate([odd, -odd], axis=0)


def xx_factors(gx_ref):
    even, odd = spread(gx_ref)
    return -(even * even), -(odd * odd)


def component(even, odd, gx_ref, gy_ref, comp):
    halves = []
    for half, first, second, third in zip(
        (even, odd), x_factors(gx_ref), spread(gy_ref), xx_factors(gx_ref)
    ):
        met = jnp.where(comp == 1, swap_x(half), jnp.where(comp == 2, swap_y(half), half))
        factor = jnp.where(comp == 1, first, jnp.where(comp == 2, second, third))
        halves.append(met * jnp.where(comp == 0, 1.0, factor))
    return halves


def comp_index():
    return lax.axis_index("l") * 2 + lax.axis_index("k")


KEPT = HX + 8


def wave_grid():
    row = lax.broadcasted_iota(jnp.int32, (KEPT, NY), 0)
    col = lax.broadcasted_iota(jnp.int32, (KEPT, NY), 1)
    wave_x = jnp.where(row >= HX, HX, 2 * (row % QX) + (row >= QX).astype(jnp.int32))
    nyquist_y = col == HY
    wave_y = jnp.where(nyquist_y, HY, col % HY)
    kx = wave_x.astype(F32) * (TWO_PI / NX)
    ky = wave_y.astype(F32) * (TWO_PI / NY)
    return kx, ky, col >= HY, nyquist_y


def prepare_kernel(
    top_ref, fx_in, ty_in, dens_in, weight_in, obs_in,
    fx, bx, ty, dens_ref, weight_ref, obs_ref, decay_ref, gx_ref, gy_ref,
):
    dens_ref[...] = dens_in[0]
    weight_ref[...] = weight_in[0]
    obs_ref[...] = obs_in[0]
    for place in range(4):
        table = fx_in[place]
        fx[place] = table
        bx[place] = table.astype(F32).T.astype(BF16)
    for place in range(2):
        ty[place] = ty_in[place]
    kx, ky, sine_y, nyquist_y = wave_grid()
    kabs = jnp.sqrt(kx * kx + ky * ky)
    inverse = 1.0 / jnp.maximum(kabs, TWO_PI / max(NX, NY))
    decay_ref[...] = 4.0 * jnp.exp(-kabs * top_ref[0]) * (1.0 - jnp.exp(-kabs))
    gx_ref[...] = kx * inverse
    ry = ky * inverse
    gy_ref[...] = jnp.where(nyquist_y, 0.0, jnp.where(sine_y, -ry, ry))


def gather_rows(pieces, full_ref):
    comp = comp_index()
    for step, piece in enumerate(pieces):
        full_ref[pl.ds(pl.multiple_of(jnp.bitwise_xor(comp, step) * QX, QX), QX), :] = piece[...]


def forward_plane(field, decay_ref, gx_ref, gy_ref, fx, bx, ty):
    even, odd = to_waves(field, fx, ty)
    decay = spread(decay_ref)
    even, odd = component(even * decay[0], odd * decay[1], gx_ref, gy_ref, comp_index())
    return from_waves(even, odd, bx, ty)


def start_kernel(
    nxy, m0, m1, m2, m3, top_ref, decay_ref, gx_ref, gy_ref, fx, bx, ty, out_ref, far_ref, full_ref, pull_ref, sem
):
    rows = NX // nxy
    gather_rows((m0, m1, m2, m3), full_ref)
    copy = pltpu.make_async_copy(full_ref, far_ref, sem)
    copy.start()
    dens = full_ref[...]
    pull_ref[...] = 0.5 * (dens * (1.0 / (dens * dens + 0.25)))
    for place, field in enumerate((full_ref, pull_ref)):
        plane = forward_plane(field[...], decay_ref, gx_ref, gy_ref, fx, bx, ty)
        for target in range(nxy):
            out_ref[target, place * rows : (place + 1) * rows, :] = plane[
                target * rows : (target + 1) * rows
            ]
    for target in range(nxy):
        out_ref[target, 2 * rows : 2 * rows + 8, :] = jnp.full((8, NY), top_ref[0], F32)
    copy.wait()


def collect_kernel(nxy, got_ref, weight_ref, obs_ref, sum_ref):
    rows = NX // nxy
    total = got_ref[0, : 2 * rows, :]
    for source in range(1, nxy):
        total = total + got_ref[source, : 2 * rows, :]
    sum_ref[: 2 * rows] = total
    left = lax.broadcasted_iota(jnp.int32, (1, NY), 1) < HY
    for pair in range(nxy // 2):
        first, second = (got_ref[2 * pair + i, 2 * rows : 2 * rows + 1, :] for i in (0, 1))
        sum_ref[2 * rows + pair : 2 * rows + pair + 1, :] = jnp.where(left, first, second)
    part = weight_ref.shape[0]
    start = 2 * rows + nxy // 2
    sum_ref[start : start + part] = weight_ref[...]
    sum_ref[start + part : start + 2 * part] = obs_ref[...]


def residual_kernel(nxy, nh, *refs):
    rows = NX // nxy
    part = rows // nh
    pairs = nxy // 2
    start = 2 * rows + pairs
    sums = refs[:nh]
    pred_ref, pull_ref, weight_ref, tops_ref, send_ref, meas_ref = refs[nh:]
    chip = lax.axis_index("h")
    total = sums[0][: 2 * rows]
    for step in range(1, nh):
        total = total + sums[step][: 2 * rows]
    for step in range(nh):
        tops_ref[step * pairs : (step + 1) * pairs] = sums[step][2 * rows : start]
        place = pl.ds(pl.multiple_of(lax.rem(chip + (nh - step), nh) * part, part), part)
        weight_ref[place, :] = sums[step][start : start + part]
        meas_ref[place, :] = sums[step][start + part :]
    weight = weight_ref[...]
    pred = total[:rows]
    pred_ref[...] = pred
    pull_ref[...] = total[rows:]
    res = weight * (weight * (pred - meas_ref[...]))
    for target in range(nxy):
        send_ref[target] = res


def power_kernel(layers, tops_ref, power_ref):
    kx, ky, *_ = wave_grid()
    for start in range(0, KEPT, 64):
        stop = min(start + 64, KEPT)
        ks = jnp.sqrt(kx[start:stop] ** 2 + ky[start:stop] ** 2)
        double = -2.0 * ks

        def add(step, total):
            for pair in range(2):
                tops = tops_ref[pl.ds(2 * step + pair, 1), :]
                for top in (tops[:, :HY], tops[:, HY:]):
                    total = total + jnp.exp(double * jnp.concatenate([top, top], axis=1))
            return total

        total = lax.fori_loop(0, layers // 4, add, jnp.zeros_like(ks))
        rise = 1.0 - jnp.exp(-ks)
        power_ref[start:stop] = (16.0 * (rise * rise)) * total


def adjoint_kernel(
    nxy, res_ref, decay_ref, gx_ref, gy_ref, power_ref, fx, bx, ty, o0, o1, o2, o3, z_ref, i_ref
):
    rows = NX // nxy
    comp = comp_index()
    even, odd = to_waves(res_ref[...], fx, ty)
    even, odd = component(even, odd, gx_ref, gy_ref, comp)
    sign = jnp.where((comp == 1) | (comp == 2), -1.0, 1.0)
    even = even * sign
    odd = odd * sign
    decay = spread(decay_ref)
    z_ref[...] = from_waves(even * decay[0], odd * decay[1], bx, ty)
    power = spread(power_ref)
    even = even * power[0]
    odd = odd * power[1]
    block = lax.axis_index("x") * lax.axis_size("y") + lax.axis_index("y")
    upper = block * rows < HX
    near = pl.ds(pl.multiple_of(lax.rem(block * rows, HX), rows), rows)
    flip = jnp.where(upper, 1.0, -1.0)
    for target in range(4):
        if target == 0:
            e, o = even, odd
        elif target == 1:
            first = x_factors(gx_ref)
            e, o = swap_x(even) * first[0], swap_x(odd) * first[1]
        elif target == 2:
            second = spread(gy_ref)
            e, o = swap_y(even) * second[0], swap_y(odd) * second[1]
        else:
            third = xx_factors(gx_ref)
            e, o = even * third[0], odd * third[1]
        line = table_times(bx[0, near, :], bx[1, near, :], e)
        line = line + flip * table_times(bx[2, near, :], bx[3, near, :], o)
        i_ref[target * rows : (target + 1) * rows, :] = line
    i_ref[...] = times_turned(i_ref[...], ty[0], ty[1])
    for step, out in enumerate((o0, o1, o2, o3)):
        other = jnp.bitwise_xor(comp, step)
        out[:QX] = z_ref[pl.ds(pl.multiple_of(other * QX, QX), QX), :]
        out[QX:] = i_ref[pl.ds(pl.multiple_of(other * rows, rows), rows), :]


def share(grad, quad, image, weight, scratch, part):
    scratch[...] = weight * image
    place = pl.ds(pl.multiple_of(lax.axis_index("h") * part, part), part)
    mine = scratch[place, :]
    lane = lax.broadcasted_iota(jnp.int32, (1, NY), 1)
    square = grad * grad
    gg = jnp.sum(square)
    qgg = jnp.sum(quad * square)
    curv = jnp.sum(mine * mine)
    return jnp.where(lane == 0, gg, jnp.where(lane == 1, qgg, jnp.where(lane == 2, curv, 0.0)))


def step_length(shares):
    total = jnp.sum(shares, axis=0, keepdims=True)
    lane = lax.broadcasted_iota(jnp.int32, total.shape, 1)
    pick = lambda place: jnp.sum(jnp.where(lane == place, total, 0.0), keepdims=True)
    return pick(0) / (pick(2) + 0.5 * pick(1))


def gradient_kernel(nxy, nh, *refs):
    rows = NX // nxy
    part = rows // nh
    pieces = refs[:4]
    pull_ref, dens_ref, weight_ref = refs[4:7]
    send_ref, grad_ref, line_ref, image_ref, scratch = refs[7:]
    total = pieces[0][...] + pieces[1][...] + (pieces[2][...] + pieces[3][...])
    data = total[:QX]
    line = total[QX:]
    dens = dens_ref[...]
    quad = 1.0 / (dens * dens + 0.25)
    grad = data + 0.5 * (quad * dens)
    image = line + pull_ref[...]
    weight = weight_ref[...]
    mine = jnp.broadcast_to(share(grad, quad, image, weight, scratch, part), (8, NY))
    grad_ref[...] = grad
    line_ref[...] = line
    image_ref[...] = image
    back = weight * (weight * image)
    for target in range(nxy):
        send_ref[target, :rows] = back
        send_ref[target, rows:] = mine


def part_kernel(nxy, got_ref, plane_ref, share_ref):
    rows = NX // nxy
    total = got_ref[0, rows:, :]
    for source in range(1, nxy):
        total = total + got_ref[source, rows:, :]
    share_ref[...] = total
    for source in range(nxy):
        plane_ref[source * rows : (source + 1) * rows] = got_ref[source, :rows, :]


def add_kernel(*refs):
    total = refs[0][...]
    for part in refs[1:-1]:
        total = total + part[...]
    refs[-1][...] = total


def second_kernel(
    s0, s1, s2, s3, dens_ref, full_ref, g0, g1, g2, g3, decay_ref, gx_ref, gy_ref, fx, bx, ty,
    out_ref, dens_out, base_out, alpha_ref, all_ref,
):
    gather_rows((g0, g1, g2, g3), all_ref)
    alpha = step_length(s0[:1] + s1[:1] + (s2[:1] + s3[:1]))
    alpha_ref[...] = jnp.broadcast_to(alpha, alpha_ref.shape)
    old = dens_ref[...]
    grad = g0[...]
    dens = old - alpha * grad
    dens_out[...] = dens
    data = grad - 0.5 * ((1.0 / (old * old + 0.25)) * old)
    base_out[...] = data + 0.5 * (dens * (1.0 / (dens * dens + 0.25)))
    dens = full_ref[...] - alpha * all_ref[...]
    all_ref[...] = 0.5 * (dens * (1.0 / (dens * dens + 0.25)))
    plane = forward_plane(all_ref[...], decay_ref, gx_ref, gy_ref, fx, bx, ty)
    out_ref[...] = plane.reshape(out_ref.shape)


def sum_kernel(nxy, got_ref, half_ref, sum_ref):
    rows = NX // nxy
    total = got_ref[0]
    for source in range(1, nxy):
        total = total + got_ref[source]
    sum_ref[:rows] = total
    sum_ref[rows:] = half_ref[...]


def second_gradient_kernel(
    u0, u1, u2, u3, alpha_ref, base_ref, dens_ref, line_ref, grad_ref, image_ref, share_ref
):
    alpha = alpha_ref[:1, :1]
    total = u0[...] + u1[...] + (u2[...] + u3[...])
    dens = dens_ref[...]
    grad = base_ref[...] - alpha * total[:QX]
    quad = 1.0 / (dens * dens + 0.25)
    grad_ref[...] = grad
    image_ref[...] = line_ref[...] - alpha * total[QX:]
    square = grad * grad
    lane = lax.broadcasted_iota(jnp.int32, (8, NY), 1)
    share_ref[...] = jnp.where(
        lane == 0, jnp.sum(square), jnp.where(lane == 1, jnp.sum(quad * square), 0.0)
    )


def curvature_kernel(nh, part, *refs):
    parts = refs[:nh]
    image_ref, weight_ref, share_ref, out_ref, scratch = refs[nh:]
    rows = image_ref.shape[0]
    total = parts[0][...]
    for piece in parts[1:]:
        total = total + piece[...]
    image = image_ref[...] + total[:rows]
    scratch[...] = image
    out_ref[...] = scratch[pl.ds(pl.multiple_of(lax.axis_index("h") * part, part), part), :]
    mine = weight_ref[...] * image
    lane = lax.broadcasted_iota(jnp.int32, (1, 128), 1)
    share_ref[...] = jnp.broadcast_to(
        jnp.where(lane == 2, jnp.sum(mine * mine), total[rows : rows + 1, :128]), share_ref.shape
    )


def finish_kernel(
    shares_ref, dens_ref, grad_ref, alpha_ref, pred_ref, first_ref, second_ref, obs_ref, w_ref, dens_out, err_out
):
    part = obs_ref.shape[0]
    alpha = step_length(shares_ref[...])
    dens_out[0] = dens_ref[...] - alpha * grad_ref[...]
    place = pl.ds(pl.multiple_of(lax.axis_index("h") * part, part), part)
    pred = pred_ref[place, :] - alpha_ref[:1, :1] * first_ref[place, :]
    pred = pred - alpha * second_ref[...]
    err_out[0] = w_ref[...] * (pred - obs_ref[...])


VMEM = pl.BlockSpec(memory_space=pltpu.VMEM)
SMEM = pl.BlockSpec(memory_space=pltpu.SMEM)
ANY = pl.BlockSpec(memory_space=pl.ANY)


class Program:
    def __init__(self):
        self.alive = []

    def hold(self, *values):
        self.alive += values

    def drop(self, *values):
        self.alive = [item for item in self.alive if all(item is not value for value in values)]

    def call(self, kernel, outs, *args, scratch=(), scalars=(), far_out=(), sems=0, mib=8):
        used = len(args)
        keep = [item for item in self.alive if all(item is not value for value in args)]
        kept = len(keep)

        def inner(*refs):
            kernel(*refs[:used], *refs[used + kept :])

        kinds = [(item, F32) if isinstance(item, tuple) else (item.shape, item.dtype) for item in outs]
        return pl.pallas_call(
            inner,
            out_shape=[jax.ShapeDtypeStruct(shape, dtype) for shape, dtype in kinds],
            in_specs=[
                SMEM if place in scalars else VMEM for place in range(used)
            ]
            + [ANY] * kept,
            out_specs=[ANY if place in far_out else VMEM for place in range(len(outs))],
            scratch_shapes=[pltpu.VMEM(shape, F32) for shape in scratch]
            + [pltpu.SemaphoreType.DMA((sems,) if sems > 1 else ())] * (sems > 0),
            compiler_params=pltpu.CompilerParams(vmem_limit_bytes=mib << 20),
        )(*args, *keep)


def from_comps(values):
    return [values[0]] + [
        lax.ppermute(values[step], COMP, [(i, i ^ step) for i in range(4)]) for step in (1, 2, 3)
    ]


def from_axis(values, axis):
    size = len(values)
    return [values[0]] + [
        lax.ppermute(values[step], axis, [(i, (i + step) % size) for i in range(size)])
        for step in range(1, size)
    ]


def exchange(value, axes):
    return lax.all_to_all(value, axes, 0, 0, tiled=True)


def after(values, *others):
    if isinstance(values, (list, tuple)):
        return list(lax.optimization_barrier((tuple(values), others))[0])
    return lax.optimization_barrier((values, others))[0]


def body(density, observed, data_weight, layer_top):
    nx, ny, nh = (lax.axis_size(axis) for axis in DEPTH)
    nxy = nx * ny
    rows = NX // nxy
    part = rows // nh
    fx, ty = (jnp.asarray(table) for table in make_tables())
    bind = functools.partial
    program = Program()
    call = program.call

    layers = from_comps([density[0]] * 4)
    *tables, dens, weight_own, obs_own, decay, gx, gy = call(
        prepare_kernel,
        [
            fx, fx, ty, (QX, NY), (part, NY), (part, NY), (KEPT, NY), (KEPT, NY), (KEPT, NY),
        ],
        layer_top, fx, ty, density, data_weight, observed, scalars=(0,),
    )
    factors = (decay, gx, gy)
    program.hold(*tables, *factors, dens, weight_own, obs_own)
    message, full = call(
        bind(start_kernel, nxy), [(nxy, 2 * rows + 8, NY), (NX, NY)],
        dens, *layers[1:], layer_top, *factors, *tables,
        scratch=[(NX, NY)] * 2, scalars=(4,), far_out=(1,), sems=1,
    )
    got = exchange(message, XY)
    (sums,) = call(
        bind(collect_kernel, nxy), [(2 * rows + nxy // 2 + 2 * part, NY)], got, weight_own, obs_own
    )
    sums = from_axis([sums] * nh, "h")
    pred, pulled, weight, tops, message = call(
        bind(residual_kernel, nxy, nh),
        [(rows, NY), (rows, NY), (rows, NY), (nxy * nh // 2, NY), (nxy, rows, NY)],
        *sums, scratch=[(rows, NY)],
    )
    program.hold(pred, pulled, weight)
    got = exchange(message, XY)
    (power,) = call(bind(power_kernel, nxy * nh), [(KEPT, NY)], tops)
    program.hold(power)
    adjoint = lambda plane: call(
        bind(adjoint_kernel, nxy), [(QX + rows, NY)] * 4,
        plane.reshape(NX, NY), *factors, power, *tables,
        scratch=[(NX, NY), (4 * rows, NY)],
    )
    pieces = from_comps(adjoint(got))
    message, grad, line, image = call(
        bind(gradient_kernel, nxy, nh),
        [(nxy, rows + 8, NY), (QX, NY), (rows, NY), (rows, NY)],
        *pieces, pulled, dens, weight, scratch=[(rows, NY)],
    )
    program.drop(pulled)
    program.hold(line, image)
    grads = from_comps([grad] * 4)
    got = after(exchange(message, XY), *grads)
    plane, shares = call(bind(part_kernel, nxy), [(NX, NY), (8, NY)], got)
    pieces = adjoint(plane)
    shares = after(from_axis([shares] * nh, "h"), *pieces)
    (shares,) = call(add_kernel, [(8, NY)], *shares)
    shares = from_comps([shares] * 4)
    message, dens, base, alpha = call(
        second_kernel, [(nxy, rows, NY), (QX, NY), (QX, NY), (8, 128)],
        *shares, dens, full, *grads, *factors, *tables, scratch=[(NX, NY)],
    )
    program.alive = [weight_own, obs_own, weight, pred, line, image, dens, base, alpha]
    got = exchange(message, XY)
    pieces = from_comps(after(pieces, message))
    grad2, image2, half = call(
        second_gradient_kernel, [(QX, NY), (rows, NY), (8, NY)],
        *pieces, alpha, base, dens, line,
    )
    (parts,) = call(bind(sum_kernel, nxy), [(rows + 8, NY)], got, half)
    program.alive = [weight_own, obs_own, pred, image, dens, alpha, grad2]
    shares, image2 = call(
        bind(curvature_kernel, nh, part), [(nxy * 4, 128), (part, NY)],
        *from_axis([parts] * nh, "h"), image2, weight, scratch=[(rows, NY)],
    )
    shares = exchange(shares, (*XY, *COMP))
    program.alive = []
    return tuple(
        call(
            finish_kernel, [density.shape, observed.shape],
            shares, dens, grad2, alpha, pred, image, image2, obs_own, weight_own,
        )
    )


def solution(mesh):
    depth = mesh.shape["depth"]
    sizes = {64: (4, 4, 4), 4: (2, 1, 2)}[depth]
    fine = Mesh(mesh.devices.reshape(*sizes, 2, 2), ALL)
    data = P(COMP, DEPTH, None)
    layer = P(DEPTH, COMP, None)
    return jax.shard_map(
        body,
        mesh=fine,
        in_specs=(layer, data, data, P(DEPTH)),
        out_specs=(layer, data),
        check_vma=False,
    )
```

```python
import functools
import math

import jax
import jax.numpy as jnp
import numpy as np
from jax import lax
from jax.experimental import pallas as pl
from jax.experimental.pallas import tpu as pltpu
from jax.sharding import Mesh
from jax.sharding import PartitionSpec as P

TWO_PI = 2.0 * math.pi
F32 = jnp.float32
BF16 = jnp.bfloat16
XY = ("x", "y")
DEPTH = ("x", "y", "h")
COMP = ("l", "k")
ALL = ("x", "y", "h", "l", "k")

NX = 512
NY = 256
HX = NX // 2
QX = NX // 4
HY = NY // 2


def split_table(table):
    high = table.astype(jnp.bfloat16)
    low = (table - high.astype(np.float64)).astype(jnp.bfloat16)
    return np.stack([high, low])


def basis(count, waves):
    place = np.arange(count)
    rows = []
    for wave in waves:
        norm = math.sqrt((1.0 if wave == 0 else 2.0) / count)
        rows.append(norm * np.cos(TWO_PI * (wave * place % count) / count))
    for wave in waves:
        if wave == 0:
            rows.append(math.sqrt(1.0 / count) * (1.0 - 2.0 * (place % 2)))
        else:
            rows.append(math.sqrt(2.0 / count) * np.sin(TWO_PI * (wave * place % count) / count))
    return np.stack(rows)


def make_tables():
    even = basis(NX, range(0, HX, 2))[:, :HX]
    odd = basis(NX, range(1, HX, 2))[:, :HX]
    col = basis(NY, range(HY))
    return (
        np.concatenate([split_table(even), split_table(odd)]),
        split_table(col.T),
    )


def split(value):
    high = value.astype(BF16)
    low = (value - high.astype(F32)).astype(BF16)
    return high, low


def dot(left, right):
    return jnp.dot(left, right, preferred_element_type=F32)


def dot_turned(left, right):
    return lax.dot_general(left, right, (((1,), (1,)), ((), ())), preferred_element_type=F32)


def times_table(value, high, low):
    vh, vl = split(value)
    return dot(vh, high) + (dot(vl, high) + dot(vh, low))


def times_turned(value, high, low):
    vh, vl = split(value)
    return dot_turned(vh, high) + (dot_turned(vl, high) + dot_turned(vh, low))


def table_times(high, low, value):
    vh, vl = split(value)
    return dot(high, vh) + (dot(high, vl) + dot(low, vh))


def to_waves(field, fx, ty):
    cols = times_table(field, ty[0], ty[1])
    upper, lower = cols[:HX], cols[HX:]
    return (
        table_times(fx[0], fx[1], upper + lower),
        table_times(fx[2], fx[3], upper - lower),
    )


def from_waves(even, odd, bx, ty):
    first = table_times(bx[0], bx[1], even)
    second = table_times(bx[2], bx[3], odd)
    rows = jnp.concatenate([first + second, first - second], axis=0)
    return times_turned(rows, ty[0], ty[1])


def swap_x(half):
    return jnp.concatenate([half[HX // 2 :], half[: HX // 2]], axis=0)


def swap_y(half):
    return jnp.concatenate([half[:, HY:], half[:, :HY]], axis=1)


def sines(cosines, nyquist):
    row = lax.broadcasted_iota(jnp.int32, cosines.shape, 0)
    return jnp.where(row == 0, nyquist, cosines)


def spread(ref):
    even, odd = ref[:QX], ref[QX:HX]
    return (
        jnp.concatenate([even, sines(even, ref[HX : HX + 1])], axis=0),
        jnp.concatenate([odd, odd], axis=0),
    )


def x_factors(gx_ref):
    even, odd = gx_ref[:QX], gx_ref[QX:HX]
    return jnp.concatenate([even, -even], axis=0), jnp.concatenate([odd, -odd], axis=0)


def xx_factors(gx_ref):
    even, odd = spread(gx_ref)
    return -(even * even), -(odd * odd)


def component(even, odd, gx_ref, gy_ref, comp):
    halves = []
    for half, first, second, third in zip(
        (even, odd), x_factors(gx_ref), spread(gy_ref), xx_factors(gx_ref)
    ):
        met = jnp.where(comp == 1, swap_x(half), jnp.where(comp == 2, swap_y(half), half))
        factor = jnp.where(comp == 1, first, jnp.where(comp == 2, second, third))
        halves.append(met * jnp.where(comp == 0, 1.0, factor))
    return halves


def comp_index():
    return lax.axis_index("l") * 2 + lax.axis_index("k")


KEPT = HX + 8


def wave_grid():
    row = lax.broadcasted_iota(jnp.int32, (KEPT, NY), 0)
    col = lax.broadcasted_iota(jnp.int32, (KEPT, NY), 1)
    wave_x = jnp.where(row >= HX, HX, 2 * (row % QX) + (row >= QX).astype(jnp.int32))
    nyquist_y = col == HY
    wave_y = jnp.where(nyquist_y, HY, col % HY)
    kx = wave_x.astype(F32) * (TWO_PI / NX)
    ky = wave_y.astype(F32) * (TWO_PI / NY)
    return kx, ky, col >= HY, nyquist_y


def prepare_kernel(
    top_ref, fx_in, ty_in, dens_in, fx, bx, ty, dens_ref, decay_ref, gx_ref, gy_ref
):
    dens_ref[...] = dens_in[0]
    for place in range(4):
        table = fx_in[place]
        fx[place] = table
        bx[place] = table.astype(F32).T.astype(BF16)
    for place in range(2):
        ty[place] = ty_in[place]
    kx, ky, sine_y, nyquist_y = wave_grid()
    kabs = jnp.sqrt(kx * kx + ky * ky)
    inverse = 1.0 / jnp.maximum(kabs, TWO_PI / max(NX, NY))
    decay_ref[...] = 4.0 * jnp.exp(-kabs * top_ref[0]) * (1.0 - jnp.exp(-kabs))
    gx_ref[...] = kx * inverse
    ry = ky * inverse
    gy_ref[...] = jnp.where(nyquist_y, 0.0, jnp.where(sine_y, -ry, ry))


def gather_rows(pieces, full_ref):
    comp = comp_index()
    for step, piece in enumerate(pieces):
        full_ref[pl.ds(pl.multiple_of(jnp.bitwise_xor(comp, step) * QX, QX), QX), :] = piece[...]


def forward_plane(field, decay_ref, gx_ref, gy_ref, fx, bx, ty):
    even, odd = to_waves(field, fx, ty)
    decay = spread(decay_ref)
    even, odd = component(even * decay[0], odd * decay[1], gx_ref, gy_ref, comp_index())
    return from_waves(even, odd, bx, ty)


def start_kernel(
    nxy, m0, m1, m2, m3, top_ref, decay_ref, gx_ref, gy_ref, fx, bx, ty, out_ref, far_ref, full_ref, pull_ref, sem
):
    rows = NX // nxy
    gather_rows((m0, m1, m2, m3), full_ref)
    copy = pltpu.make_async_copy(full_ref, far_ref, sem)
    copy.start()
    dens = full_ref[...]
    pull_ref[...] = 0.5 * (dens * (1.0 / (dens * dens + 0.25)))
    for place, field in enumerate((full_ref, pull_ref)):
        plane = forward_plane(field[...], decay_ref, gx_ref, gy_ref, fx, bx, ty)
        for target in range(nxy):
            out_ref[target, place * rows : (place + 1) * rows, :] = plane[
                target * rows : (target + 1) * rows
            ]
    for target in range(nxy):
        out_ref[target, 2 * rows : 2 * rows + 8, :] = jnp.full((8, NY), top_ref[0], F32)
    copy.wait()


def collect_kernel(nxy, got_ref, weight_ref, obs_ref, sum_ref):
    rows = NX // nxy
    total = got_ref[0, : 2 * rows, :]
    for source in range(1, nxy):
        total = total + got_ref[source, : 2 * rows, :]
    sum_ref[: 2 * rows] = total
    left = lax.broadcasted_iota(jnp.int32, (1, NY), 1) < HY
    for pair in range(nxy // 2):
        first, second = (got_ref[2 * pair + i, 2 * rows : 2 * rows + 1, :] for i in (0, 1))
        sum_ref[2 * rows + pair : 2 * rows + pair + 1, :] = jnp.where(left, first, second)
    part = weight_ref.shape[0]
    start = 2 * rows + nxy // 2
    sum_ref[start : start + part] = weight_ref[...]
    sum_ref[start + part : start + 2 * part] = obs_ref[...]


def residual_kernel(nxy, nh, *refs):
    rows = NX // nxy
    part = rows // nh
    pairs = nxy // 2
    start = 2 * rows + pairs
    sums = refs[:nh]
    pred_ref, pull_ref, weight_ref, tops_ref, send_ref, meas_ref = refs[nh:]
    chip = lax.axis_index("h")
    total = sums[0][: 2 * rows]
    for step in range(1, nh):
        total = total + sums[step][: 2 * rows]
    for step in range(nh):
        tops_ref[step * pairs : (step + 1) * pairs] = sums[step][2 * rows : start]
        place = pl.ds(pl.multiple_of(lax.rem(chip + (nh - step), nh) * part, part), part)
        weight_ref[place, :] = sums[step][start : start + part]
        meas_ref[place, :] = sums[step][start + part :]
    weight = weight_ref[...]
    pred = total[:rows]
    pred_ref[...] = pred
    pull_ref[...] = total[rows:]
    res = weight * (weight * (pred - meas_ref[...]))
    for target in range(nxy):
        send_ref[target] = res


def power_kernel(layers, tops_ref, power_ref):
    kx, ky, *_ = wave_grid()
    for start in range(0, KEPT, 64):
        stop = min(start + 64, KEPT)
        ks = jnp.sqrt(kx[start:stop] ** 2 + ky[start:stop] ** 2)
        double = -2.0 * ks

        def add(step, total):
            for pair in range(2):
                tops = tops_ref[pl.ds(2 * step + pair, 1), :]
                for top in (tops[:, :HY], tops[:, HY:]):
                    total = total + jnp.exp(double * jnp.concatenate([top, top], axis=1))
            return total

        total = lax.fori_loop(0, layers // 4, add, jnp.zeros_like(ks))
        rise = 1.0 - jnp.exp(-ks)
        power_ref[start:stop] = (16.0 * (rise * rise)) * total


def adjoint_kernel(
    nxy, res_ref, decay_ref, gx_ref, gy_ref, power_ref, fx, bx, ty, own_out, other_out, z_ref, i_ref
):
    rows = NX // nxy
    comp = comp_index()
    even, odd = to_waves(res_ref[...], fx, ty)
    even, odd = component(even, odd, gx_ref, gy_ref, comp)
    sign = jnp.where((comp == 1) | (comp == 2), -1.0, 1.0)
    even = even * sign
    odd = odd * sign
    decay = spread(decay_ref)
    z_ref[...] = from_waves(even * decay[0], odd * decay[1], bx, ty)
    power = spread(power_ref)
    even = even * power[0]
    odd = odd * power[1]
    block = lax.axis_index("x") * lax.axis_size("y") + lax.axis_index("y")
    upper = block * rows < HX
    near = pl.ds(pl.multiple_of(lax.rem(block * rows, HX), rows), rows)
    flip = jnp.where(upper, 1.0, -1.0)
    for target in range(4):
        if target == 0:
            e, o = even, odd
        elif target == 1:
            first = x_factors(gx_ref)
            e, o = swap_x(even) * first[0], swap_x(odd) * first[1]
        elif target == 2:
            second = spread(gy_ref)
            e, o = swap_y(even) * second[0], swap_y(odd) * second[1]
        else:
            third = xx_factors(gx_ref)
            e, o = even * third[0], odd * third[1]
        line = table_times(bx[0, near, :], bx[1, near, :], e)
        line = line + flip * table_times(bx[2, near, :], bx[3, near, :], o)
        i_ref[target * rows : (target + 1) * rows, :] = line
    i_ref[...] = times_turned(i_ref[...], ty[0], ty[1])
    for step in range(4):
        out = (own_out, other_out)[step % 2]
        begin = (step // 2) * (QX + rows)
        other = jnp.bitwise_xor(comp, step)
        out[begin : begin + QX] = z_ref[pl.ds(pl.multiple_of(other * QX, QX), QX), :]
        out[begin + QX : begin + QX + rows] = i_ref[
            pl.ds(pl.multiple_of(other * rows, rows), rows), :
        ]


def pair_kernel(own_ref, got_ref, near_ref, far_ref):
    half = near_ref.shape[0]
    near_ref[...] = own_ref[:half] + got_ref[:half]
    far_ref[...] = own_ref[half:] + got_ref[half:]


def share(grad, quad, image, weight, scratch, part):
    scratch[...] = weight * image
    place = pl.ds(pl.multiple_of(lax.axis_index("h") * part, part), part)
    mine = scratch[place, :]
    lane = lax.broadcasted_iota(jnp.int32, (1, NY), 1)
    square = grad * grad
    gg = jnp.sum(square)
    qgg = jnp.sum(quad * square)
    curv = jnp.sum(mine * mine)
    return jnp.where(lane == 0, gg, jnp.where(lane == 1, qgg, jnp.where(lane == 2, curv, 0.0)))


def step_length(shares):
    total = jnp.sum(shares, axis=0, keepdims=True)
    lane = lax.broadcasted_iota(jnp.int32, total.shape, 1)
    pick = lambda place: jnp.sum(jnp.where(lane == place, total, 0.0), keepdims=True)
    return pick(0) / (pick(2) + 0.5 * pick(1))


def gradient_kernel(nxy, nh, *refs):
    rows = NX // nxy
    part = rows // nh
    pieces = refs[:2]
    pull_ref, dens_ref, weight_ref = refs[2:5]
    send_ref, grad_ref, line_ref, image_ref, scratch = refs[5:]
    total = pieces[0][...] + pieces[1][...]
    data = total[:QX]
    line = total[QX:]
    dens = dens_ref[...]
    quad = 1.0 / (dens * dens + 0.25)
    grad = data + 0.5 * (quad * dens)
    image = line + pull_ref[...]
    weight = weight_ref[...]
    mine = jnp.broadcast_to(share(grad, quad, image, weight, scratch, part), (8, NY))
    grad_ref[...] = grad
    line_ref[...] = line
    image_ref[...] = image
    back = weight * (weight * image)
    for target in range(nxy):
        send_ref[target, :rows] = back
        send_ref[target, rows:] = mine


def part_kernel(nxy, got_ref, plane_ref, share_ref):
    rows = NX // nxy
    total = got_ref[0, rows:, :]
    for source in range(1, nxy):
        total = total + got_ref[source, rows:, :]
    share_ref[...] = total
    for source in range(nxy):
        plane_ref[source * rows : (source + 1) * rows] = got_ref[source, :rows, :]


def add_kernel(*refs):
    total = refs[0][...]
    for part in refs[1:-1]:
        total = total + part[...]
    refs[-1][...] = total


def second_kernel(
    s0, s1, s2, s3, dens_ref, full_ref, g0, g1, g2, g3, decay_ref, gx_ref, gy_ref, fx, bx, ty,
    out_ref, dens_out, base_out, alpha_ref, all_ref,
):
    gather_rows((g0, g1, g2, g3), all_ref)
    alpha = step_length(s0[:1] + s1[:1] + (s2[:1] + s3[:1]))
    alpha_ref[...] = jnp.broadcast_to(alpha, alpha_ref.shape)
    old = dens_ref[...]
    grad = g0[...]
    dens = old - alpha * grad
    dens_out[...] = dens
    data = grad - 0.5 * ((1.0 / (old * old + 0.25)) * old)
    base_out[...] = data + 0.5 * (dens * (1.0 / (dens * dens + 0.25)))
    dens = full_ref[...] - alpha * all_ref[...]
    all_ref[...] = 0.5 * (dens * (1.0 / (dens * dens + 0.25)))
    plane = forward_plane(all_ref[...], decay_ref, gx_ref, gy_ref, fx, bx, ty)
    out_ref[...] = plane.reshape(out_ref.shape)


def sum_kernel(nxy, got_ref, half_ref, sum_ref):
    rows = NX // nxy
    total = got_ref[0]
    for source in range(1, nxy):
        total = total + got_ref[source]
    sum_ref[:rows] = total
    sum_ref[rows:] = half_ref[...]


def second_gradient_kernel(
    u0, u1, alpha_ref, base_ref, dens_ref, line_ref, grad_ref, image_ref, share_ref
):
    alpha = alpha_ref[:1, :1]
    total = u0[...] + u1[...]
    dens = dens_ref[...]
    grad = base_ref[...] - alpha * total[:QX]
    quad = 1.0 / (dens * dens + 0.25)
    grad_ref[...] = grad
    image_ref[...] = line_ref[...] - alpha * total[QX:]
    square = grad * grad
    lane = lax.broadcasted_iota(jnp.int32, (8, NY), 1)
    share_ref[...] = jnp.where(
        lane == 0, jnp.sum(square), jnp.where(lane == 1, jnp.sum(quad * square), 0.0)
    )


def curvature_kernel(nh, part, *refs):
    parts = refs[:nh]
    image_ref, weight_ref, share_ref, out_ref, scratch = refs[nh:]
    rows = image_ref.shape[0]
    total = parts[0][...]
    for piece in parts[1:]:
        total = total + piece[...]
    image = image_ref[...] + total[:rows]
    scratch[...] = image
    out_ref[...] = scratch[pl.ds(pl.multiple_of(lax.axis_index("h") * part, part), part), :]
    mine = weight_ref[...] * image
    lane = lax.broadcasted_iota(jnp.int32, (1, 128), 1)
    share_ref[...] = jnp.broadcast_to(
        jnp.where(lane == 2, jnp.sum(mine * mine), total[rows : rows + 1, :128]), share_ref.shape
    )


def finish_kernel(
    shares_ref, dens_ref, grad_ref, alpha_ref, pred_ref, first_ref, second_ref, obs_ref, w_ref, dens_out, err_out
):
    part = obs_ref.shape[0]
    alpha = step_length(shares_ref[...])
    dens_out[0] = dens_ref[...] - alpha * grad_ref[...]
    place = pl.ds(pl.multiple_of(lax.axis_index("h") * part, part), part)
    pred = pred_ref[place, :] - alpha_ref[:1, :1] * first_ref[place, :]
    pred = pred - alpha * second_ref[...]
    err_out[0] = w_ref[...] * (pred - obs_ref[...])


VMEM = pl.BlockSpec(memory_space=pltpu.VMEM)
SMEM = pl.BlockSpec(memory_space=pltpu.SMEM)
ANY = pl.BlockSpec(memory_space=pl.ANY)


class Program:
    def __init__(self):
        self.alive = []

    def hold(self, *values):
        self.alive += values

    def drop(self, *values):
        self.alive = [item for item in self.alive if all(item is not value for value in values)]

    def call(self, kernel, outs, *args, scratch=(), scalars=(), far_out=(), sems=0, mib=8):
        used = len(args)
        keep = [item for item in self.alive if all(item is not value for value in args)]
        kept = len(keep)

        def inner(*refs):
            kernel(*refs[:used], *refs[used + kept :])

        kinds = [(item, F32) if isinstance(item, tuple) else (item.shape, item.dtype) for item in outs]
        return pl.pallas_call(
            inner,
            out_shape=[jax.ShapeDtypeStruct(shape, dtype) for shape, dtype in kinds],
            in_specs=[
                SMEM if place in scalars else VMEM for place in range(used)
            ]
            + [ANY] * kept,
            out_specs=[ANY if place in far_out else VMEM for place in range(len(outs))],
            scratch_shapes=[pltpu.VMEM(shape, F32) for shape in scratch]
            + [pltpu.SemaphoreType.DMA((sems,) if sems > 1 else ())] * (sems > 0),
            compiler_params=pltpu.CompilerParams(vmem_limit_bytes=mib << 20),
        )(*args, *keep)


def from_comps(values):
    return [values[0]] + [
        lax.ppermute(values[step], COMP, [(i, i ^ step) for i in range(4)]) for step in (1, 2, 3)
    ]


def flip(value, axis):
    return lax.ppermute(value, axis, [(0, 1), (1, 0)])


def gather_comps(value):
    across = flip(value, "l")
    return [value, flip(value, "k"), across, flip(across, "k")]


def from_axis(values, axis):
    size = len(values)
    return [values[0]] + [
        lax.ppermute(values[step], axis, [(i, (i + step) % size) for i in range(size)])
        for step in range(1, size)
    ]


def exchange(value, axes):
    return lax.all_to_all(value, axes, 0, 0, tiled=True)


def after(values, *others):
    if isinstance(values, (list, tuple)):
        return list(lax.optimization_barrier((tuple(values), others))[0])
    return lax.optimization_barrier((values, others))[0]


def body(density, observed, data_weight, layer_top):
    nx, ny, nh = (lax.axis_size(axis) for axis in DEPTH)
    nxy = nx * ny
    rows = NX // nxy
    part = rows // nh
    fx, ty = (jnp.asarray(table) for table in make_tables())
    bind = functools.partial
    program = Program()
    call = program.call

    near, across = flip(density[0], "k"), flip(density[0], "l")
    *tables, dens, decay, gx, gy = call(
        prepare_kernel,
        [fx, fx, ty, (QX, NY), (KEPT, NY), (KEPT, NY), (KEPT, NY)],
        layer_top, fx, ty, density, scalars=(0,),
    )
    layers = [near, across, flip(after(across, dens), "k")]
    factors = (decay, gx, gy)
    weight_own, obs_own = data_weight[0], observed[0]
    program.hold(*tables, *factors, dens)
    message, full = call(
        bind(start_kernel, nxy), [(nxy, 2 * rows + 8, NY), (NX, NY)],
        dens, *layers, layer_top, *factors, *tables,
        scratch=[(NX, NY)] * 2, scalars=(4,), far_out=(1,), sems=1,
    )
    got = exchange(message, XY)
    (sums,) = call(
        bind(collect_kernel, nxy), [(2 * rows + nxy // 2 + 2 * part, NY)], got, weight_own, obs_own
    )
    sums = from_axis([sums] * nh, "h")
    pred, pulled, weight, tops, message = call(
        bind(residual_kernel, nxy, nh),
        [(rows, NY), (rows, NY), (rows, NY), (nxy * nh // 2, NY), (nxy, rows, NY)],
        *sums, scratch=[(rows, NY)],
    )
    program.hold(pred, pulled, weight)
    got = exchange(message, XY)
    (power,) = call(bind(power_kernel, nxy * nh), [(KEPT, NY)], tops)
    program.hold(power)
    adjoint = lambda plane: call(
        bind(adjoint_kernel, nxy), [(2 * (QX + rows), NY)] * 2,
        plane.reshape(NX, NY), *factors, power, *tables,
        scratch=[(NX, NY), (4 * rows, NY)],
    )

    def reduce_comps(own, other):
        near, far = call(pair_kernel, [(QX + rows, NY)] * 2, own, flip(other, "k"))
        return near, flip(far, "l")

    pieces = reduce_comps(*adjoint(got))
    message, grad, line, image = call(
        bind(gradient_kernel, nxy, nh),
        [(nxy, rows + 8, NY), (QX, NY), (rows, NY), (rows, NY)],
        *pieces, pulled, dens, weight, scratch=[(rows, NY)],
    )
    program.drop(pulled)
    program.hold(line, image)
    grads = gather_comps(grad)
    got = after(exchange(message, XY), *grads)
    plane, shares = call(bind(part_kernel, nxy), [(NX, NY), (8, NY)], got)
    pieces = adjoint(plane)
    shares = after(from_axis([shares] * nh, "h"), *pieces)
    (shares,) = call(add_kernel, [(8, NY)], *shares)
    shares = from_comps([shares] * 4)
    message, dens, base, alpha = call(
        second_kernel, [(nxy, rows, NY), (QX, NY), (QX, NY), (8, 128)],
        *shares, dens, full, *grads, *factors, *tables, scratch=[(NX, NY)],
    )
    program.alive = [weight, pred, line, image, dens, base, alpha]
    got = exchange(message, XY)
    pieces = reduce_comps(*after(pieces, message))
    grad2, image2, half = call(
        second_gradient_kernel, [(QX, NY), (rows, NY), (8, NY)],
        *pieces, alpha, base, dens, line,
    )
    (parts,) = call(bind(sum_kernel, nxy), [(rows + 8, NY)], got, half)
    program.alive = [pred, image, dens, alpha, grad2]
    shares, image2 = call(
        bind(curvature_kernel, nh, part), [(nxy * 4, 128), (part, NY)],
        *from_axis([parts] * nh, "h"), image2, weight, scratch=[(rows, NY)],
    )
    shares = exchange(shares, (*XY, *COMP))
    program.alive = []
    return tuple(
        call(
            finish_kernel, [density.shape, observed.shape],
            shares, dens, grad2, alpha, pred, image, image2, obs_own, weight_own,
        )
    )


def solution(mesh):
    depth = mesh.shape["depth"]
    sizes = {64: (4, 4, 4), 4: (2, 1, 2)}[depth]
    fine = Mesh(mesh.devices.reshape(*sizes, 2, 2), ALL)
    data = P(COMP, DEPTH, None)
    layer = P(DEPTH, COMP, None)
    return jax.shard_map(
        body,
        mesh=fine,
        in_specs=(layer, data, data, P(DEPTH)),
        out_specs=(layer, data),
        check_vma=False,
    )
```

```python
import functools
import math

import jax
import jax.numpy as jnp
import numpy as np
from jax import lax
from jax.experimental import pallas as pl
from jax.experimental.pallas import tpu as pltpu
from jax.sharding import Mesh
from jax.sharding import PartitionSpec as P

TWO_PI = 2.0 * math.pi
F32 = jnp.float32
BF16 = jnp.bfloat16
XY = ("x", "y")
DEPTH = ("x", "y", "h")
COMP = ("l", "k")
ALL = ("x", "y", "h", "l", "k")

NX = 512
NY = 256
HX = NX // 2
QX = NX // 4
HY = NY // 2


def split_table(table):
    high = table.astype(jnp.bfloat16)
    low = (table - high.astype(np.float64)).astype(jnp.bfloat16)
    return np.stack([high, low])


def basis(count, waves):
    place = np.arange(count)
    rows = []
    for wave in waves:
        norm = math.sqrt((1.0 if wave == 0 else 2.0) / count)
        rows.append(norm * np.cos(TWO_PI * (wave * place % count) / count))
    for wave in waves:
        if wave == 0:
            rows.append(math.sqrt(1.0 / count) * (1.0 - 2.0 * (place % 2)))
        else:
            rows.append(math.sqrt(2.0 / count) * np.sin(TWO_PI * (wave * place % count) / count))
    return np.stack(rows)


def make_tables():
    even = basis(NX, range(0, HX, 2))[:, :HX]
    odd = basis(NX, range(1, HX, 2))[:, :HX]
    col = basis(NY, range(HY))
    return (
        np.concatenate([split_table(even), split_table(odd)]),
        split_table(col.T),
    )


def split(value):
    high = value.astype(BF16)
    low = (value - high.astype(F32)).astype(BF16)
    return high, low


def dot(left, right):
    return jnp.dot(left, right, preferred_element_type=F32)


def dot_turned(left, right):
    return lax.dot_general(left, right, (((1,), (1,)), ((), ())), preferred_element_type=F32)


def times_table(value, high, low):
    vh, vl = split(value)
    return dot(vh, high) + (dot(vl, high) + dot(vh, low))


def times_turned(value, high, low):
    vh, vl = split(value)
    return dot_turned(vh, high) + (dot_turned(vl, high) + dot_turned(vh, low))


def table_times(high, low, value):
    vh, vl = split(value)
    return dot(high, vh) + (dot(high, vl) + dot(low, vh))


def to_waves(field, fx, ty):
    cols = times_table(field, ty[0], ty[1])
    upper, lower = cols[:HX], cols[HX:]
    return (
        table_times(fx[0], fx[1], upper + lower),
        table_times(fx[2], fx[3], upper - lower),
    )


def from_waves(even, odd, bx, ty):
    first = table_times(bx[0], bx[1], even)
    second = table_times(bx[2], bx[3], odd)
    rows = jnp.concatenate([first + second, first - second], axis=0)
    return times_turned(rows, ty[0], ty[1])


def swap_x(half):
    return jnp.concatenate([half[HX // 2 :], half[: HX // 2]], axis=0)


def swap_y(half):
    return jnp.concatenate([half[:, HY:], half[:, :HY]], axis=1)


def sines(cosines, nyquist):
    row = lax.broadcasted_iota(jnp.int32, cosines.shape, 0)
    return jnp.where(row == 0, nyquist, cosines)


def spread(ref):
    even, odd = ref[:QX], ref[QX:HX]
    return (
        jnp.concatenate([even, sines(even, ref[HX : HX + 1])], axis=0),
        jnp.concatenate([odd, odd], axis=0),
    )


def x_factors(gx_ref):
    even, odd = gx_ref[:QX], gx_ref[QX:HX]
    return jnp.concatenate([even, -even], axis=0), jnp.concatenate([odd, -odd], axis=0)


def xx_factors(gx_ref):
    even, odd = spread(gx_ref)
    return -(even * even), -(odd * odd)


def component(even, odd, gx_ref, gy_ref, comp):
    halves = []
    for half, first, second, third in zip(
        (even, odd), x_factors(gx_ref), spread(gy_ref), xx_factors(gx_ref)
    ):
        met = jnp.where(comp == 1, swap_x(half), jnp.where(comp == 2, swap_y(half), half))
        factor = jnp.where(comp == 1, first, jnp.where(comp == 2, second, third))
        halves.append(met * jnp.where(comp == 0, 1.0, factor))
    return halves


def comp_index():
    return lax.axis_index("l") * 2 + lax.axis_index("k")


KEPT = HX + 8


def wave_grid():
    row = lax.broadcasted_iota(jnp.int32, (KEPT, NY), 0)
    col = lax.broadcasted_iota(jnp.int32, (KEPT, NY), 1)
    wave_x = jnp.where(row >= HX, HX, 2 * (row % QX) + (row >= QX).astype(jnp.int32))
    nyquist_y = col == HY
    wave_y = jnp.where(nyquist_y, HY, col % HY)
    kx = wave_x.astype(F32) * (TWO_PI / NX)
    ky = wave_y.astype(F32) * (TWO_PI / NY)
    return kx, ky, col >= HY, nyquist_y


def prepare_kernel(
    top_ref, fx_in, ty_in, dens_in, fx, bx, ty, dens_ref, decay_ref, gx_ref, gy_ref
):
    dens_ref[...] = dens_in[0]
    for place in range(4):
        table = fx_in[place]
        fx[place] = table
        bx[place] = table.astype(F32).T.astype(BF16)
    for place in range(2):
        ty[place] = ty_in[place]
    kx, ky, sine_y, nyquist_y = wave_grid()
    kabs = jnp.sqrt(kx * kx + ky * ky)
    inverse = 1.0 / jnp.maximum(kabs, TWO_PI / max(NX, NY))
    decay_ref[...] = 4.0 * jnp.exp(-kabs * top_ref[0]) * (1.0 - jnp.exp(-kabs))
    gx_ref[...] = kx * inverse
    ry = ky * inverse
    gy_ref[...] = jnp.where(nyquist_y, 0.0, jnp.where(sine_y, -ry, ry))


def gather_rows(pieces, full_ref):
    comp = comp_index()
    for step, piece in enumerate(pieces):
        full_ref[pl.ds(pl.multiple_of(jnp.bitwise_xor(comp, step) * QX, QX), QX), :] = piece[...]


def forward_plane(field, decay_ref, gx_ref, gy_ref, fx, bx, ty):
    even, odd = to_waves(field, fx, ty)
    decay = spread(decay_ref)
    even, odd = component(even * decay[0], odd * decay[1], gx_ref, gy_ref, comp_index())
    return from_waves(even, odd, bx, ty)


def start_kernel(
    nxy, m0, m1, m2, m3, top_ref, decay_ref, gx_ref, gy_ref, fx, bx, ty, out_ref, far_ref, full_ref, pull_ref, sem
):
    rows = NX // nxy
    gather_rows((m0, m1, m2, m3), full_ref)
    copy = pltpu.make_async_copy(full_ref, far_ref, sem)
    copy.start()
    dens = full_ref[...]
    pull_ref[...] = 0.5 * (dens * (1.0 / (dens * dens + 0.25)))
    for place, field in enumerate((full_ref, pull_ref)):
        plane = forward_plane(field[...], decay_ref, gx_ref, gy_ref, fx, bx, ty)
        for target in range(nxy):
            out_ref[target, place * rows : (place + 1) * rows, :] = plane[
                target * rows : (target + 1) * rows
            ]
    for target in range(nxy):
        out_ref[target, 2 * rows : 2 * rows + 8, :] = jnp.full((8, NY), top_ref[0], F32)
    copy.wait()


def collect_kernel(nxy, got_ref, weight_ref, obs_ref, sum_ref):
    rows = NX // nxy
    total = got_ref[0, : 2 * rows, :]
    for source in range(1, nxy):
        total = total + got_ref[source, : 2 * rows, :]
    sum_ref[: 2 * rows] = total
    left = lax.broadcasted_iota(jnp.int32, (1, NY), 1) < HY
    for pair in range(nxy // 2):
        first, second = (got_ref[2 * pair + i, 2 * rows : 2 * rows + 1, :] for i in (0, 1))
        sum_ref[2 * rows + pair : 2 * rows + pair + 1, :] = jnp.where(left, first, second)
    part = weight_ref.shape[0]
    start = 2 * rows + nxy // 2
    sum_ref[start : start + part] = weight_ref[...]
    sum_ref[start + part : start + 2 * part] = obs_ref[...]


def residual_kernel(nxy, nh, *refs):
    rows = NX // nxy
    part = rows // nh
    pairs = nxy // 2
    start = 2 * rows + pairs
    sums = refs[:nh]
    pred_ref, pull_ref, weight_ref, tops_ref, send_ref, meas_ref = refs[nh:]
    chip = lax.axis_index("h")
    total = sums[0][: 2 * rows]
    for step in range(1, nh):
        total = total + sums[step][: 2 * rows]
    for step in range(nh):
        tops_ref[step * pairs : (step + 1) * pairs] = sums[step][2 * rows : start]
        place = pl.ds(pl.multiple_of(lax.rem(chip + (nh - step), nh) * part, part), part)
        weight_ref[place, :] = sums[step][start : start + part]
        meas_ref[place, :] = sums[step][start + part :]
    weight = weight_ref[...]
    pred = total[:rows]
    pred_ref[...] = pred
    pull_ref[...] = total[rows:]
    res = weight * (weight * (pred - meas_ref[...]))
    for target in range(nxy):
        send_ref[target] = res


def power_kernel(layers, tops_ref, power_ref):
    kx, ky, *_ = wave_grid()
    for start in range(0, KEPT, 64):
        stop = min(start + 64, KEPT)
        ks = jnp.sqrt(kx[start:stop] ** 2 + ky[start:stop] ** 2)
        double = -2.0 * ks

        def add(step, total):
            for pair in range(2):
                tops = tops_ref[pl.ds(2 * step + pair, 1), :]
                for top in (tops[:, :HY], tops[:, HY:]):
                    total = total + jnp.exp(double * jnp.concatenate([top, top], axis=1))
            return total

        total = lax.fori_loop(0, layers // 4, add, jnp.zeros_like(ks))
        rise = 1.0 - jnp.exp(-ks)
        power_ref[start:stop] = (16.0 * (rise * rise)) * total


def adjoint_kernel(
    nxy, res_ref, decay_ref, gx_ref, gy_ref, power_ref, fx, bx, ty, own_out, other_out, z_ref, i_ref
):
    rows = NX // nxy
    comp = comp_index()
    even, odd = to_waves(res_ref[...], fx, ty)
    even, odd = component(even, odd, gx_ref, gy_ref, comp)
    sign = jnp.where((comp == 1) | (comp == 2), -1.0, 1.0)
    even = even * sign
    odd = odd * sign
    decay = spread(decay_ref)
    z_ref[...] = from_waves(even * decay[0], odd * decay[1], bx, ty)
    power = spread(power_ref)
    even = even * power[0]
    odd = odd * power[1]
    block = lax.axis_index("x") * lax.axis_size("y") + lax.axis_index("y")
    upper = block * rows < HX
    near = pl.ds(pl.multiple_of(lax.rem(block * rows, HX), rows), rows)
    flip = jnp.where(upper, 1.0, -1.0)
    for target in range(4):
        if target == 0:
            e, o = even, odd
        elif target == 1:
            first = x_factors(gx_ref)
            e, o = swap_x(even) * first[0], swap_x(odd) * first[1]
        elif target == 2:
            second = spread(gy_ref)
            e, o = swap_y(even) * second[0], swap_y(odd) * second[1]
        else:
            third = xx_factors(gx_ref)
            e, o = even * third[0], odd * third[1]
        line = table_times(bx[0, near, :], bx[1, near, :], e)
        line = line + flip * table_times(bx[2, near, :], bx[3, near, :], o)
        i_ref[target * rows : (target + 1) * rows, :] = line
    i_ref[...] = times_turned(i_ref[...], ty[0], ty[1])
    for step in range(4):
        out = (own_out, other_out)[step % 2]
        begin = (step // 2) * (QX + rows)
        other = jnp.bitwise_xor(comp, step)
        out[begin : begin + QX] = z_ref[pl.ds(pl.multiple_of(other * QX, QX), QX), :]
        out[begin + QX : begin + QX + rows] = i_ref[
            pl.ds(pl.multiple_of(other * rows, rows), rows), :
        ]


def pair_kernel(own_ref, got_ref, near_ref, far_ref):
    half = near_ref.shape[0]
    near_ref[...] = own_ref[:half] + got_ref[:half]
    far_ref[...] = own_ref[half:] + got_ref[half:]


def share(grad, quad, image, weight, scratch, part):
    scratch[...] = weight * image
    place = pl.ds(pl.multiple_of(lax.axis_index("h") * part, part), part)
    mine = scratch[place, :]
    lane = lax.broadcasted_iota(jnp.int32, (1, NY), 1)
    square = grad * grad
    gg = jnp.sum(square)
    qgg = jnp.sum(quad * square)
    curv = jnp.sum(mine * mine)
    return jnp.where(lane == 0, gg, jnp.where(lane == 1, qgg, jnp.where(lane == 2, curv, 0.0)))


def step_length(shares):
    total = jnp.sum(shares, axis=0, keepdims=True)
    lane = lax.broadcasted_iota(jnp.int32, total.shape, 1)
    pick = lambda place: jnp.sum(jnp.where(lane == place, total, 0.0), keepdims=True)
    return pick(0) / (pick(2) + 0.5 * pick(1))


def gradient_kernel(nxy, nh, *refs):
    rows = NX // nxy
    part = rows // nh
    pieces = refs[:2]
    pull_ref, dens_ref, weight_ref = refs[2:5]
    send_ref, grad_ref, line_ref, image_ref, scratch = refs[5:]
    total = pieces[0][...] + pieces[1][...]
    data = total[:QX]
    line = total[QX:]
    dens = dens_ref[...]
    quad = 1.0 / (dens * dens + 0.25)
    grad = data + 0.5 * (quad * dens)
    image = line + pull_ref[...]
    weight = weight_ref[...]
    mine = jnp.broadcast_to(share(grad, quad, image, weight, scratch, part), (8, NY))
    grad_ref[...] = grad
    line_ref[...] = line
    image_ref[...] = image
    back = weight * (weight * image)
    for target in range(nxy):
        send_ref[target, :rows] = back
        send_ref[target, rows:] = mine


def part_kernel(nxy, got_ref, plane_ref, share_ref):
    rows = NX // nxy
    total = got_ref[0, rows:, :]
    for source in range(1, nxy):
        total = total + got_ref[source, rows:, :]
    share_ref[...] = total
    for source in range(nxy):
        plane_ref[source * rows : (source + 1) * rows] = got_ref[source, :rows, :]


def add_kernel(*refs):
    total = refs[0][...]
    for part in refs[1:-1]:
        total = total + part[...]
    refs[-1][...] = total


def second_kernel(
    s0, s1, s2, s3, dens_ref, full_ref, g0, g1, g2, g3, decay_ref, gx_ref, gy_ref, fx, bx, ty,
    out_ref, dens_out, base_out, alpha_ref, all_ref,
):
    gather_rows((g0, g1, g2, g3), all_ref)
    alpha = step_length(s0[:1] + s1[:1] + (s2[:1] + s3[:1]))
    alpha_ref[...] = jnp.broadcast_to(alpha, alpha_ref.shape)
    old = dens_ref[...]
    grad = g0[...]
    dens = old - alpha * grad
    dens_out[...] = dens
    data = grad - 0.5 * ((1.0 / (old * old + 0.25)) * old)
    base_out[...] = data + 0.5 * (dens * (1.0 / (dens * dens + 0.25)))
    dens = full_ref[...] - alpha * all_ref[...]
    all_ref[...] = 0.5 * (dens * (1.0 / (dens * dens + 0.25)))
    plane = forward_plane(all_ref[...], decay_ref, gx_ref, gy_ref, fx, bx, ty)
    out_ref[...] = plane.reshape(out_ref.shape)


def sum_kernel(nxy, got_ref, half_ref, sum_ref):
    rows = NX // nxy
    total = got_ref[0]
    for source in range(1, nxy):
        total = total + got_ref[source]
    sum_ref[:rows] = total
    sum_ref[rows:] = half_ref[...]


def second_gradient_kernel(
    u0, u1, alpha_ref, base_ref, dens_ref, line_ref, grad_ref, image_ref, share_ref
):
    alpha = alpha_ref[:1, :1]
    total = u0[...] + u1[...]
    dens = dens_ref[...]
    grad = base_ref[...] - alpha * total[:QX]
    quad = 1.0 / (dens * dens + 0.25)
    grad_ref[...] = grad
    image_ref[...] = line_ref[...] - alpha * total[QX:]
    square = grad * grad
    lane = lax.broadcasted_iota(jnp.int32, (8, NY), 1)
    share_ref[...] = jnp.where(
        lane == 0, jnp.sum(square), jnp.where(lane == 1, jnp.sum(quad * square), 0.0)
    )


def curvature_kernel(nh, part, *refs):
    parts = refs[:nh]
    image_ref, weight_ref, share_ref, out_ref, scratch = refs[nh:]
    rows = image_ref.shape[0]
    total = parts[0][...]
    for piece in parts[1:]:
        total = total + piece[...]
    image = image_ref[...] + total[:rows]
    scratch[...] = image
    out_ref[...] = scratch[pl.ds(pl.multiple_of(lax.axis_index("h") * part, part), part), :]
    mine = weight_ref[...] * image
    lane = lax.broadcasted_iota(jnp.int32, (1, 128), 1)
    share_ref[...] = jnp.broadcast_to(
        jnp.where(lane == 2, jnp.sum(mine * mine), total[rows : rows + 1, :128]), share_ref.shape
    )


def finish_kernel(
    shares_ref, dens_ref, grad_ref, alpha_ref, pred_ref, first_ref, second_ref, obs_ref, w_ref, dens_out, err_out
):
    part = obs_ref.shape[0]
    alpha = step_length(shares_ref[...])
    dens_out[0] = dens_ref[...] - alpha * grad_ref[...]
    place = pl.ds(pl.multiple_of(lax.axis_index("h") * part, part), part)
    pred = pred_ref[place, :] - alpha_ref[:1, :1] * first_ref[place, :]
    pred = pred - alpha * second_ref[...]
    err_out[0] = w_ref[...] * (pred - obs_ref[...])


VMEM = pl.BlockSpec(memory_space=pltpu.VMEM)
SMEM = pl.BlockSpec(memory_space=pltpu.SMEM)
ANY = pl.BlockSpec(memory_space=pl.ANY)


class Program:
    def __init__(self):
        self.alive = []

    def hold(self, *values):
        self.alive += values

    def drop(self, *values):
        self.alive = [item for item in self.alive if all(item is not value for value in values)]

    def call(self, kernel, outs, *args, scratch=(), scalars=(), far_out=(), sems=0, mib=8):
        used = len(args)
        keep = [item for item in self.alive if all(item is not value for value in args)]
        kept = len(keep)

        def inner(*refs):
            kernel(*refs[:used], *refs[used + kept :])

        kinds = [(item, F32) if isinstance(item, tuple) else (item.shape, item.dtype) for item in outs]
        return pl.pallas_call(
            inner,
            out_shape=[jax.ShapeDtypeStruct(shape, dtype) for shape, dtype in kinds],
            in_specs=[
                SMEM if place in scalars else VMEM for place in range(used)
            ]
            + [ANY] * kept,
            out_specs=[ANY if place in far_out else VMEM for place in range(len(outs))],
            scratch_shapes=[pltpu.VMEM(shape, F32) for shape in scratch]
            + [pltpu.SemaphoreType.DMA((sems,) if sems > 1 else ())] * (sems > 0),
            compiler_params=pltpu.CompilerParams(vmem_limit_bytes=mib << 20),
        )(*args, *keep)


def from_comps(values):
    return [values[0]] + [
        lax.ppermute(values[step], COMP, [(i, i ^ step) for i in range(4)]) for step in (1, 2, 3)
    ]


def flip(value, axis):
    return lax.ppermute(value, axis, [(0, 1), (1, 0)])


def gather_comps(value):
    across = flip(value, "l")
    return [value, flip(value, "k"), across, flip(across, "k")]


def from_axis(values, axis):
    size = len(values)
    return [values[0]] + [
        lax.ppermute(values[step], axis, [(i, (i + step) % size) for i in range(size)])
        for step in range(1, size)
    ]


def exchange(value, axes):
    return lax.all_to_all(value, axes, 0, 0, tiled=True)


def after(values, *others):
    if isinstance(values, (list, tuple)):
        return list(lax.optimization_barrier((tuple(values), others))[0])
    return lax.optimization_barrier((values, others))[0]


def body(density, observed, data_weight, layer_top):
    nx, ny, nh = (lax.axis_size(axis) for axis in DEPTH)
    nxy = nx * ny
    rows = NX // nxy
    part = rows // nh
    fx, ty = (jnp.asarray(table) for table in make_tables())
    bind = functools.partial
    program = Program()
    call = program.call

    near, across = flip(density[0], "k"), flip(density[0], "l")
    *tables, dens, decay, gx, gy = call(
        prepare_kernel,
        [fx, fx, ty, (QX, NY), (KEPT, NY), (KEPT, NY), (KEPT, NY)],
        layer_top, fx, ty, density, scalars=(0,),
    )
    layers = [near, across, flip(after(across, dens), "k")]
    factors = (decay, gx, gy)
    weight_own, obs_own = data_weight[0], observed[0]
    program.hold(*tables, *factors, dens)
    message, full = call(
        bind(start_kernel, nxy), [(nxy, 2 * rows + 8, NY), (NX, NY)],
        dens, *layers, layer_top, *factors, *tables,
        scratch=[(NX, NY)] * 2, scalars=(4,), far_out=(1,), sems=1,
    )
    got = exchange(message, XY)
    (sums,) = call(
        bind(collect_kernel, nxy), [(2 * rows + nxy // 2 + 2 * part, NY)], got, weight_own, obs_own
    )
    sums = from_axis([sums] * nh, "h")
    pred, pulled, weight, tops, message = call(
        bind(residual_kernel, nxy, nh),
        [(rows, NY), (rows, NY), (rows, NY), (nxy * nh // 2, NY), (nxy, rows, NY)],
        *sums, scratch=[(rows, NY)],
    )
    program.hold(pred, pulled, weight)
    got = exchange(message, XY)
    (power,) = call(bind(power_kernel, nxy * nh), [(KEPT, NY)], tops)
    program.hold(power)
    adjoint = lambda plane: call(
        bind(adjoint_kernel, nxy), [(2 * (QX + rows), NY)] * 2,
        plane.reshape(NX, NY), *factors, power, *tables,
        scratch=[(NX, NY), (4 * rows, NY)],
    )

    def reduce_comps(own, other):
        near, far = call(pair_kernel, [(QX + rows, NY)] * 2, own, flip(other, "k"))
        return near, flip(far, "l")

    pieces = reduce_comps(*adjoint(got))
    message, grad, line, image = call(
        bind(gradient_kernel, nxy, nh),
        [(nxy, rows + 8, NY), (QX, NY), (rows, NY), (rows, NY)],
        *pieces, pulled, dens, weight, scratch=[(rows, NY)],
    )
    program.drop(pulled)
    program.hold(line, image)
    grads = gather_comps(grad)
    got = after(exchange(message, XY), *grads)
    plane, shares = call(bind(part_kernel, nxy), [(NX, NY), (8, NY)], got)
    (shares,) = call(add_kernel, [(8, NY)], *from_axis([shares] * nh, "h"))
    pieces = adjoint(after(plane, shares))
    shares = after(from_comps([shares] * 4), *pieces)
    message, dens, base, alpha = call(
        second_kernel, [(nxy, rows, NY), (QX, NY), (QX, NY), (8, 128)],
        *shares, dens, full, *grads, *factors, *tables, scratch=[(NX, NY)],
    )
    program.alive = [weight, pred, line, image, dens, base, alpha]
    got = exchange(message, XY)
    pieces = reduce_comps(*after(pieces, message))
    grad2, image2, half = call(
        second_gradient_kernel, [(QX, NY), (rows, NY), (8, NY)],
        *pieces, alpha, base, dens, line,
    )
    (parts,) = call(bind(sum_kernel, nxy), [(rows + 8, NY)], got, half)
    program.alive = [pred, image, dens, alpha, grad2]
    shares, image2 = call(
        bind(curvature_kernel, nh, part), [(nxy * 4, 128), (part, NY)],
        *from_axis([parts] * nh, "h"), image2, weight, scratch=[(rows, NY)],
    )
    shares = exchange(shares, (*XY, *COMP))
    program.alive = []
    return tuple(
        call(
            finish_kernel, [density.shape, observed.shape],
            shares, dens, grad2, alpha, pred, image, image2, obs_own, weight_own,
        )
    )


def solution(mesh):
    depth = mesh.shape["depth"]
    sizes = {64: (4, 4, 4), 4: (2, 1, 2)}[depth]
    fine = Mesh(mesh.devices.reshape(*sizes, 2, 2), ALL)
    data = P(COMP, DEPTH, None)
    layer = P(DEPTH, COMP, None)
    return jax.shard_map(
        body,
        mesh=fine,
        in_specs=(layer, data, data, P(DEPTH)),
        out_specs=(layer, data),
        check_vma=False,
    )
```

```python
import functools
import math

import jax
import jax.numpy as jnp
import numpy as np
from jax import lax
from jax.experimental import pallas as pl
from jax.experimental.pallas import tpu as pltpu
from jax.sharding import Mesh
from jax.sharding import PartitionSpec as P

TWO_PI = 2.0 * math.pi
F32 = jnp.float32
BF16 = jnp.bfloat16
XY = ("x", "y")
DEPTH = ("x", "y", "h")
COMP = ("l", "k")
ALL = ("x", "y", "h", "l", "k")

NX = 512
NY = 256
HX = NX // 2
QX = NX // 4
HY = NY // 2


def split_table(table):
    high = table.astype(jnp.bfloat16)
    low = (table - high.astype(np.float64)).astype(jnp.bfloat16)
    return np.stack([high, low])


def basis(count, waves):
    place = np.arange(count)
    rows = []
    for wave in waves:
        norm = math.sqrt((1.0 if wave == 0 else 2.0) / count)
        rows.append(norm * np.cos(TWO_PI * (wave * place % count) / count))
    for wave in waves:
        if wave == 0:
            rows.append(math.sqrt(1.0 / count) * (1.0 - 2.0 * (place % 2)))
        else:
            rows.append(math.sqrt(2.0 / count) * np.sin(TWO_PI * (wave * place % count) / count))
    return np.stack(rows)


def make_tables():
    even = basis(NX, range(0, HX, 2))[:, :HX]
    odd = basis(NX, range(1, HX, 2))[:, :HX]
    col = basis(NY, range(HY))
    return (
        np.concatenate([split_table(even), split_table(odd)]),
        split_table(col.T),
    )


def split(value):
    high = value.astype(BF16)
    low = (value - high.astype(F32)).astype(BF16)
    return high, low


def dot(left, right):
    return jnp.dot(left, right, preferred_element_type=F32)


def dot_turned(left, right):
    return lax.dot_general(left, right, (((1,), (1,)), ((), ())), preferred_element_type=F32)


def times_table(value, high, low):
    vh, vl = split(value)
    return dot(vh, high) + (dot(vl, high) + dot(vh, low))


def times_turned(value, high, low):
    vh, vl = split(value)
    return dot_turned(vh, high) + (dot_turned(vl, high) + dot_turned(vh, low))


def table_times(high, low, value):
    vh, vl = split(value)
    return dot(high, vh) + (dot(high, vl) + dot(low, vh))


def to_waves(field, fx, ty):
    cols = times_table(field, ty[0], ty[1])
    upper, lower = cols[:HX], cols[HX:]
    return (
        table_times(fx[0], fx[1], upper + lower),
        table_times(fx[2], fx[3], upper - lower),
    )


def from_waves(even, odd, bx, ty):
    first = table_times(bx[0], bx[1], even)
    second = table_times(bx[2], bx[3], odd)
    rows = jnp.concatenate([first + second, first - second], axis=0)
    return times_turned(rows, ty[0], ty[1])


def swap_x(half):
    return jnp.concatenate([half[HX // 2 :], half[: HX // 2]], axis=0)


def swap_y(half):
    return jnp.concatenate([half[:, HY:], half[:, :HY]], axis=1)


def sines(cosines, nyquist):
    row = lax.broadcasted_iota(jnp.int32, cosines.shape, 0)
    return jnp.where(row == 0, nyquist, cosines)


def spread(ref):
    even, odd = ref[:QX], ref[QX:HX]
    return (
        jnp.concatenate([even, sines(even, ref[HX : HX + 1])], axis=0),
        jnp.concatenate([odd, odd], axis=0),
    )


def x_factors(gx_ref):
    even, odd = gx_ref[:QX], gx_ref[QX:HX]
    return jnp.concatenate([even, -even], axis=0), jnp.concatenate([odd, -odd], axis=0)


def xx_factors(gx_ref):
    even, odd = spread(gx_ref)
    return -(even * even), -(odd * odd)


def component(even, odd, gx_ref, gy_ref, comp):
    halves = []
    for half, first, second, third in zip(
        (even, odd), x_factors(gx_ref), spread(gy_ref), xx_factors(gx_ref)
    ):
        met = jnp.where(comp == 1, swap_x(half), jnp.where(comp == 2, swap_y(half), half))
        factor = jnp.where(comp == 1, first, jnp.where(comp == 2, second, third))
        halves.append(met * jnp.where(comp == 0, 1.0, factor))
    return halves


def comp_index():
    return lax.axis_index("l") * 2 + lax.axis_index("k")


KEPT = HX + 8


def wave_grid():
    row = lax.broadcasted_iota(jnp.int32, (KEPT, NY), 0)
    col = lax.broadcasted_iota(jnp.int32, (KEPT, NY), 1)
    wave_x = jnp.where(row >= HX, HX, 2 * (row % QX) + (row >= QX).astype(jnp.int32))
    nyquist_y = col == HY
    wave_y = jnp.where(nyquist_y, HY, col % HY)
    kx = wave_x.astype(F32) * (TWO_PI / NX)
    ky = wave_y.astype(F32) * (TWO_PI / NY)
    return kx, ky, col >= HY, nyquist_y


def prepare_kernel(
    top_ref, fx_in, ty_in, dens_in, fx, bx, ty, dens_ref, decay_ref, gx_ref, gy_ref
):
    dens_ref[...] = dens_in[0]
    for place in range(4):
        table = fx_in[place]
        fx[place] = table
        bx[place] = table.astype(F32).T.astype(BF16)
    for place in range(2):
        ty[place] = ty_in[place]
    kx, ky, sine_y, nyquist_y = wave_grid()
    kabs = jnp.sqrt(kx * kx + ky * ky)
    inverse = 1.0 / jnp.maximum(kabs, TWO_PI / max(NX, NY))
    decay_ref[...] = 4.0 * jnp.exp(-kabs * top_ref[0]) * (1.0 - jnp.exp(-kabs))
    gx_ref[...] = kx * inverse
    ry = ky * inverse
    gy_ref[...] = jnp.where(nyquist_y, 0.0, jnp.where(sine_y, -ry, ry))


def gather_rows(pieces, full_ref):
    comp = comp_index()
    for step, piece in enumerate(pieces):
        full_ref[pl.ds(pl.multiple_of(jnp.bitwise_xor(comp, step) * QX, QX), QX), :] = piece[...]


def forward_plane(field, decay_ref, gx_ref, gy_ref, fx, bx, ty):
    even, odd = to_waves(field, fx, ty)
    decay = spread(decay_ref)
    even, odd = component(even * decay[0], odd * decay[1], gx_ref, gy_ref, comp_index())
    return from_waves(even, odd, bx, ty)


def start_kernel(
    nxy, m0, m1, m2, m3, top_ref, decay_ref, gx_ref, gy_ref, fx, bx, ty, out_ref, far_ref, full_ref, pull_ref, sem
):
    rows = NX // nxy
    gather_rows((m0, m1, m2, m3), full_ref)
    copy = pltpu.make_async_copy(full_ref, far_ref, sem)
    copy.start()
    dens = full_ref[...]
    pull_ref[...] = 0.5 * (dens * (1.0 / (dens * dens + 0.25)))
    for place, field in enumerate((full_ref, pull_ref)):
        plane = forward_plane(field[...], decay_ref, gx_ref, gy_ref, fx, bx, ty)
        for target in range(nxy):
            out_ref[target, place * rows : (place + 1) * rows, :] = plane[
                target * rows : (target + 1) * rows
            ]
    for target in range(nxy):
        out_ref[target, 2 * rows : 2 * rows + 8, :] = jnp.full((8, NY), top_ref[0], F32)
    copy.wait()


def collect_kernel(nxy, got_ref, weight_ref, obs_ref, sum_ref):
    rows = NX // nxy
    total = got_ref[0, : 2 * rows, :]
    for source in range(1, nxy):
        total = total + got_ref[source, : 2 * rows, :]
    sum_ref[: 2 * rows] = total
    left = lax.broadcasted_iota(jnp.int32, (1, NY), 1) < HY
    for pair in range(nxy // 2):
        first, second = (got_ref[2 * pair + i, 2 * rows : 2 * rows + 1, :] for i in (0, 1))
        sum_ref[2 * rows + pair : 2 * rows + pair + 1, :] = jnp.where(left, first, second)
    part = weight_ref.shape[0]
    start = 2 * rows + nxy // 2
    sum_ref[start : start + part] = weight_ref[...]
    sum_ref[start + part : start + 2 * part] = obs_ref[...]


def send_all(block_ref, far_ref, sems):
    copies = [
        pltpu.make_async_copy(block_ref, far_ref.at[place], sems.at[place])
        for place in range(far_ref.shape[0])
    ]
    for copy in copies:
        copy.start()
    return copies


def residual_kernel(nxy, nh, *refs):
    rows = NX // nxy
    part = rows // nh
    pairs = nxy // 2
    start = 2 * rows + pairs
    sums = refs[:nh]
    pred_ref, pull_ref, weight_ref, tops_ref, far_ref, meas_ref, block_ref, sems = refs[nh:]
    chip = lax.axis_index("h")
    total = sums[0][: 2 * rows]
    for step in range(1, nh):
        total = total + sums[step][: 2 * rows]
    for step in range(nh):
        tops_ref[step * pairs : (step + 1) * pairs] = sums[step][2 * rows : start]
        place = pl.ds(pl.multiple_of(lax.rem(chip + (nh - step), nh) * part, part), part)
        weight_ref[place, :] = sums[step][start : start + part]
        meas_ref[place, :] = sums[step][start + part :]
    weight = weight_ref[...]
    pred = total[:rows]
    block_ref[...] = weight * (weight * (pred - meas_ref[...]))
    copies = send_all(block_ref, far_ref, sems)
    pred_ref[...] = pred
    pull_ref[...] = total[rows:]
    for copy in copies:
        copy.wait()


def power_kernel(layers, tops_ref, power_ref):
    kx, ky, *_ = wave_grid()
    for start in range(0, KEPT, 64):
        stop = min(start + 64, KEPT)
        ks = jnp.sqrt(kx[start:stop] ** 2 + ky[start:stop] ** 2)
        double = -2.0 * ks

        def add(step, total):
            for pair in range(2):
                tops = tops_ref[pl.ds(2 * step + pair, 1), :]
                for top in (tops[:, :HY], tops[:, HY:]):
                    total = total + jnp.exp(double * jnp.concatenate([top, top], axis=1))
            return total

        total = lax.fori_loop(0, layers // 4, add, jnp.zeros_like(ks))
        rise = 1.0 - jnp.exp(-ks)
        power_ref[start:stop] = (16.0 * (rise * rise)) * total


def adjoint_kernel(
    nxy, res_ref, decay_ref, gx_ref, gy_ref, power_ref, fx, bx, ty, own_out, other_out, z_ref, i_ref
):
    rows = NX // nxy
    comp = comp_index()
    even, odd = to_waves(res_ref[...], fx, ty)
    even, odd = component(even, odd, gx_ref, gy_ref, comp)
    sign = jnp.where((comp == 1) | (comp == 2), -1.0, 1.0)
    even = even * sign
    odd = odd * sign
    decay = spread(decay_ref)
    z_ref[...] = from_waves(even * decay[0], odd * decay[1], bx, ty)
    power = spread(power_ref)
    even = even * power[0]
    odd = odd * power[1]
    block = lax.axis_index("x") * lax.axis_size("y") + lax.axis_index("y")
    upper = block * rows < HX
    near = pl.ds(pl.multiple_of(lax.rem(block * rows, HX), rows), rows)
    flip = jnp.where(upper, 1.0, -1.0)
    for target in range(4):
        if target == 0:
            e, o = even, odd
        elif target == 1:
            first = x_factors(gx_ref)
            e, o = swap_x(even) * first[0], swap_x(odd) * first[1]
        elif target == 2:
            second = spread(gy_ref)
            e, o = swap_y(even) * second[0], swap_y(odd) * second[1]
        else:
            third = xx_factors(gx_ref)
            e, o = even * third[0], odd * third[1]
        line = table_times(bx[0, near, :], bx[1, near, :], e)
        line = line + flip * table_times(bx[2, near, :], bx[3, near, :], o)
        i_ref[target * rows : (target + 1) * rows, :] = line
    i_ref[...] = times_turned(i_ref[...], ty[0], ty[1])
    for step in range(4):
        out = (own_out, other_out)[step % 2]
        begin = (step // 2) * (QX + rows)
        other = jnp.bitwise_xor(comp, step)
        out[begin : begin + QX] = z_ref[pl.ds(pl.multiple_of(other * QX, QX), QX), :]
        out[begin + QX : begin + QX + rows] = i_ref[
            pl.ds(pl.multiple_of(other * rows, rows), rows), :
        ]


def pair_kernel(own_ref, got_ref, near_ref, far_ref):
    half = near_ref.shape[0]
    near_ref[...] = own_ref[:half] + got_ref[:half]
    far_ref[...] = own_ref[half:] + got_ref[half:]


def share(grad, quad, image, weight, scratch, part):
    scratch[...] = weight * image
    place = pl.ds(pl.multiple_of(lax.axis_index("h") * part, part), part)
    mine = scratch[place, :]
    lane = lax.broadcasted_iota(jnp.int32, (1, NY), 1)
    square = grad * grad
    gg = jnp.sum(square)
    qgg = jnp.sum(quad * square)
    curv = jnp.sum(mine * mine)
    return jnp.where(lane == 0, gg, jnp.where(lane == 1, qgg, jnp.where(lane == 2, curv, 0.0)))


def step_length(shares):
    total = jnp.sum(shares, axis=0, keepdims=True)
    lane = lax.broadcasted_iota(jnp.int32, total.shape, 1)
    pick = lambda place: jnp.sum(jnp.where(lane == place, total, 0.0), keepdims=True)
    return pick(0) / (pick(2) + 0.5 * pick(1))


def gradient_kernel(nxy, nh, *refs):
    rows = NX // nxy
    part = rows // nh
    pieces = refs[:2]
    pull_ref, dens_ref, weight_ref = refs[2:5]
    far_ref, grad_ref, line_ref, image_ref, scratch, block_ref, sems = refs[5:]
    total = pieces[0][...] + pieces[1][...]
    data = total[:QX]
    line = total[QX:]
    dens = dens_ref[...]
    quad = 1.0 / (dens * dens + 0.25)
    grad = data + 0.5 * (quad * dens)
    image = line + pull_ref[...]
    weight = weight_ref[...]
    block_ref[:rows] = weight * (weight * image)
    block_ref[rows:] = jnp.broadcast_to(share(grad, quad, image, weight, scratch, part), (8, NY))
    copies = send_all(block_ref, far_ref, sems)
    grad_ref[...] = grad
    line_ref[...] = line
    image_ref[...] = image
    for copy in copies:
        copy.wait()


def part_kernel(nxy, got_ref, plane_ref, share_ref):
    rows = NX // nxy
    total = got_ref[0, rows:, :]
    for source in range(1, nxy):
        total = total + got_ref[source, rows:, :]
    share_ref[...] = total
    for source in range(nxy):
        plane_ref[source * rows : (source + 1) * rows] = got_ref[source, :rows, :]


def add_kernel(*refs):
    total = refs[0][...]
    for part in refs[1:-1]:
        total = total + part[...]
    refs[-1][...] = total


def second_kernel(
    s0, s1, s2, s3, dens_ref, full_ref, g0, g1, g2, g3, decay_ref, gx_ref, gy_ref, fx, bx, ty,
    out_ref, dens_out, base_out, alpha_ref, all_ref,
):
    gather_rows((g0, g1, g2, g3), all_ref)
    alpha = step_length(s0[:1] + s1[:1] + (s2[:1] + s3[:1]))
    alpha_ref[...] = jnp.broadcast_to(alpha, alpha_ref.shape)
    old = dens_ref[...]
    grad = g0[...]
    dens = old - alpha * grad
    dens_out[...] = dens
    data = grad - 0.5 * ((1.0 / (old * old + 0.25)) * old)
    base_out[...] = data + 0.5 * (dens * (1.0 / (dens * dens + 0.25)))
    dens = full_ref[...] - alpha * all_ref[...]
    all_ref[...] = 0.5 * (dens * (1.0 / (dens * dens + 0.25)))
    plane = forward_plane(all_ref[...], decay_ref, gx_ref, gy_ref, fx, bx, ty)
    out_ref[...] = plane.reshape(out_ref.shape)


def sum_kernel(nxy, got_ref, half_ref, sum_ref):
    rows = NX // nxy
    total = got_ref[0]
    for source in range(1, nxy):
        total = total + got_ref[source]
    sum_ref[:rows] = total
    sum_ref[rows:] = half_ref[...]


def second_gradient_kernel(
    u0, u1, alpha_ref, base_ref, dens_ref, line_ref, grad_ref, image_ref, share_ref
):
    alpha = alpha_ref[:1, :1]
    total = u0[...] + u1[...]
    dens = dens_ref[...]
    grad = base_ref[...] - alpha * total[:QX]
    quad = 1.0 / (dens * dens + 0.25)
    grad_ref[...] = grad
    image_ref[...] = line_ref[...] - alpha * total[QX:]
    square = grad * grad
    lane = lax.broadcasted_iota(jnp.int32, (8, NY), 1)
    share_ref[...] = jnp.where(
        lane == 0, jnp.sum(square), jnp.where(lane == 1, jnp.sum(quad * square), 0.0)
    )


def curvature_kernel(nh, part, *refs):
    parts = refs[:nh]
    image_ref, weight_ref, share_ref, out_ref, scratch = refs[nh:]
    rows = image_ref.shape[0]
    total = parts[0][...]
    for piece in parts[1:]:
        total = total + piece[...]
    image = image_ref[...] + total[:rows]
    scratch[...] = image
    out_ref[...] = scratch[pl.ds(pl.multiple_of(lax.axis_index("h") * part, part), part), :]
    mine = weight_ref[...] * image
    lane = lax.broadcasted_iota(jnp.int32, (1, 128), 1)
    share_ref[...] = jnp.broadcast_to(
        jnp.where(lane == 2, jnp.sum(mine * mine), total[rows : rows + 1, :128]), share_ref.shape
    )


def finish_kernel(
    shares_ref, dens_ref, grad_ref, alpha_ref, pred_ref, first_ref, second_ref, obs_ref, w_ref, dens_out, err_out
):
    part = obs_ref.shape[0]
    alpha = step_length(shares_ref[...])
    dens_out[0] = dens_ref[...] - alpha * grad_ref[...]
    place = pl.ds(pl.multiple_of(lax.axis_index("h") * part, part), part)
    pred = pred_ref[place, :] - alpha_ref[:1, :1] * first_ref[place, :]
    pred = pred - alpha * second_ref[...]
    err_out[0] = w_ref[...] * (pred - obs_ref[...])


VMEM = pl.BlockSpec(memory_space=pltpu.VMEM)
SMEM = pl.BlockSpec(memory_space=pltpu.SMEM)
ANY = pl.BlockSpec(memory_space=pl.ANY)
FAR = pl.BlockSpec(memory_space=pltpu.HBM)


class Program:
    def __init__(self):
        self.alive = []

    def hold(self, *values):
        self.alive += values

    def drop(self, *values):
        self.alive = [item for item in self.alive if all(item is not value for value in values)]

    def call(self, kernel, outs, *args, scratch=(), scalars=(), far_out=(), sems=0, mib=8):
        used = len(args)
        keep = [item for item in self.alive if all(item is not value for value in args)]
        kept = len(keep)

        def inner(*refs):
            kernel(*refs[:used], *refs[used + kept :])

        kinds = [(item, F32) if isinstance(item, tuple) else (item.shape, item.dtype) for item in outs]
        return pl.pallas_call(
            inner,
            out_shape=[
                (pltpu.HBM if place in far_out else jax.ShapeDtypeStruct)(*kind)
                for place, kind in enumerate(kinds)
            ],
            in_specs=[
                SMEM if place in scalars else VMEM for place in range(used)
            ]
            + [ANY] * kept,
            out_specs=[FAR if place in far_out else VMEM for place in range(len(outs))],
            scratch_shapes=[pltpu.VMEM(shape, F32) for shape in scratch]
            + [pltpu.SemaphoreType.DMA((sems,) if sems > 1 else ())] * (sems > 0),
            compiler_params=pltpu.CompilerParams(vmem_limit_bytes=mib << 20),
        )(*args, *keep)


def from_comps(values):
    return [values[0]] + [
        lax.ppermute(values[step], COMP, [(i, i ^ step) for i in range(4)]) for step in (1, 2, 3)
    ]


def flip(value, axis):
    return lax.ppermute(value, axis, [(0, 1), (1, 0)])


def gather_comps(value):
    across = flip(value, "l")
    return [value, flip(value, "k"), across, flip(across, "k")]


def from_axis(values, axis):
    size = len(values)
    got = {0: values[0]}
    for step in sorted(range(1, size), key=lambda step: min(step, size - step)):
        got[step] = lax.ppermute(values[step], axis, [(i, (i + step) % size) for i in range(size)])
    return [got[step] for step in range(size)]


def exchange(value, axes):
    return lax.all_to_all(value, axes, 0, 0, tiled=True)


def after(values, *others):
    if isinstance(values, (list, tuple)):
        return list(lax.optimization_barrier((tuple(values), others))[0])
    return lax.optimization_barrier((values, others))[0]


def body(density, observed, data_weight, layer_top):
    nx, ny, nh = (lax.axis_size(axis) for axis in DEPTH)
    nxy = nx * ny
    rows = NX // nxy
    part = rows // nh
    fx, ty = (jnp.asarray(table) for table in make_tables())
    bind = functools.partial
    program = Program()
    call = program.call

    near, across = flip(density[0], "k"), flip(density[0], "l")
    *tables, dens, decay, gx, gy = call(
        prepare_kernel,
        [fx, fx, ty, (QX, NY), (KEPT, NY), (KEPT, NY), (KEPT, NY)],
        layer_top, fx, ty, density, scalars=(0,),
    )
    layers = [near, across, flip(after(across, dens), "k")]
    factors = (decay, gx, gy)
    weight_own, obs_own = data_weight[0], observed[0]
    program.hold(*tables, *factors, dens)
    message, full = call(
        bind(start_kernel, nxy), [(nxy, 2 * rows + 8, NY), (NX, NY)],
        dens, *layers, layer_top, *factors, *tables,
        scratch=[(NX, NY)] * 2, scalars=(4,), far_out=(1,), sems=1,
    )
    got = exchange(message, XY)
    (sums,) = call(
        bind(collect_kernel, nxy), [(2 * rows + nxy // 2 + 2 * part, NY)], got, weight_own, obs_own
    )
    sums = from_axis([sums] * nh, "h")
    pred, pulled, weight, tops, message = call(
        bind(residual_kernel, nxy, nh),
        [(rows, NY), (rows, NY), (rows, NY), (nxy * nh // 2, NY), (nxy, rows, NY)],
        *sums, scratch=[(rows, NY)] * 2, far_out=(4,), sems=nxy,
    )
    program.hold(pred, pulled, weight)
    got = exchange(message, XY)
    (power,) = call(bind(power_kernel, nxy * nh), [(KEPT, NY)], tops)
    program.hold(power)
    adjoint = lambda plane: call(
        bind(adjoint_kernel, nxy), [(2 * (QX + rows), NY)] * 2,
        plane.reshape(NX, NY), *factors, power, *tables,
        scratch=[(NX, NY), (4 * rows, NY)],
    )

    def reduce_comps(own, other):
        near, far = call(pair_kernel, [(QX + rows, NY)] * 2, own, flip(other, "k"))
        return near, flip(far, "l")

    pieces = reduce_comps(*adjoint(got))
    message, grad, line, image = call(
        bind(gradient_kernel, nxy, nh),
        [(nxy, rows + 8, NY), (QX, NY), (rows, NY), (rows, NY)],
        *pieces, pulled, dens, weight,
        scratch=[(rows, NY), (rows + 8, NY)], far_out=(0,), sems=nxy,
    )
    program.drop(pulled)
    program.hold(line, image)
    grads = gather_comps(grad)
    got = after(exchange(message, XY), *grads)
    plane, shares = call(bind(part_kernel, nxy), [(NX, NY), (8, NY)], got)
    pieces = adjoint(plane)
    shares = after(from_axis([shares] * nh, "h"), *pieces)
    (shares,) = call(add_kernel, [(8, NY)], *shares)
    shares = from_comps([shares] * 4)
    message, dens, base, alpha = call(
        second_kernel, [(nxy, rows, NY), (QX, NY), (QX, NY), (8, 128)],
        *shares, dens, full, *grads, *factors, *tables, scratch=[(NX, NY)],
    )
    program.alive = [weight, pred, line, image, dens, base, alpha]
    got = exchange(message, XY)
    pieces = reduce_comps(*after(pieces, message))
    grad2, image2, half = call(
        second_gradient_kernel, [(QX, NY), (rows, NY), (8, NY)],
        *pieces, alpha, base, dens, line,
    )
    (parts,) = call(bind(sum_kernel, nxy), [(rows + 8, NY)], got, half)
    program.alive = [pred, image, dens, alpha, grad2]
    shares, image2 = call(
        bind(curvature_kernel, nh, part), [(nxy * 4, 128), (part, NY)],
        *from_axis([parts] * nh, "h"), image2, weight, scratch=[(rows, NY)],
    )
    shares = exchange(shares, (*XY, *COMP))
    program.alive = []
    return tuple(
        call(
            finish_kernel, [density.shape, observed.shape],
            shares, dens, grad2, alpha, pred, image, image2, obs_own, weight_own,
        )
    )


def solution(mesh):
    depth = mesh.shape["depth"]
    sizes = {64: (4, 4, 4), 4: (2, 1, 2)}[depth]
    fine = Mesh(mesh.devices.reshape(*sizes, 2, 2), ALL)
    data = P(COMP, DEPTH, None)
    layer = P(DEPTH, COMP, None)
    return jax.shard_map(
        body,
        mesh=fine,
        in_specs=(layer, data, data, P(DEPTH)),
        out_specs=(layer, data),
        check_vma=False,
    )
```

```python
import functools
import math

import jax
import jax.numpy as jnp
import numpy as np
from jax import lax
from jax.experimental import pallas as pl
from jax.experimental.pallas import tpu as pltpu
from jax.sharding import Mesh
from jax.sharding import PartitionSpec as P

TWO_PI = 2.0 * math.pi
F32 = jnp.float32
BF16 = jnp.bfloat16
XY = ("x", "y")
DEPTH = ("x", "y", "h")
COMP = ("l", "k")
ALL = ("x", "y", "h", "l", "k")

NX = 512
NY = 256
HX = NX // 2
QX = NX // 4
HY = NY // 2


def split_table(table):
    high = table.astype(jnp.bfloat16)
    low = (table - high.astype(np.float64)).astype(jnp.bfloat16)
    return np.stack([high, low])


def basis(count, waves):
    place = np.arange(count)
    rows = []
    for wave in waves:
        norm = math.sqrt((1.0 if wave == 0 else 2.0) / count)
        rows.append(norm * np.cos(TWO_PI * (wave * place % count) / count))
    for wave in waves:
        if wave == 0:
            rows.append(math.sqrt(1.0 / count) * (1.0 - 2.0 * (place % 2)))
        else:
            rows.append(math.sqrt(2.0 / count) * np.sin(TWO_PI * (wave * place % count) / count))
    return np.stack(rows)


def make_tables():
    even = basis(NX, range(0, HX, 2))[:, :HX]
    odd = basis(NX, range(1, HX, 2))[:, :HX]
    col = basis(NY, range(HY))
    return (
        np.concatenate([split_table(even), split_table(odd)]),
        split_table(col.T),
    )


def split(value):
    high = value.astype(BF16)
    low = (value - high.astype(F32)).astype(BF16)
    return high, low


def dot(left, right):
    return jnp.dot(left, right, preferred_element_type=F32)


def dot_turned(left, right):
    return lax.dot_general(left, right, (((1,), (1,)), ((), ())), preferred_element_type=F32)


def times_table(value, high, low):
    vh, vl = split(value)
    return dot(vh, high) + (dot(vl, high) + dot(vh, low))


def times_turned(value, high, low):
    vh, vl = split(value)
    return dot_turned(vh, high) + (dot_turned(vl, high) + dot_turned(vh, low))


def table_times(high, low, value):
    vh, vl = split(value)
    return dot(high, vh) + (dot(high, vl) + dot(low, vh))


def to_waves(field, fx, ty):
    cols = times_table(field, ty[0], ty[1])
    upper, lower = cols[:HX], cols[HX:]
    return (
        table_times(fx[0], fx[1], upper + lower),
        table_times(fx[2], fx[3], upper - lower),
    )


def from_waves(even, odd, bx, ty):
    first = table_times(bx[0], bx[1], even)
    second = table_times(bx[2], bx[3], odd)
    rows = jnp.concatenate([first + second, first - second], axis=0)
    return times_turned(rows, ty[0], ty[1])


def swap_x(half):
    return jnp.concatenate([half[HX // 2 :], half[: HX // 2]], axis=0)


def swap_y(half):
    return jnp.concatenate([half[:, HY:], half[:, :HY]], axis=1)


def sines(cosines, nyquist):
    row = lax.broadcasted_iota(jnp.int32, cosines.shape, 0)
    return jnp.where(row == 0, nyquist, cosines)


def spread(ref):
    even, odd = ref[:QX], ref[QX:HX]
    return (
        jnp.concatenate([even, sines(even, ref[HX : HX + 1])], axis=0),
        jnp.concatenate([odd, odd], axis=0),
    )


def x_factors(gx_ref):
    even, odd = gx_ref[:QX], gx_ref[QX:HX]
    return jnp.concatenate([even, -even], axis=0), jnp.concatenate([odd, -odd], axis=0)


def xx_factors(gx_ref):
    even, odd = spread(gx_ref)
    return -(even * even), -(odd * odd)


def component(even, odd, gx_ref, gy_ref, comp):
    halves = []
    for half, first, second, third in zip(
        (even, odd), x_factors(gx_ref), spread(gy_ref), xx_factors(gx_ref)
    ):
        met = jnp.where(comp == 1, swap_x(half), jnp.where(comp == 2, swap_y(half), half))
        factor = jnp.where(comp == 1, first, jnp.where(comp == 2, second, third))
        halves.append(met * jnp.where(comp == 0, 1.0, factor))
    return halves


def comp_index():
    return lax.axis_index("l") * 2 + lax.axis_index("k")


KEPT = HX + 8


def wave_grid():
    row = lax.broadcasted_iota(jnp.int32, (KEPT, NY), 0)
    col = lax.broadcasted_iota(jnp.int32, (KEPT, NY), 1)
    wave_x = jnp.where(row >= HX, HX, 2 * (row % QX) + (row >= QX).astype(jnp.int32))
    nyquist_y = col == HY
    wave_y = jnp.where(nyquist_y, HY, col % HY)
    kx = wave_x.astype(F32) * (TWO_PI / NX)
    ky = wave_y.astype(F32) * (TWO_PI / NY)
    return kx, ky, col >= HY, nyquist_y


def prepare_kernel(
    top_ref, fx_in, ty_in, dens_in, fx, bx, ty, dens_ref, decay_ref, gx_ref, gy_ref
):
    dens_ref[...] = dens_in[0]
    for place in range(4):
        table = fx_in[place]
        fx[place] = table
        bx[place] = table.astype(F32).T.astype(BF16)
    for place in range(2):
        ty[place] = ty_in[place]
    kx, ky, sine_y, nyquist_y = wave_grid()
    kabs = jnp.sqrt(kx * kx + ky * ky)
    inverse = 1.0 / jnp.maximum(kabs, TWO_PI / max(NX, NY))
    decay_ref[...] = 4.0 * jnp.exp(-kabs * top_ref[0]) * (1.0 - jnp.exp(-kabs))
    gx_ref[...] = kx * inverse
    ry = ky * inverse
    gy_ref[...] = jnp.where(nyquist_y, 0.0, jnp.where(sine_y, -ry, ry))


def gather_rows(pieces, full_ref):
    comp = comp_index()
    for step, piece in enumerate(pieces):
        full_ref[pl.ds(pl.multiple_of(jnp.bitwise_xor(comp, step) * QX, QX), QX), :] = piece[...]


def forward_plane(field, decay_ref, gx_ref, gy_ref, fx, bx, ty):
    even, odd = to_waves(field, fx, ty)
    decay = spread(decay_ref)
    even, odd = component(even * decay[0], odd * decay[1], gx_ref, gy_ref, comp_index())
    return from_waves(even, odd, bx, ty)


def start_kernel(
    nxy, m0, m1, m2, m3, top_ref, decay_ref, gx_ref, gy_ref, fx, bx, ty, out_ref, far_ref, full_ref, pull_ref, sem
):
    rows = NX // nxy
    gather_rows((m0, m1, m2, m3), full_ref)
    copy = pltpu.make_async_copy(full_ref, far_ref, sem)
    copy.start()
    dens = full_ref[...]
    pull_ref[...] = 0.5 * (dens * (1.0 / (dens * dens + 0.25)))
    for place, field in enumerate((full_ref, pull_ref)):
        plane = forward_plane(field[...], decay_ref, gx_ref, gy_ref, fx, bx, ty)
        for target in range(nxy):
            out_ref[target, place * rows : (place + 1) * rows, :] = plane[
                target * rows : (target + 1) * rows
            ]
    for target in range(nxy):
        out_ref[target, 2 * rows : 2 * rows + 8, :] = jnp.full((8, NY), top_ref[0], F32)
    copy.wait()


def collect_kernel(nxy, got_ref, weight_ref, obs_ref, sum_ref):
    rows = NX // nxy
    total = got_ref[0, : 2 * rows, :]
    for source in range(1, nxy):
        total = total + got_ref[source, : 2 * rows, :]
    sum_ref[: 2 * rows] = total
    part = weight_ref.shape[0]
    place = pl.ds(pl.multiple_of(lax.axis_index("h") * part, part), part)
    sum_ref[place, :] = sum_ref[place, :] - obs_ref[...]
    left = lax.broadcasted_iota(jnp.int32, (1, NY), 1) < HY
    for pair in range(nxy // 2):
        first, second = (got_ref[2 * pair + i, 2 * rows : 2 * rows + 1, :] for i in (0, 1))
        sum_ref[2 * rows + pair : 2 * rows + pair + 1, :] = jnp.where(left, first, second)
    sum_ref[2 * rows + nxy // 2 :] = weight_ref[...]


def send_all(block_ref, far_ref, sems):
    copies = [
        pltpu.make_async_copy(block_ref, far_ref.at[place], sems.at[place])
        for place in range(far_ref.shape[0])
    ]
    for copy in copies:
        copy.start()
    return copies


def residual_kernel(nxy, nh, *refs):
    rows = NX // nxy
    part = rows // nh
    pairs = nxy // 2
    start = 2 * rows + pairs
    sums = refs[:nh]
    error_ref, pull_ref, weight_ref, tops_ref, far_ref, block_ref, sems = refs[nh:]
    chip = lax.axis_index("h")
    total = sums[0][: 2 * rows]
    for step in range(1, nh):
        total = total + sums[step][: 2 * rows]
    for step in range(nh):
        tops_ref[step * pairs : (step + 1) * pairs] = sums[step][2 * rows : start]
        place = pl.ds(pl.multiple_of(lax.rem(chip + (nh - step), nh) * part, part), part)
        weight_ref[place, :] = sums[step][start:]
    weight = weight_ref[...]
    error = total[:rows]
    block_ref[...] = weight * (weight * error)
    copies = send_all(block_ref, far_ref, sems)
    error_ref[...] = error
    pull_ref[...] = total[rows:]
    for copy in copies:
        copy.wait()


def power_kernel(layers, tops_ref, power_ref):
    kx, ky, *_ = wave_grid()
    for start in range(0, KEPT, 64):
        stop = min(start + 64, KEPT)
        ks = jnp.sqrt(kx[start:stop] ** 2 + ky[start:stop] ** 2)
        double = -2.0 * ks

        def add(step, total):
            for pair in range(2):
                tops = tops_ref[pl.ds(2 * step + pair, 1), :]
                for top in (tops[:, :HY], tops[:, HY:]):
                    total = total + jnp.exp(double * jnp.concatenate([top, top], axis=1))
            return total

        total = lax.fori_loop(0, layers // 4, add, jnp.zeros_like(ks))
        rise = 1.0 - jnp.exp(-ks)
        power_ref[start:stop] = (16.0 * (rise * rise)) * total


def adjoint_kernel(
    nxy, res_ref, decay_ref, gx_ref, gy_ref, power_ref, fx, bx, ty, own_out, other_out, z_ref, i_ref
):
    rows = NX // nxy
    comp = comp_index()
    even, odd = to_waves(res_ref[...], fx, ty)
    even, odd = component(even, odd, gx_ref, gy_ref, comp)
    sign = jnp.where((comp == 1) | (comp == 2), -1.0, 1.0)
    even = even * sign
    odd = odd * sign
    decay = spread(decay_ref)
    z_ref[...] = from_waves(even * decay[0], odd * decay[1], bx, ty)
    power = spread(power_ref)
    even = even * power[0]
    odd = odd * power[1]
    block = lax.axis_index("x") * lax.axis_size("y") + lax.axis_index("y")
    upper = block * rows < HX
    near = pl.ds(pl.multiple_of(lax.rem(block * rows, HX), rows), rows)
    flip = jnp.where(upper, 1.0, -1.0)
    for target in range(4):
        if target == 0:
            e, o = even, odd
        elif target == 1:
            first = x_factors(gx_ref)
            e, o = swap_x(even) * first[0], swap_x(odd) * first[1]
        elif target == 2:
            second = spread(gy_ref)
            e, o = swap_y(even) * second[0], swap_y(odd) * second[1]
        else:
            third = xx_factors(gx_ref)
            e, o = even * third[0], odd * third[1]
        line = table_times(bx[0, near, :], bx[1, near, :], e)
        line = line + flip * table_times(bx[2, near, :], bx[3, near, :], o)
        i_ref[target * rows : (target + 1) * rows, :] = line
    i_ref[...] = times_turned(i_ref[...], ty[0], ty[1])
    for step in range(4):
        out = (own_out, other_out)[step % 2]
        begin = (step // 2) * (QX + rows)
        other = jnp.bitwise_xor(comp, step)
        out[begin : begin + QX] = z_ref[pl.ds(pl.multiple_of(other * QX, QX), QX), :]
        out[begin + QX : begin + QX + rows] = i_ref[
            pl.ds(pl.multiple_of(other * rows, rows), rows), :
        ]


def pair_kernel(own_ref, got_ref, near_ref, far_ref):
    half = near_ref.shape[0]
    near_ref[...] = own_ref[:half] + got_ref[:half]
    far_ref[...] = own_ref[half:] + got_ref[half:]


def share(grad, quad, image, weight, scratch, part):
    scratch[...] = weight * image
    place = pl.ds(pl.multiple_of(lax.axis_index("h") * part, part), part)
    mine = scratch[place, :]
    lane = lax.broadcasted_iota(jnp.int32, (1, NY), 1)
    square = grad * grad
    gg = jnp.sum(square)
    qgg = jnp.sum(quad * square)
    curv = jnp.sum(mine * mine)
    return jnp.where(lane == 0, gg, jnp.where(lane == 1, qgg, jnp.where(lane == 2, curv, 0.0)))


def step_length(shares):
    total = jnp.sum(shares, axis=0, keepdims=True)
    lane = lax.broadcasted_iota(jnp.int32, total.shape, 1)
    pick = lambda place: jnp.sum(jnp.where(lane == place, total, 0.0), keepdims=True)
    return pick(0) / (pick(2) + 0.5 * pick(1))


def gradient_kernel(nxy, nh, *refs):
    rows = NX // nxy
    part = rows // nh
    pieces = refs[:2]
    pull_ref, dens_ref, weight_ref = refs[2:5]
    far_ref, grad_ref, line_ref, image_ref, scratch, block_ref, sems = refs[5:]
    total = pieces[0][...] + pieces[1][...]
    data = total[:QX]
    line = total[QX:]
    dens = dens_ref[...]
    quad = 1.0 / (dens * dens + 0.25)
    grad = data + 0.5 * (quad * dens)
    image = line + pull_ref[...]
    weight = weight_ref[...]
    block_ref[:rows] = weight * (weight * image)
    block_ref[rows:] = jnp.broadcast_to(share(grad, quad, image, weight, scratch, part), (8, NY))
    copies = send_all(block_ref, far_ref, sems)
    grad_ref[...] = grad
    line_ref[...] = line
    image_ref[...] = image
    for copy in copies:
        copy.wait()


def part_kernel(nxy, got_ref, plane_ref, share_ref):
    rows = NX // nxy
    total = got_ref[0, rows:, :]
    for source in range(1, nxy):
        total = total + got_ref[source, rows:, :]
    share_ref[...] = total
    for source in range(nxy):
        plane_ref[source * rows : (source + 1) * rows] = got_ref[source, :rows, :]


def add_kernel(*refs):
    total = refs[0][...]
    for part in refs[1:-1]:
        total = total + part[...]
    refs[-1][...] = total


def second_kernel(
    s0, s1, s2, s3, dens_ref, full_ref, g0, g1, g2, g3, decay_ref, gx_ref, gy_ref, fx, bx, ty,
    out_ref, dens_out, base_out, alpha_ref, all_ref,
):
    gather_rows((g0, g1, g2, g3), all_ref)
    alpha = step_length(s0[:1] + s1[:1] + (s2[:1] + s3[:1]))
    alpha_ref[...] = jnp.broadcast_to(alpha, alpha_ref.shape)
    old = dens_ref[...]
    grad = g0[...]
    dens = old - alpha * grad
    dens_out[...] = dens
    data = grad - 0.5 * ((1.0 / (old * old + 0.25)) * old)
    base_out[...] = data + 0.5 * (dens * (1.0 / (dens * dens + 0.25)))
    dens = full_ref[...] - alpha * all_ref[...]
    all_ref[...] = 0.5 * (dens * (1.0 / (dens * dens + 0.25)))
    plane = forward_plane(all_ref[...], decay_ref, gx_ref, gy_ref, fx, bx, ty)
    out_ref[...] = plane.reshape(out_ref.shape)


def sum_kernel(nxy, got_ref, half_ref, sum_ref):
    rows = NX // nxy
    total = got_ref[0]
    for source in range(1, nxy):
        total = total + got_ref[source]
    sum_ref[:rows] = total
    sum_ref[rows:] = half_ref[...]


def second_gradient_kernel(
    u0, u1, alpha_ref, base_ref, dens_ref, line_ref, grad_ref, image_ref, share_ref
):
    alpha = alpha_ref[:1, :1]
    total = u0[...] + u1[...]
    dens = dens_ref[...]
    grad = base_ref[...] - alpha * total[:QX]
    quad = 1.0 / (dens * dens + 0.25)
    grad_ref[...] = grad
    image_ref[...] = line_ref[...] - alpha * total[QX:]
    square = grad * grad
    lane = lax.broadcasted_iota(jnp.int32, (8, NY), 1)
    share_ref[...] = jnp.where(
        lane == 0, jnp.sum(square), jnp.where(lane == 1, jnp.sum(quad * square), 0.0)
    )


def curvature_kernel(nh, part, *refs):
    parts = refs[:nh]
    image_ref, weight_ref, share_ref, out_ref, scratch = refs[nh:]
    rows = image_ref.shape[0]
    total = parts[0][...]
    for piece in parts[1:]:
        total = total + piece[...]
    image = image_ref[...] + total[:rows]
    scratch[...] = image
    out_ref[...] = scratch[pl.ds(pl.multiple_of(lax.axis_index("h") * part, part), part), :]
    mine = weight_ref[...] * image
    lane = lax.broadcasted_iota(jnp.int32, (1, 128), 1)
    share_ref[...] = jnp.broadcast_to(
        jnp.where(lane == 2, jnp.sum(mine * mine), total[rows : rows + 1, :128]), share_ref.shape
    )


def finish_kernel(
    shares_ref, dens_ref, grad_ref, alpha_ref, error_ref, first_ref, second_ref, w_ref, dens_out, err_out
):
    part = w_ref.shape[0]
    alpha = step_length(shares_ref[...])
    dens_out[0] = dens_ref[...] - alpha * grad_ref[...]
    place = pl.ds(pl.multiple_of(lax.axis_index("h") * part, part), part)
    error = error_ref[place, :] - alpha_ref[:1, :1] * first_ref[place, :]
    err_out[0] = w_ref[...] * (error - alpha * second_ref[...])


VMEM = pl.BlockSpec(memory_space=pltpu.VMEM)
SMEM = pl.BlockSpec(memory_space=pltpu.SMEM)
ANY = pl.BlockSpec(memory_space=pl.ANY)
FAR = pl.BlockSpec(memory_space=pltpu.HBM)


class Program:
    def __init__(self):
        self.alive = []

    def hold(self, *values):
        self.alive += values

    def drop(self, *values):
        self.alive = [item for item in self.alive if all(item is not value for value in values)]

    def call(self, kernel, outs, *args, scratch=(), scalars=(), far_out=(), sems=0, mib=8):
        used = len(args)
        keep = [item for item in self.alive if all(item is not value for value in args)]
        kept = len(keep)

        def inner(*refs):
            kernel(*refs[:used], *refs[used + kept :])

        kinds = [(item, F32) if isinstance(item, tuple) else (item.shape, item.dtype) for item in outs]
        return pl.pallas_call(
            inner,
            out_shape=[
                (pltpu.HBM if place in far_out else jax.ShapeDtypeStruct)(*kind)
                for place, kind in enumerate(kinds)
            ],
            in_specs=[
                SMEM if place in scalars else VMEM for place in range(used)
            ]
            + [ANY] * kept,
            out_specs=[FAR if place in far_out else VMEM for place in range(len(outs))],
            scratch_shapes=[pltpu.VMEM(shape, F32) for shape in scratch]
            + [pltpu.SemaphoreType.DMA((sems,) if sems > 1 else ())] * (sems > 0),
            compiler_params=pltpu.CompilerParams(vmem_limit_bytes=mib << 20),
        )(*args, *keep)


def from_comps(values):
    return [values[0]] + [
        lax.ppermute(values[step], COMP, [(i, i ^ step) for i in range(4)]) for step in (1, 2, 3)
    ]


def flip(value, axis):
    return lax.ppermute(value, axis, [(0, 1), (1, 0)])


def gather_comps(value):
    across = flip(value, "l")
    return [value, flip(value, "k"), across, flip(across, "k")]


def from_axis(values, axis):
    size = len(values)
    got = {0: values[0]}
    for step in sorted(range(1, size), key=lambda step: min(step, size - step)):
        got[step] = lax.ppermute(values[step], axis, [(i, (i + step) % size) for i in range(size)])
    return [got[step] for step in range(size)]


def exchange(value, axes):
    return lax.all_to_all(value, axes, 0, 0, tiled=True)


def after(values, *others):
    if isinstance(values, (list, tuple)):
        return list(lax.optimization_barrier((tuple(values), others))[0])
    return lax.optimization_barrier((values, others))[0]


def body(density, observed, data_weight, layer_top):
    nx, ny, nh = (lax.axis_size(axis) for axis in DEPTH)
    nxy = nx * ny
    rows = NX // nxy
    part = rows // nh
    fx, ty = (jnp.asarray(table) for table in make_tables())
    bind = functools.partial
    program = Program()
    call = program.call

    near, across = flip(density[0], "k"), flip(density[0], "l")
    *tables, dens, decay, gx, gy = call(
        prepare_kernel,
        [fx, fx, ty, (QX, NY), (KEPT, NY), (KEPT, NY), (KEPT, NY)],
        layer_top, fx, ty, density, scalars=(0,),
    )
    layers = [near, across, flip(after(across, dens), "k")]
    factors = (decay, gx, gy)
    weight_own, obs_own = data_weight[0], observed[0]
    program.hold(*tables, *factors, dens)
    message, full = call(
        bind(start_kernel, nxy), [(nxy, 2 * rows + 8, NY), (NX, NY)],
        dens, *layers, layer_top, *factors, *tables,
        scratch=[(NX, NY)] * 2, scalars=(4,), far_out=(1,), sems=1,
    )
    got = exchange(message, XY)
    (sums,) = call(
        bind(collect_kernel, nxy), [(2 * rows + nxy // 2 + part, NY)], got, weight_own, obs_own
    )
    sums = from_axis([sums] * nh, "h")
    error, pulled, weight, tops, message = call(
        bind(residual_kernel, nxy, nh),
        [(rows, NY), (rows, NY), (rows, NY), (nxy * nh // 2, NY), (nxy, rows, NY)],
        *sums, scratch=[(rows, NY)], far_out=(4,), sems=nxy,
    )
    program.hold(error, pulled, weight)
    got = exchange(message, XY)
    (power,) = call(bind(power_kernel, nxy * nh), [(KEPT, NY)], tops)
    program.hold(power)
    adjoint = lambda plane: call(
        bind(adjoint_kernel, nxy), [(2 * (QX + rows), NY)] * 2,
        plane.reshape(NX, NY), *factors, power, *tables,
        scratch=[(NX, NY), (4 * rows, NY)],
    )

    def reduce_comps(own, other):
        near, far = call(pair_kernel, [(QX + rows, NY)] * 2, own, flip(other, "k"))
        return near, flip(far, "l")

    pieces = reduce_comps(*adjoint(got))
    message, grad, line, image = call(
        bind(gradient_kernel, nxy, nh),
        [(nxy, rows + 8, NY), (QX, NY), (rows, NY), (rows, NY)],
        *pieces, pulled, dens, weight,
        scratch=[(rows, NY), (rows + 8, NY)], far_out=(0,), sems=nxy,
    )
    program.drop(pulled)
    program.hold(line, image)
    grads = gather_comps(grad)
    got = after(exchange(message, XY), *grads)
    plane, shares = call(bind(part_kernel, nxy), [(NX, NY), (8, NY)], got)
    pieces = adjoint(plane)
    shares = after(from_axis([shares] * nh, "h"), *pieces)
    (shares,) = call(add_kernel, [(8, NY)], *shares)
    shares = from_comps([shares] * 4)
    message, dens, base, alpha = call(
        second_kernel, [(nxy, rows, NY), (QX, NY), (QX, NY), (8, 128)],
        *shares, dens, full, *grads, *factors, *tables, scratch=[(NX, NY)],
    )
    program.alive = [weight, error, line, image, dens, base, alpha]
    got = exchange(message, XY)
    pieces = reduce_comps(*after(pieces, message))
    grad2, image2, half = call(
        second_gradient_kernel, [(QX, NY), (rows, NY), (8, NY)],
        *pieces, alpha, base, dens, line,
    )
    (parts,) = call(bind(sum_kernel, nxy), [(rows + 8, NY)], got, half)
    program.alive = [error, image, dens, alpha, grad2]
    shares, image2 = call(
        bind(curvature_kernel, nh, part), [(nxy * 4, 128), (part, NY)],
        *from_axis([parts] * nh, "h"), image2, weight, scratch=[(rows, NY)],
    )
    shares = exchange(shares, (*XY, *COMP))
    program.alive = []
    return tuple(
        call(
            finish_kernel, [density.shape, observed.shape],
            shares, dens, grad2, alpha, error, image, image2, weight_own,
        )
    )


def solution(mesh):
    depth = mesh.shape["depth"]
    sizes = {64: (4, 4, 4), 4: (2, 1, 2)}[depth]
    fine = Mesh(mesh.devices.reshape(*sizes, 2, 2), ALL)
    data = P(COMP, DEPTH, None)
    layer = P(DEPTH, COMP, None)
    return jax.shard_map(
        body,
        mesh=fine,
        in_specs=(layer, data, data, P(DEPTH)),
        out_specs=(layer, data),
        check_vma=False,
    )
```

```python
import functools
import math

import jax
import jax.numpy as jnp
import numpy as np
from jax import lax
from jax.experimental import pallas as pl
from jax.experimental.pallas import tpu as pltpu
from jax.sharding import Mesh
from jax.sharding import PartitionSpec as P

TWO_PI = 2.0 * math.pi
F32 = jnp.float32
BF16 = jnp.bfloat16
XY = ("x", "y")
DEPTH = ("x", "y", "h")
COMP = ("l", "k")
ALL = ("x", "y", "h", "l", "k")

NX = 512
NY = 256
HX = NX // 2
QX = NX // 4
HY = NY // 2


def split_table(table):
    high = table.astype(jnp.bfloat16)
    low = (table - high.astype(np.float64)).astype(jnp.bfloat16)
    return np.stack([high, low])


def basis(count, waves):
    place = np.arange(count)
    rows = []
    for wave in waves:
        norm = math.sqrt((1.0 if wave == 0 else 2.0) / count)
        rows.append(norm * np.cos(TWO_PI * (wave * place % count) / count))
    for wave in waves:
        if wave == 0:
            rows.append(math.sqrt(1.0 / count) * (1.0 - 2.0 * (place % 2)))
        else:
            rows.append(math.sqrt(2.0 / count) * np.sin(TWO_PI * (wave * place % count) / count))
    return np.stack(rows)


def make_tables():
    even = basis(NX, range(0, HX, 2))[:, :HX]
    odd = basis(NX, range(1, HX, 2))[:, :HX]
    col = basis(NY, range(HY))
    return (
        np.concatenate([split_table(even), split_table(odd)]),
        split_table(col.T),
    )


def split(value):
    high = value.astype(BF16)
    low = (value - high.astype(F32)).astype(BF16)
    return high, low


def dot(left, right):
    return jnp.dot(left, right, preferred_element_type=F32)


def dot_turned(left, right):
    return lax.dot_general(left, right, (((1,), (1,)), ((), ())), preferred_element_type=F32)


def times_table(value, high, low):
    vh, vl = split(value)
    return dot(vh, high) + (dot(vl, high) + dot(vh, low))


def times_turned(value, high, low):
    vh, vl = split(value)
    return dot_turned(vh, high) + (dot_turned(vl, high) + dot_turned(vh, low))


def table_times(high, low, value):
    vh, vl = split(value)
    return dot(high, vh) + (dot(high, vl) + dot(low, vh))


def to_waves(field, fx, ty):
    cols = times_table(field, ty[0], ty[1])
    upper, lower = cols[:HX], cols[HX:]
    return (
        table_times(fx[0], fx[1], upper + lower),
        table_times(fx[2], fx[3], upper - lower),
    )


def from_waves(even, odd, bx, ty):
    first = table_times(bx[0], bx[1], even)
    second = table_times(bx[2], bx[3], odd)
    rows = jnp.concatenate([first + second, first - second], axis=0)
    return times_turned(rows, ty[0], ty[1])


def swap_x(half):
    return jnp.concatenate([half[HX // 2 :], half[: HX // 2]], axis=0)


def swap_y(half):
    return jnp.concatenate([half[:, HY:], half[:, :HY]], axis=1)


def sines(cosines, nyquist):
    row = lax.broadcasted_iota(jnp.int32, cosines.shape, 0)
    return jnp.where(row == 0, nyquist, cosines)


def spread(ref):
    even, odd = ref[:QX], ref[QX:HX]
    return (
        jnp.concatenate([even, sines(even, ref[HX : HX + 1])], axis=0),
        jnp.concatenate([odd, odd], axis=0),
    )


def x_factors(gx_ref):
    even, odd = gx_ref[:QX], gx_ref[QX:HX]
    return jnp.concatenate([even, -even], axis=0), jnp.concatenate([odd, -odd], axis=0)


def xx_factors(gx_ref):
    even, odd = spread(gx_ref)
    return -(even * even), -(odd * odd)


def component(even, odd, gx_ref, gy_ref, comp):
    halves = []
    for half, first, second, third in zip(
        (even, odd), x_factors(gx_ref), spread(gy_ref), xx_factors(gx_ref)
    ):
        met = jnp.where(comp == 1, swap_x(half), jnp.where(comp == 2, swap_y(half), half))
        factor = jnp.where(comp == 1, first, jnp.where(comp == 2, second, third))
        halves.append(met * jnp.where(comp == 0, 1.0, factor))
    return halves


def comp_index():
    return lax.axis_index("l") * 2 + lax.axis_index("k")


KEPT = HX + 8


def wave_grid():
    row = lax.broadcasted_iota(jnp.int32, (KEPT, NY), 0)
    col = lax.broadcasted_iota(jnp.int32, (KEPT, NY), 1)
    wave_x = jnp.where(row >= HX, HX, 2 * (row % QX) + (row >= QX).astype(jnp.int32))
    nyquist_y = col == HY
    wave_y = jnp.where(nyquist_y, HY, col % HY)
    kx = wave_x.astype(F32) * (TWO_PI / NX)
    ky = wave_y.astype(F32) * (TWO_PI / NY)
    return kx, ky, col >= HY, nyquist_y


def prepare_kernel(
    top_ref, fx_in, ty_in, dens_in, fx, bx, ty, dens_ref, decay_ref, gx_ref, gy_ref
):
    dens_ref[...] = dens_in[0]
    for place in range(4):
        table = fx_in[place]
        fx[place] = table
        bx[place] = table.astype(F32).T.astype(BF16)
    for place in range(2):
        ty[place] = ty_in[place]
    kx, ky, sine_y, nyquist_y = wave_grid()
    kabs = jnp.sqrt(kx * kx + ky * ky)
    inverse = 1.0 / jnp.maximum(kabs, TWO_PI / max(NX, NY))
    decay_ref[...] = 4.0 * jnp.exp(-kabs * top_ref[0]) * (1.0 - jnp.exp(-kabs))
    gx_ref[...] = kx * inverse
    ry = ky * inverse
    gy_ref[...] = jnp.where(nyquist_y, 0.0, jnp.where(sine_y, -ry, ry))


def gather_rows(pieces, full_ref):
    comp = comp_index()
    for step, piece in enumerate(pieces):
        full_ref[pl.ds(pl.multiple_of(jnp.bitwise_xor(comp, step) * QX, QX), QX), :] = piece[...]


def forward_plane(field, decay_ref, gx_ref, gy_ref, fx, bx, ty):
    even, odd = to_waves(field, fx, ty)
    decay = spread(decay_ref)
    even, odd = component(even * decay[0], odd * decay[1], gx_ref, gy_ref, comp_index())
    return from_waves(even, odd, bx, ty)


def start_kernel(
    nxy, m0, m1, m2, m3, top_ref, decay_ref, gx_ref, gy_ref, fx, bx, ty, out_ref, far_ref, full_ref, pull_ref, sem
):
    rows = NX // nxy
    gather_rows((m0, m1, m2, m3), full_ref)
    copy = pltpu.make_async_copy(full_ref, far_ref, sem)
    copy.start()
    dens = full_ref[...]
    pull_ref[...] = 0.5 * (dens * (1.0 / (dens * dens + 0.25)))
    for place, field in enumerate((full_ref, pull_ref)):
        plane = forward_plane(field[...], decay_ref, gx_ref, gy_ref, fx, bx, ty)
        for target in range(nxy):
            out_ref[target, place * rows : (place + 1) * rows, :] = plane[
                target * rows : (target + 1) * rows
            ]
    for target in range(nxy):
        out_ref[target, 2 * rows : 2 * rows + 8, :] = jnp.full((8, NY), top_ref[0], F32)
    copy.wait()


def collect_kernel(nxy, got_ref, weight_ref, obs_ref, sum_ref):
    rows = NX // nxy
    total = got_ref[0, : 2 * rows, :]
    for source in range(1, nxy):
        total = total + got_ref[source, : 2 * rows, :]
    sum_ref[: 2 * rows] = total
    part = weight_ref.shape[0]
    place = pl.ds(pl.multiple_of(lax.axis_index("h") * part, part), part)
    sum_ref[place, :] = sum_ref[place, :] - obs_ref[...]
    left = lax.broadcasted_iota(jnp.int32, (1, NY), 1) < HY
    for pair in range(nxy // 2):
        first, second = (got_ref[2 * pair + i, 2 * rows : 2 * rows + 1, :] for i in (0, 1))
        sum_ref[2 * rows + pair : 2 * rows + pair + 1, :] = jnp.where(left, first, second)
    sum_ref[2 * rows + nxy // 2 :] = weight_ref[...]


def send_all(block_ref, far_ref, sems):
    copies = [
        pltpu.make_async_copy(block_ref, far_ref.at[place], sems.at[place])
        for place in range(far_ref.shape[0])
    ]
    for copy in copies:
        copy.start()
    return copies


def residual_kernel(nxy, nh, *refs):
    rows = NX // nxy
    part = rows // nh
    pairs = nxy // 2
    start = 2 * rows + pairs
    sums = refs[:nh]
    error_ref, pull_ref, weight_ref, tops_ref, far_ref, block_ref, sems = refs[nh:]
    chip = lax.axis_index("h")
    total = sums[0][: 2 * rows]
    for step in range(1, nh):
        total = total + sums[step][: 2 * rows]
    for step in range(nh):
        tops_ref[step * pairs : (step + 1) * pairs] = sums[step][2 * rows : start]
        place = pl.ds(pl.multiple_of(lax.rem(chip + (nh - step), nh) * part, part), part)
        weight_ref[place, :] = sums[step][start:]
    weight = weight_ref[...]
    error = total[:rows]
    block_ref[...] = weight * (weight * error)
    copies = send_all(block_ref, far_ref, sems)
    error_ref[...] = error
    pull_ref[...] = total[rows:]
    for copy in copies:
        copy.wait()


def power_kernel(layers, tops_ref, power_ref):
    kx, ky, *_ = wave_grid()
    for start in range(0, KEPT, 64):
        stop = min(start + 64, KEPT)
        ks = jnp.sqrt(kx[start:stop] ** 2 + ky[start:stop] ** 2)
        double = -2.0 * ks

        def add(step, total):
            for pair in range(2):
                tops = tops_ref[pl.ds(2 * step + pair, 1), :]
                for top in (tops[:, :HY], tops[:, HY:]):
                    total = total + jnp.exp(double * jnp.concatenate([top, top], axis=1))
            return total

        total = lax.fori_loop(0, layers // 4, add, jnp.zeros_like(ks))
        rise = 1.0 - jnp.exp(-ks)
        power_ref[start:stop] = (16.0 * (rise * rise)) * total


def adjoint_kernel(
    nxy, res_ref, decay_ref, gx_ref, gy_ref, power_ref, fx, bx, ty, own_out, other_out, z_ref, i_ref
):
    rows = NX // nxy
    comp = comp_index()
    even, odd = to_waves(res_ref[...], fx, ty)
    even, odd = component(even, odd, gx_ref, gy_ref, comp)
    sign = jnp.where((comp == 1) | (comp == 2), -1.0, 1.0)
    even = even * sign
    odd = odd * sign
    decay = spread(decay_ref)
    z_ref[...] = from_waves(even * decay[0], odd * decay[1], bx, ty)
    power = spread(power_ref)
    even = even * power[0]
    odd = odd * power[1]
    block = lax.axis_index("x") * lax.axis_size("y") + lax.axis_index("y")
    upper = block * rows < HX
    near = pl.ds(pl.multiple_of(lax.rem(block * rows, HX), rows), rows)
    flip = jnp.where(upper, 1.0, -1.0)
    for target in range(4):
        if target == 0:
            e, o = even, odd
        elif target == 1:
            first = x_factors(gx_ref)
            e, o = swap_x(even) * first[0], swap_x(odd) * first[1]
        elif target == 2:
            second = spread(gy_ref)
            e, o = swap_y(even) * second[0], swap_y(odd) * second[1]
        else:
            third = xx_factors(gx_ref)
            e, o = even * third[0], odd * third[1]
        line = table_times(bx[0, near, :], bx[1, near, :], e)
        line = line + flip * table_times(bx[2, near, :], bx[3, near, :], o)
        i_ref[target * rows : (target + 1) * rows, :] = line
    i_ref[...] = times_turned(i_ref[...], ty[0], ty[1])
    for step in range(4):
        out = (own_out, other_out)[step % 2]
        begin = (step // 2) * (QX + rows)
        other = jnp.bitwise_xor(comp, step)
        out[begin : begin + QX] = z_ref[pl.ds(pl.multiple_of(other * QX, QX), QX), :]
        out[begin + QX : begin + QX + rows] = i_ref[
            pl.ds(pl.multiple_of(other * rows, rows), rows), :
        ]


def pair_kernel(own_ref, got_ref, near_ref, far_ref):
    half = near_ref.shape[0]
    near_ref[...] = own_ref[:half] + got_ref[:half]
    far_ref[...] = own_ref[half:] + got_ref[half:]


def share(grad, quad, image, weight, scratch, part):
    scratch[...] = weight * image
    place = pl.ds(pl.multiple_of(lax.axis_index("h") * part, part), part)
    mine = scratch[place, :]
    lane = lax.broadcasted_iota(jnp.int32, (1, NY), 1)
    square = grad * grad
    gg = jnp.sum(square)
    qgg = jnp.sum(quad * square)
    curv = jnp.sum(mine * mine)
    return jnp.where(lane == 0, gg, jnp.where(lane == 1, qgg, jnp.where(lane == 2, curv, 0.0)))


def step_length(shares):
    total = jnp.sum(shares, axis=0, keepdims=True)
    lane = lax.broadcasted_iota(jnp.int32, total.shape, 1)
    pick = lambda place: jnp.sum(jnp.where(lane == place, total, 0.0), keepdims=True)
    return pick(0) / (pick(2) + 0.5 * pick(1))


def gradient_kernel(nxy, nh, *refs):
    rows = NX // nxy
    part = rows // nh
    pieces = refs[:2]
    pull_ref, dens_ref, weight_ref = refs[2:5]
    far_ref, grad_ref, line_ref, image_ref, scratch, block_ref, sems = refs[5:]
    total = pieces[0][...] + pieces[1][...]
    data = total[:QX]
    line = total[QX:]
    dens = dens_ref[...]
    quad = 1.0 / (dens * dens + 0.25)
    grad = data + 0.5 * (quad * dens)
    image = line + pull_ref[...]
    weight = weight_ref[...]
    block_ref[:rows] = weight * (weight * image)
    block_ref[rows:] = jnp.broadcast_to(share(grad, quad, image, weight, scratch, part), (8, NY))
    copies = send_all(block_ref, far_ref, sems)
    grad_ref[...] = grad
    line_ref[...] = line
    image_ref[...] = image
    for copy in copies:
        copy.wait()


def part_kernel(nxy, got_ref, plane_ref, share_ref):
    rows = NX // nxy
    total = got_ref[0, rows:, :]
    for source in range(1, nxy):
        total = total + got_ref[source, rows:, :]
    share_ref[...] = jnp.broadcast_to(total[:1, :128], share_ref.shape)
    for source in range(nxy):
        plane_ref[source * rows : (source + 1) * rows] = got_ref[source, :rows, :]


def second_kernel(
    shares_ref, dens_ref, full_ref, g0, g1, g2, g3, decay_ref, gx_ref, gy_ref, fx, bx, ty,
    out_ref, dens_out, base_out, alpha_ref, all_ref, near_ref, sems,
):
    comp = comp_index()
    copies = [pltpu.make_async_copy(full_ref, near_ref, sems.at[4])]
    for step, piece in enumerate((g0, g1, g2, g3)):
        place = pl.ds(pl.multiple_of(jnp.bitwise_xor(comp, step) * QX, QX), QX)
        copies.append(pltpu.make_async_copy(piece, all_ref.at[place, :], sems.at[step]))
    for copy in copies:
        copy.start()
    alpha = step_length(shares_ref[...])
    alpha_ref[...] = jnp.broadcast_to(alpha, alpha_ref.shape)
    old = dens_ref[...]
    for copy in copies:
        copy.wait()
    grad = all_ref[pl.ds(pl.multiple_of(comp * QX, QX), QX), :]
    dens = old - alpha * grad
    dens_out[...] = dens
    data = grad - 0.5 * ((1.0 / (old * old + 0.25)) * old)
    base_out[...] = data + 0.5 * (dens * (1.0 / (dens * dens + 0.25)))
    dens = near_ref[...] - alpha * all_ref[...]
    all_ref[...] = 0.5 * (dens * (1.0 / (dens * dens + 0.25)))
    plane = forward_plane(all_ref[...], decay_ref, gx_ref, gy_ref, fx, bx, ty)
    near_ref[...] = plane
    rows = out_ref.shape[1]
    copies = [
        pltpu.make_async_copy(near_ref.at[pl.ds(place * rows, rows), :], out_ref.at[place], sems.at[place])
        for place in range(out_ref.shape[0])
    ]
    for copy in copies:
        copy.start()
    for copy in copies:
        copy.wait()


def sum_kernel(nxy, got_ref, half_ref, sum_ref):
    rows = NX // nxy
    total = got_ref[0]
    for source in range(1, nxy):
        total = total + got_ref[source]
    sum_ref[:rows] = total
    sum_ref[rows:] = half_ref[...]


def second_gradient_kernel(
    u0, u1, alpha_ref, base_ref, dens_ref, line_ref, grad_ref, image_ref, share_ref
):
    alpha = alpha_ref[:1, :1]
    total = u0[...] + u1[...]
    dens = dens_ref[...]
    grad = base_ref[...] - alpha * total[:QX]
    quad = 1.0 / (dens * dens + 0.25)
    grad_ref[...] = grad
    image_ref[...] = line_ref[...] - alpha * total[QX:]
    square = grad * grad
    lane = lax.broadcasted_iota(jnp.int32, (8, NY), 1)
    share_ref[...] = jnp.where(
        lane == 0, jnp.sum(square), jnp.where(lane == 1, jnp.sum(quad * square), 0.0)
    )


def curvature_kernel(nh, part, *refs):
    parts = refs[:nh]
    image_ref, weight_ref, share_ref, out_ref, scratch = refs[nh:]
    rows = image_ref.shape[0]
    total = parts[0][...]
    for piece in parts[1:]:
        total = total + piece[...]
    image = image_ref[...] + total[:rows]
    scratch[...] = image
    out_ref[...] = scratch[pl.ds(pl.multiple_of(lax.axis_index("h") * part, part), part), :]
    mine = weight_ref[...] * image
    lane = lax.broadcasted_iota(jnp.int32, (1, 128), 1)
    share_ref[...] = jnp.broadcast_to(
        jnp.where(lane == 2, jnp.sum(mine * mine), total[rows : rows + 1, :128]), share_ref.shape
    )


def finish_kernel(
    shares_ref, dens_ref, grad_ref, alpha_ref, error_ref, first_ref, second_ref, w_ref, dens_out, err_out
):
    part = w_ref.shape[0]
    alpha = step_length(shares_ref[...])
    dens_out[0] = dens_ref[...] - alpha * grad_ref[...]
    place = pl.ds(pl.multiple_of(lax.axis_index("h") * part, part), part)
    error = error_ref[place, :] - alpha_ref[:1, :1] * first_ref[place, :]
    err_out[0] = w_ref[...] * (error - alpha * second_ref[...])


VMEM = pl.BlockSpec(memory_space=pltpu.VMEM)
SMEM = pl.BlockSpec(memory_space=pltpu.SMEM)
ANY = pl.BlockSpec(memory_space=pl.ANY)
FAR = pl.BlockSpec(memory_space=pltpu.HBM)


class Program:
    def __init__(self):
        self.alive = []

    def hold(self, *values):
        self.alive += values

    def drop(self, *values):
        self.alive = [item for item in self.alive if all(item is not value for value in values)]

    def call(self, kernel, outs, *args, scratch=(), scalars=(), far=(), far_out=(), sems=0, mib=8):
        used = len(args)
        keep = [item for item in self.alive if all(item is not value for value in args)]
        kept = len(keep)

        def inner(*refs):
            kernel(*refs[:used], *refs[used + kept :])

        args = [
            pltpu.with_memory_space_constraint(item, pltpu.HBM) if place in far else item
            for place, item in enumerate(args)
        ]
        kinds = [(item, F32) if isinstance(item, tuple) else (item.shape, item.dtype) for item in outs]
        return pl.pallas_call(
            inner,
            out_shape=[
                (pltpu.HBM if place in far_out else jax.ShapeDtypeStruct)(*kind)
                for place, kind in enumerate(kinds)
            ],
            in_specs=[
                SMEM if place in scalars else FAR if place in far else VMEM
                for place in range(used)
            ]
            + [ANY] * kept,
            out_specs=[FAR if place in far_out else VMEM for place in range(len(outs))],
            scratch_shapes=[pltpu.VMEM(shape, F32) for shape in scratch]
            + [pltpu.SemaphoreType.DMA((sems,) if sems > 1 else ())] * (sems > 0),
            compiler_params=pltpu.CompilerParams(vmem_limit_bytes=mib << 20),
        )(*args, *keep)


def from_comps(values):
    return [values[0]] + [
        lax.ppermute(values[step], COMP, [(i, i ^ step) for i in range(4)]) for step in (1, 2, 3)
    ]


def flip(value, axis):
    return lax.ppermute(value, axis, [(0, 1), (1, 0)])


def gather_comps(value):
    across = flip(value, "l")
    return [value, flip(value, "k"), across, flip(across, "k")]


def from_axis(values, axis):
    size = len(values)
    got = {0: values[0]}
    for step in sorted(range(1, size), key=lambda step: min(step, size - step)):
        got[step] = lax.ppermute(values[step], axis, [(i, (i + step) % size) for i in range(size)])
    return [got[step] for step in range(size)]


def exchange(value, axes):
    return lax.all_to_all(value, axes, 0, 0, tiled=True)


def after(values, *others):
    if isinstance(values, (list, tuple)):
        return list(lax.optimization_barrier((tuple(values), others))[0])
    return lax.optimization_barrier((values, others))[0]


def body(density, observed, data_weight, layer_top):
    nx, ny, nh = (lax.axis_size(axis) for axis in DEPTH)
    nxy = nx * ny
    rows = NX // nxy
    part = rows // nh
    fx, ty = (jnp.asarray(table) for table in make_tables())
    bind = functools.partial
    program = Program()
    call = program.call

    near, across = flip(density[0], "k"), flip(density[0], "l")
    *tables, dens, decay, gx, gy = call(
        prepare_kernel,
        [fx, fx, ty, (QX, NY), (KEPT, NY), (KEPT, NY), (KEPT, NY)],
        layer_top, fx, ty, density, scalars=(0,),
    )
    layers = [near, across, flip(after(across, dens), "k")]
    factors = (decay, gx, gy)
    weight_own, obs_own = data_weight[0], observed[0]
    program.hold(*tables, *factors, dens)
    message, full = call(
        bind(start_kernel, nxy), [(nxy, 2 * rows + 8, NY), (NX, NY)],
        dens, *layers, layer_top, *factors, *tables,
        scratch=[(NX, NY)] * 2, scalars=(4,), far_out=(1,), sems=1,
    )
    got = exchange(message, XY)
    (sums,) = call(
        bind(collect_kernel, nxy), [(2 * rows + nxy // 2 + part, NY)], got, weight_own, obs_own
    )
    sums = from_axis([sums] * nh, "h")
    error, pulled, weight, tops, message = call(
        bind(residual_kernel, nxy, nh),
        [(rows, NY), (rows, NY), (rows, NY), (nxy * nh // 2, NY), (nxy, rows, NY)],
        *sums, scratch=[(rows, NY)], far_out=(4,), sems=nxy,
    )
    program.hold(error, pulled, weight)
    got = exchange(message, XY)
    (power,) = call(bind(power_kernel, nxy * nh), [(KEPT, NY)], tops)
    program.hold(power)
    adjoint = lambda plane: call(
        bind(adjoint_kernel, nxy), [(2 * (QX + rows), NY)] * 2,
        plane.reshape(NX, NY), *factors, power, *tables,
        scratch=[(NX, NY), (4 * rows, NY)],
    )

    def reduce_comps(own, other):
        near, far = call(pair_kernel, [(QX + rows, NY)] * 2, own, flip(other, "k"))
        return near, flip(far, "l")

    pieces = reduce_comps(*adjoint(got))
    message, grad, line, image = call(
        bind(gradient_kernel, nxy, nh),
        [(nxy, rows + 8, NY), (QX, NY), (rows, NY), (rows, NY)],
        *pieces, pulled, dens, weight,
        scratch=[(rows, NY), (rows + 8, NY)], far_out=(0,), sems=nxy,
    )
    program.drop(pulled)
    program.hold(line, image)
    grads = gather_comps(grad)
    got = after(exchange(message, XY), *grads)
    plane, shares = call(bind(part_kernel, nxy), [(NX, NY), (nh * 4, 128)], got)
    pieces = adjoint(plane)
    shares = after(exchange(shares, ("h", *COMP)), *pieces)
    message, dens, base, alpha = call(
        second_kernel, [(nxy, rows, NY), (QX, NY), (QX, NY), (8, 128)],
        shares, dens, full, *grads, *factors, *tables,
        scratch=[(NX, NY)] * 2, far=(2, 3, 4, 5, 6), far_out=(0,), sems=max(nxy, 5),
    )
    program.alive = [weight, error, line, image, dens, base, alpha]
    got = exchange(message, XY)
    pieces = reduce_comps(*after(pieces, message))
    grad2, image2, half = call(
        second_gradient_kernel, [(QX, NY), (rows, NY), (8, NY)],
        *pieces, alpha, base, dens, line,
    )
    (parts,) = call(bind(sum_kernel, nxy), [(rows + 8, NY)], got, half)
    program.alive = [error, image, dens, alpha, grad2]
    shares, image2 = call(
        bind(curvature_kernel, nh, part), [(nxy * 4, 128), (part, NY)],
        *from_axis([parts] * nh, "h"), image2, weight, scratch=[(rows, NY)],
    )
    shares = exchange(shares, (*XY, *COMP))
    program.alive = []
    return tuple(
        call(
            finish_kernel, [density.shape, observed.shape],
            shares, dens, grad2, alpha, error, image, image2, weight_own,
        )
    )


def solution(mesh):
    depth = mesh.shape["depth"]
    sizes = {64: (4, 4, 4), 4: (2, 1, 2)}[depth]
    fine = Mesh(mesh.devices.reshape(*sizes, 2, 2), ALL)
    data = P(COMP, DEPTH, None)
    layer = P(DEPTH, COMP, None)
    return jax.shard_map(
        body,
        mesh=fine,
        in_specs=(layer, data, data, P(DEPTH)),
        out_specs=(layer, data),
        check_vma=False,
    )
```

```python
import functools
import math

import jax
import jax.numpy as jnp
import numpy as np
from jax import lax
from jax.experimental import pallas as pl
from jax.experimental.pallas import tpu as pltpu
from jax.sharding import Mesh
from jax.sharding import PartitionSpec as P

TWO_PI = 2.0 * math.pi
F32 = jnp.float32
BF16 = jnp.bfloat16
XY = ("x", "y")
DEPTH = ("x", "y", "h")
COMP = ("l", "k")
ALL = ("x", "y", "h", "l", "k")

NX = 512
NY = 256
HX = NX // 2
QX = NX // 4
HY = NY // 2


def split_table(table):
    high = table.astype(jnp.bfloat16)
    low = (table - high.astype(np.float64)).astype(jnp.bfloat16)
    return np.stack([high, low])


def basis(count, waves):
    place = np.arange(count)
    rows = []
    for wave in waves:
        norm = math.sqrt((1.0 if wave == 0 else 2.0) / count)
        rows.append(norm * np.cos(TWO_PI * (wave * place % count) / count))
    for wave in waves:
        if wave == 0:
            rows.append(math.sqrt(1.0 / count) * (1.0 - 2.0 * (place % 2)))
        else:
            rows.append(math.sqrt(2.0 / count) * np.sin(TWO_PI * (wave * place % count) / count))
    return np.stack(rows)


def make_tables():
    even = basis(NX, range(0, HX, 2))[:, :HX]
    odd = basis(NX, range(1, HX, 2))[:, :HX]
    col = basis(NY, range(HY))
    return (
        np.concatenate([split_table(even), split_table(odd)]),
        split_table(col.T),
    )


def split(value):
    high = value.astype(BF16)
    low = (value - high.astype(F32)).astype(BF16)
    return high, low


def dot(left, right):
    return jnp.dot(left, right, preferred_element_type=F32)


def dot_turned(left, right):
    return lax.dot_general(left, right, (((1,), (1,)), ((), ())), preferred_element_type=F32)


def times_table(value, high, low):
    vh, vl = split(value)
    return dot(vh, high) + (dot(vl, high) + dot(vh, low))


def times_turned(value, high, low):
    vh, vl = split(value)
    return dot_turned(vh, high) + (dot_turned(vl, high) + dot_turned(vh, low))


def table_times(high, low, value):
    vh, vl = split(value)
    return dot(high, vh) + (dot(high, vl) + dot(low, vh))


def to_waves(field, fx, ty):
    cols = times_table(field, ty[0], ty[1])
    upper, lower = cols[:HX], cols[HX:]
    return (
        table_times(fx[0], fx[1], upper + lower),
        table_times(fx[2], fx[3], upper - lower),
    )


def from_waves(even, odd, bx, ty):
    first = table_times(bx[0], bx[1], even)
    second = table_times(bx[2], bx[3], odd)
    rows = jnp.concatenate([first + second, first - second], axis=0)
    return times_turned(rows, ty[0], ty[1])


def swap_x(half):
    return jnp.concatenate([half[HX // 2 :], half[: HX // 2]], axis=0)


def swap_y(half):
    return jnp.concatenate([half[:, HY:], half[:, :HY]], axis=1)


def sines(cosines, nyquist):
    row = lax.broadcasted_iota(jnp.int32, cosines.shape, 0)
    return jnp.where(row == 0, nyquist, cosines)


def spread(ref):
    even, odd = ref[:QX], ref[QX:HX]
    return (
        jnp.concatenate([even, sines(even, ref[HX : HX + 1])], axis=0),
        jnp.concatenate([odd, odd], axis=0),
    )


def x_factors(gx_ref):
    even, odd = gx_ref[:QX], gx_ref[QX:HX]
    return jnp.concatenate([even, -even], axis=0), jnp.concatenate([odd, -odd], axis=0)


def xx_factors(gx_ref):
    even, odd = spread(gx_ref)
    return -(even * even), -(odd * odd)


def component(even, odd, gx_ref, gy_ref, comp):
    halves = []
    for half, first, second, third in zip(
        (even, odd), x_factors(gx_ref), spread(gy_ref), xx_factors(gx_ref)
    ):
        met = jnp.where(comp == 1, swap_x(half), jnp.where(comp == 2, swap_y(half), half))
        factor = jnp.where(comp == 1, first, jnp.where(comp == 2, second, third))
        halves.append(met * jnp.where(comp == 0, 1.0, factor))
    return halves


def comp_index():
    return lax.axis_index("l") * 2 + lax.axis_index("k")


KEPT = HX + 8


def wave_grid():
    row = lax.broadcasted_iota(jnp.int32, (KEPT, NY), 0)
    col = lax.broadcasted_iota(jnp.int32, (KEPT, NY), 1)
    wave_x = jnp.where(row >= HX, HX, 2 * (row % QX) + (row >= QX).astype(jnp.int32))
    nyquist_y = col == HY
    wave_y = jnp.where(nyquist_y, HY, col % HY)
    kx = wave_x.astype(F32) * (TWO_PI / NX)
    ky = wave_y.astype(F32) * (TWO_PI / NY)
    return kx, ky, col >= HY, nyquist_y


def prepare_kernel(
    top_ref, fx_in, ty_in, dens_in, fx, bx, ty, dens_ref, decay_ref, gx_ref, gy_ref, sems
):
    copies = [
        pltpu.make_async_copy(source, target, sems.at[place])
        for place, (source, target) in enumerate(
            ((fx_in, fx), (ty_in, ty), (dens_in.at[0], dens_ref))
        )
    ]
    for copy in copies:
        copy.start()
    kx, ky, sine_y, nyquist_y = wave_grid()
    kabs = jnp.sqrt(kx * kx + ky * ky)
    inverse = 1.0 / jnp.maximum(kabs, TWO_PI / max(NX, NY))
    decay_ref[...] = 4.0 * jnp.exp(-kabs * top_ref[0]) * (1.0 - jnp.exp(-kabs))
    gx_ref[...] = kx * inverse
    ry = ky * inverse
    gy_ref[...] = jnp.where(nyquist_y, 0.0, jnp.where(sine_y, -ry, ry))
    for copy in copies:
        copy.wait()
    for place in range(4):
        bx[place] = fx[place].astype(F32).T.astype(BF16)


def gather_rows(pieces, full_ref):
    comp = comp_index()
    for step, piece in enumerate(pieces):
        full_ref[pl.ds(pl.multiple_of(jnp.bitwise_xor(comp, step) * QX, QX), QX), :] = piece[...]


def forward_plane(field, decay_ref, gx_ref, gy_ref, fx, bx, ty):
    even, odd = to_waves(field, fx, ty)
    decay = spread(decay_ref)
    even, odd = component(even * decay[0], odd * decay[1], gx_ref, gy_ref, comp_index())
    return from_waves(even, odd, bx, ty)


def start_kernel(
    nxy, m0, m1, m2, m3, top_ref, decay_ref, gx_ref, gy_ref, fx, bx, ty, out_ref, far_ref, full_ref, pull_ref, sem
):
    rows = NX // nxy
    gather_rows((m0, m1, m2, m3), full_ref)
    copy = pltpu.make_async_copy(full_ref, far_ref, sem)
    copy.start()
    dens = full_ref[...]
    pull_ref[...] = 0.5 * (dens * (1.0 / (dens * dens + 0.25)))
    for place, field in enumerate((full_ref, pull_ref)):
        plane = forward_plane(field[...], decay_ref, gx_ref, gy_ref, fx, bx, ty)
        for target in range(nxy):
            out_ref[target, place * rows : (place + 1) * rows, :] = plane[
                target * rows : (target + 1) * rows
            ]
    for target in range(nxy):
        out_ref[target, 2 * rows : 2 * rows + 8, :] = jnp.full((8, NY), top_ref[0], F32)
    copy.wait()


def collect_kernel(nxy, got_ref, weight_ref, obs_ref, sum_ref):
    rows = NX // nxy
    total = got_ref[0, : 2 * rows, :]
    for source in range(1, nxy):
        total = total + got_ref[source, : 2 * rows, :]
    sum_ref[: 2 * rows] = total
    part = weight_ref.shape[0]
    place = pl.ds(pl.multiple_of(lax.axis_index("h") * part, part), part)
    sum_ref[place, :] = sum_ref[place, :] - obs_ref[...]
    left = lax.broadcasted_iota(jnp.int32, (1, NY), 1) < HY
    for pair in range(nxy // 2):
        first, second = (got_ref[2 * pair + i, 2 * rows : 2 * rows + 1, :] for i in (0, 1))
        sum_ref[2 * rows + pair : 2 * rows + pair + 1, :] = jnp.where(left, first, second)
    sum_ref[2 * rows + nxy // 2 :] = weight_ref[...]


def send_all(block_ref, far_ref, sems):
    copies = [
        pltpu.make_async_copy(block_ref, far_ref.at[place], sems.at[place])
        for place in range(far_ref.shape[0])
    ]
    for copy in copies:
        copy.start()
    return copies


def residual_kernel(nxy, nh, *refs):
    rows = NX // nxy
    part = rows // nh
    pairs = nxy // 2
    start = 2 * rows + pairs
    sums = refs[:nh]
    error_ref, pull_ref, weight_ref, tops_ref, far_ref, block_ref, sems = refs[nh:]
    chip = lax.axis_index("h")
    total = sums[0][: 2 * rows]
    for step in range(1, nh):
        total = total + sums[step][: 2 * rows]
    for step in range(nh):
        tops_ref[step * pairs : (step + 1) * pairs] = sums[step][2 * rows : start]
        place = pl.ds(pl.multiple_of(lax.rem(chip + (nh - step), nh) * part, part), part)
        weight_ref[place, :] = sums[step][start:]
    weight = weight_ref[...]
    error = total[:rows]
    block_ref[...] = weight * (weight * error)
    copies = send_all(block_ref, far_ref, sems)
    error_ref[...] = error
    pull_ref[...] = total[rows:]
    for copy in copies:
        copy.wait()


def power_kernel(layers, tops_ref, power_ref):
    kx, ky, *_ = wave_grid()
    for start in range(0, KEPT, 64):
        stop = min(start + 64, KEPT)
        ks = jnp.sqrt(kx[start:stop] ** 2 + ky[start:stop] ** 2)
        double = -2.0 * ks

        def add(step, total):
            for pair in range(2):
                tops = tops_ref[pl.ds(2 * step + pair, 1), :]
                for top in (tops[:, :HY], tops[:, HY:]):
                    total = total + jnp.exp(double * jnp.concatenate([top, top], axis=1))
            return total

        total = lax.fori_loop(0, layers // 4, add, jnp.zeros_like(ks))
        rise = 1.0 - jnp.exp(-ks)
        power_ref[start:stop] = (16.0 * (rise * rise)) * total


def adjoint_kernel(
    nxy, res_ref, decay_ref, gx_ref, gy_ref, power_ref, fx, bx, ty, own_out, other_out, z_ref, i_ref
):
    rows = NX // nxy
    comp = comp_index()
    even, odd = to_waves(res_ref[...], fx, ty)
    even, odd = component(even, odd, gx_ref, gy_ref, comp)
    sign = jnp.where((comp == 1) | (comp == 2), -1.0, 1.0)
    even = even * sign
    odd = odd * sign
    decay = spread(decay_ref)
    z_ref[...] = from_waves(even * decay[0], odd * decay[1], bx, ty)
    power = spread(power_ref)
    even = even * power[0]
    odd = odd * power[1]
    block = lax.axis_index("x") * lax.axis_size("y") + lax.axis_index("y")
    upper = block * rows < HX
    near = pl.ds(pl.multiple_of(lax.rem(block * rows, HX), rows), rows)
    flip = jnp.where(upper, 1.0, -1.0)
    for target in range(4):
        if target == 0:
            e, o = even, odd
        elif target == 1:
            first = x_factors(gx_ref)
            e, o = swap_x(even) * first[0], swap_x(odd) * first[1]
        elif target == 2:
            second = spread(gy_ref)
            e, o = swap_y(even) * second[0], swap_y(odd) * second[1]
        else:
            third = xx_factors(gx_ref)
            e, o = even * third[0], odd * third[1]
        line = table_times(bx[0, near, :], bx[1, near, :], e)
        line = line + flip * table_times(bx[2, near, :], bx[3, near, :], o)
        i_ref[target * rows : (target + 1) * rows, :] = line
    i_ref[...] = times_turned(i_ref[...], ty[0], ty[1])
    for step in range(4):
        out = (own_out, other_out)[step % 2]
        begin = (step // 2) * (QX + rows)
        other = jnp.bitwise_xor(comp, step)
        out[begin : begin + QX] = z_ref[pl.ds(pl.multiple_of(other * QX, QX), QX), :]
        out[begin + QX : begin + QX + rows] = i_ref[
            pl.ds(pl.multiple_of(other * rows, rows), rows), :
        ]


def pair_kernel(own_ref, got_ref, near_ref, far_ref):
    half = near_ref.shape[0]
    near_ref[...] = own_ref[:half] + got_ref[:half]
    far_ref[...] = own_ref[half:] + got_ref[half:]


def share(grad, quad, image, weight, scratch, part):
    scratch[...] = weight * image
    place = pl.ds(pl.multiple_of(lax.axis_index("h") * part, part), part)
    mine = scratch[place, :]
    lane = lax.broadcasted_iota(jnp.int32, (1, NY), 1)
    square = grad * grad
    gg = jnp.sum(square)
    qgg = jnp.sum(quad * square)
    curv = jnp.sum(mine * mine)
    return jnp.where(lane == 0, gg, jnp.where(lane == 1, qgg, jnp.where(lane == 2, curv, 0.0)))


def step_length(shares):
    total = jnp.sum(shares, axis=0, keepdims=True)
    lane = lax.broadcasted_iota(jnp.int32, total.shape, 1)
    pick = lambda place: jnp.sum(jnp.where(lane == place, total, 0.0), keepdims=True)
    return pick(0) / (pick(2) + 0.5 * pick(1))


def gradient_kernel(nxy, nh, *refs):
    rows = NX // nxy
    part = rows // nh
    pieces = refs[:2]
    pull_ref, dens_ref, weight_ref = refs[2:5]
    far_ref, grad_ref, line_ref, image_ref, scratch, block_ref, sems = refs[5:]
    total = pieces[0][...] + pieces[1][...]
    data = total[:QX]
    line = total[QX:]
    dens = dens_ref[...]
    quad = 1.0 / (dens * dens + 0.25)
    grad = data + 0.5 * (quad * dens)
    image = line + pull_ref[...]
    weight = weight_ref[...]
    block_ref[:rows] = weight * (weight * image)
    block_ref[rows:] = jnp.broadcast_to(share(grad, quad, image, weight, scratch, part), (8, NY))
    copies = send_all(block_ref, far_ref, sems)
    grad_ref[...] = grad
    line_ref[...] = line
    image_ref[...] = image
    for copy in copies:
        copy.wait()


def part_kernel(nxy, got_ref, plane_ref, share_ref):
    rows = NX // nxy
    total = got_ref[0, rows:, :]
    for source in range(1, nxy):
        total = total + got_ref[source, rows:, :]
    share_ref[...] = total
    for source in range(nxy):
        plane_ref[source * rows : (source + 1) * rows] = got_ref[source, :rows, :]


def add_kernel(*refs):
    total = refs[0][...]
    for part in refs[1:-1]:
        total = total + part[...]
    refs[-1][...] = total


def second_kernel(
    s0, s1, s2, s3, dens_ref, full_ref, g0, g1, g2, g3, decay_ref, gx_ref, gy_ref, fx, bx, ty,
    out_ref, dens_out, base_out, alpha_ref, all_ref,
):
    gather_rows((g0, g1, g2, g3), all_ref)
    alpha = step_length(s0[:1] + s1[:1] + (s2[:1] + s3[:1]))
    alpha_ref[...] = jnp.broadcast_to(alpha, alpha_ref.shape)
    old = dens_ref[...]
    grad = g0[...]
    dens = old - alpha * grad
    dens_out[...] = dens
    data = grad - 0.5 * ((1.0 / (old * old + 0.25)) * old)
    base_out[...] = data + 0.5 * (dens * (1.0 / (dens * dens + 0.25)))
    dens = full_ref[...] - alpha * all_ref[...]
    all_ref[...] = 0.5 * (dens * (1.0 / (dens * dens + 0.25)))
    plane = forward_plane(all_ref[...], decay_ref, gx_ref, gy_ref, fx, bx, ty)
    out_ref[...] = plane.reshape(out_ref.shape)


def sum_kernel(nxy, got_ref, half_ref, sum_ref):
    rows = NX // nxy
    total = got_ref[0]
    for source in range(1, nxy):
        total = total + got_ref[source]
    sum_ref[:rows] = total
    sum_ref[rows:] = half_ref[...]


def second_gradient_kernel(
    u0, u1, alpha_ref, base_ref, dens_ref, line_ref, grad_ref, image_ref, share_ref
):
    alpha = alpha_ref[:1, :1]
    total = u0[...] + u1[...]
    dens = dens_ref[...]
    grad = base_ref[...] - alpha * total[:QX]
    quad = 1.0 / (dens * dens + 0.25)
    grad_ref[...] = grad
    image_ref[...] = line_ref[...] - alpha * total[QX:]
    square = grad * grad
    lane = lax.broadcasted_iota(jnp.int32, (8, NY), 1)
    share_ref[...] = jnp.where(
        lane == 0, jnp.sum(square), jnp.where(lane == 1, jnp.sum(quad * square), 0.0)
    )


def curvature_kernel(nh, part, *refs):
    parts = refs[:nh]
    image_ref, weight_ref, share_ref, out_ref, scratch = refs[nh:]
    rows = image_ref.shape[0]
    total = parts[0][...]
    for piece in parts[1:]:
        total = total + piece[...]
    image = image_ref[...] + total[:rows]
    scratch[...] = image
    out_ref[...] = scratch[pl.ds(pl.multiple_of(lax.axis_index("h") * part, part), part), :]
    mine = weight_ref[...] * image
    lane = lax.broadcasted_iota(jnp.int32, (1, 128), 1)
    share_ref[...] = jnp.broadcast_to(
        jnp.where(lane == 2, jnp.sum(mine * mine), total[rows : rows + 1, :128]), share_ref.shape
    )


def finish_kernel(
    shares_ref, dens_ref, grad_ref, alpha_ref, error_ref, first_ref, second_ref, w_ref, dens_out, err_out
):
    part = w_ref.shape[0]
    alpha = step_length(shares_ref[...])
    dens_out[0] = dens_ref[...] - alpha * grad_ref[...]
    place = pl.ds(pl.multiple_of(lax.axis_index("h") * part, part), part)
    error = error_ref[place, :] - alpha_ref[:1, :1] * first_ref[place, :]
    err_out[0] = w_ref[...] * (error - alpha * second_ref[...])


VMEM = pl.BlockSpec(memory_space=pltpu.VMEM)
SMEM = pl.BlockSpec(memory_space=pltpu.SMEM)
ANY = pl.BlockSpec(memory_space=pl.ANY)
FAR = pl.BlockSpec(memory_space=pltpu.HBM)


class Program:
    def __init__(self):
        self.alive = []

    def hold(self, *values):
        self.alive += values

    def drop(self, *values):
        self.alive = [item for item in self.alive if all(item is not value for value in values)]

    def call(self, kernel, outs, *args, scratch=(), scalars=(), far=(), far_out=(), sems=0, mib=8):
        used = len(args)
        keep = [item for item in self.alive if all(item is not value for value in args)]
        kept = len(keep)

        def inner(*refs):
            kernel(*refs[:used], *refs[used + kept :])

        args = [
            pltpu.with_memory_space_constraint(item, pltpu.HBM) if place in far else item
            for place, item in enumerate(args)
        ]
        kinds = [(item, F32) if isinstance(item, tuple) else (item.shape, item.dtype) for item in outs]
        return pl.pallas_call(
            inner,
            out_shape=[
                (pltpu.HBM if place in far_out else jax.ShapeDtypeStruct)(*kind)
                for place, kind in enumerate(kinds)
            ],
            in_specs=[
                SMEM if place in scalars else FAR if place in far else VMEM
                for place in range(used)
            ]
            + [ANY] * kept,
            out_specs=[FAR if place in far_out else VMEM for place in range(len(outs))],
            scratch_shapes=[pltpu.VMEM(shape, F32) for shape in scratch]
            + [pltpu.SemaphoreType.DMA((sems,) if sems > 1 else ())] * (sems > 0),
            compiler_params=pltpu.CompilerParams(vmem_limit_bytes=mib << 20),
        )(*args, *keep)


def from_comps(values):
    return [values[0]] + [
        lax.ppermute(values[step], COMP, [(i, i ^ step) for i in range(4)]) for step in (1, 2, 3)
    ]


def flip(value, axis):
    return lax.ppermute(value, axis, [(0, 1), (1, 0)])


def gather_comps(value):
    across = flip(value, "l")
    return [value, flip(value, "k"), across, flip(across, "k")]


def from_axis(values, axis):
    size = len(values)
    got = {0: values[0]}
    for step in sorted(range(1, size), key=lambda step: min(step, size - step)):
        got[step] = lax.ppermute(values[step], axis, [(i, (i + step) % size) for i in range(size)])
    return [got[step] for step in range(size)]


def exchange(value, axes):
    return lax.all_to_all(value, axes, 0, 0, tiled=True)


def after(values, *others):
    if isinstance(values, (list, tuple)):
        return list(lax.optimization_barrier((tuple(values), others))[0])
    return lax.optimization_barrier((values, others))[0]


def body(density, observed, data_weight, layer_top):
    nx, ny, nh = (lax.axis_size(axis) for axis in DEPTH)
    nxy = nx * ny
    rows = NX // nxy
    part = rows // nh
    fx, ty = (jnp.asarray(table) for table in make_tables())
    bind = functools.partial
    program = Program()
    call = program.call

    near, across = flip(density[0], "k"), flip(density[0], "l")
    *tables, dens, decay, gx, gy = call(
        prepare_kernel,
        [fx, fx, ty, (QX, NY), (KEPT, NY), (KEPT, NY), (KEPT, NY)],
        layer_top, fx, ty, density, scalars=(0,), far=(1, 2, 3), sems=3,
    )
    layers = [near, across, flip(after(across, dens), "k")]
    factors = (decay, gx, gy)
    weight_own, obs_own = data_weight[0], observed[0]
    program.hold(*tables, *factors, dens)
    message, full = call(
        bind(start_kernel, nxy), [(nxy, 2 * rows + 8, NY), (NX, NY)],
        dens, *layers, layer_top, *factors, *tables,
        scratch=[(NX, NY)] * 2, scalars=(4,), far_out=(1,), sems=1,
    )
    got = exchange(message, XY)
    (sums,) = call(
        bind(collect_kernel, nxy), [(2 * rows + nxy // 2 + part, NY)], got, weight_own, obs_own
    )
    sums = from_axis([sums] * nh, "h")
    error, pulled, weight, tops, message = call(
        bind(residual_kernel, nxy, nh),
        [(rows, NY), (rows, NY), (rows, NY), (nxy * nh // 2, NY), (nxy, rows, NY)],
        *sums, scratch=[(rows, NY)], far_out=(4,), sems=nxy,
    )
    program.hold(error, pulled, weight)
    got = exchange(message, XY)
    (power,) = call(bind(power_kernel, nxy * nh), [(KEPT, NY)], tops)
    program.hold(power)
    adjoint = lambda plane: call(
        bind(adjoint_kernel, nxy), [(2 * (QX + rows), NY)] * 2,
        plane.reshape(NX, NY), *factors, power, *tables,
        scratch=[(NX, NY), (4 * rows, NY)],
    )

    def reduce_comps(own, other):
        near, far = call(pair_kernel, [(QX + rows, NY)] * 2, own, flip(other, "k"))
        return near, flip(far, "l")

    pieces = reduce_comps(*adjoint(got))
    message, grad, line, image = call(
        bind(gradient_kernel, nxy, nh),
        [(nxy, rows + 8, NY), (QX, NY), (rows, NY), (rows, NY)],
        *pieces, pulled, dens, weight,
        scratch=[(rows, NY), (rows + 8, NY)], far_out=(0,), sems=nxy,
    )
    program.drop(pulled)
    program.hold(line, image)
    grads = gather_comps(grad)
    got = after(exchange(message, XY), *grads)
    plane, shares = call(bind(part_kernel, nxy), [(NX, NY), (8, NY)], got)
    pieces = adjoint(plane)
    shares = after(from_axis([shares] * nh, "h"), *pieces)
    (shares,) = call(add_kernel, [(8, NY)], *shares)
    shares = from_comps([shares] * 4)
    message, dens, base, alpha = call(
        second_kernel, [(nxy, rows, NY), (QX, NY), (QX, NY), (8, 128)],
        *shares, dens, full, *grads, *factors, *tables, scratch=[(NX, NY)],
    )
    program.alive = [weight, error, line, image, dens, base, alpha]
    got = exchange(message, XY)
    pieces = reduce_comps(*after(pieces, message))
    grad2, image2, half = call(
        second_gradient_kernel, [(QX, NY), (rows, NY), (8, NY)],
        *pieces, alpha, base, dens, line,
    )
    (parts,) = call(bind(sum_kernel, nxy), [(rows + 8, NY)], got, half)
    program.alive = [error, image, dens, alpha, grad2]
    shares, image2 = call(
        bind(curvature_kernel, nh, part), [(nxy * 4, 128), (part, NY)],
        *from_axis([parts] * nh, "h"), image2, weight, scratch=[(rows, NY)],
    )
    shares = exchange(shares, (*XY, *COMP))
    program.alive = []
    return tuple(
        call(
            finish_kernel, [density.shape, observed.shape],
            shares, dens, grad2, alpha, error, image, image2, weight_own,
        )
    )


def solution(mesh):
    depth = mesh.shape["depth"]
    sizes = {64: (4, 4, 4), 4: (2, 1, 2)}[depth]
    fine = Mesh(mesh.devices.reshape(*sizes, 2, 2), ALL)
    data = P(COMP, DEPTH, None)
    layer = P(DEPTH, COMP, None)
    return jax.shard_map(
        body,
        mesh=fine,
        in_specs=(layer, data, data, P(DEPTH)),
        out_specs=(layer, data),
        check_vma=False,
    )
```

```python
import functools
import math

import jax
import jax.numpy as jnp
import numpy as np
from jax import lax
from jax.experimental import pallas as pl
from jax.experimental.pallas import tpu as pltpu
from jax.sharding import Mesh
from jax.sharding import PartitionSpec as P

TWO_PI = 2.0 * math.pi
F32 = jnp.float32
BF16 = jnp.bfloat16
XY = ("x", "y")
DEPTH = ("x", "y", "h")
COMP = ("l", "k")
ALL = ("x", "y", "h", "l", "k")

NX = 512
NY = 256
HX = NX // 2
QX = NX // 4
HY = NY // 2


def split_table(table):
    high = table.astype(jnp.bfloat16)
    low = (table - high.astype(np.float64)).astype(jnp.bfloat16)
    return np.stack([high, low])


def basis(count, waves):
    place = np.arange(count)
    rows = []
    for wave in waves:
        norm = math.sqrt((1.0 if wave == 0 else 2.0) / count)
        rows.append(norm * np.cos(TWO_PI * (wave * place % count) / count))
    for wave in waves:
        if wave == 0:
            rows.append(math.sqrt(1.0 / count) * (1.0 - 2.0 * (place % 2)))
        else:
            rows.append(math.sqrt(2.0 / count) * np.sin(TWO_PI * (wave * place % count) / count))
    return np.stack(rows)


def make_tables():
    even = basis(NX, range(0, HX, 2))[:, :HX]
    odd = basis(NX, range(1, HX, 2))[:, :HX]
    col = basis(NY, range(HY))
    return (
        np.concatenate([split_table(even), split_table(odd)]),
        split_table(col.T),
    )


def split(value):
    high = value.astype(BF16)
    low = (value - high.astype(F32)).astype(BF16)
    return high, low


def dot(left, right):
    return jnp.dot(left, right, preferred_element_type=F32)


def dot_turned(left, right):
    return lax.dot_general(left, right, (((1,), (1,)), ((), ())), preferred_element_type=F32)


def times_table(value, high, low):
    vh, vl = split(value)
    return dot(vh, high) + (dot(vl, high) + dot(vh, low))


def times_turned(value, high, low):
    vh, vl = split(value)
    return dot_turned(vh, high) + (dot_turned(vl, high) + dot_turned(vh, low))


def table_times(high, low, value):
    vh, vl = split(value)
    return dot(high, vh) + (dot(high, vl) + dot(low, vh))


def to_waves(field, fx, ty):
    cols = times_table(field, ty[0], ty[1])
    upper, lower = cols[:HX], cols[HX:]
    return (
        table_times(fx[0], fx[1], upper + lower),
        table_times(fx[2], fx[3], upper - lower),
    )


def from_waves(even, odd, bx, ty):
    first = table_times(bx[0], bx[1], even)
    second = table_times(bx[2], bx[3], odd)
    rows = jnp.concatenate([first + second, first - second], axis=0)
    return times_turned(rows, ty[0], ty[1])


def swap_x(half):
    return jnp.concatenate([half[HX // 2 :], half[: HX // 2]], axis=0)


def swap_y(half):
    return jnp.concatenate([half[:, HY:], half[:, :HY]], axis=1)


def sines(cosines, nyquist):
    row = lax.broadcasted_iota(jnp.int32, cosines.shape, 0)
    return jnp.where(row == 0, nyquist, cosines)


def spread(ref):
    even, odd = ref[:QX], ref[QX:HX]
    return (
        jnp.concatenate([even, sines(even, ref[HX : HX + 1])], axis=0),
        jnp.concatenate([odd, odd], axis=0),
    )


def x_factors(gx_ref):
    even, odd = gx_ref[:QX], gx_ref[QX:HX]
    return jnp.concatenate([even, -even], axis=0), jnp.concatenate([odd, -odd], axis=0)


def xx_factors(gx_ref):
    even, odd = spread(gx_ref)
    return -(even * even), -(odd * odd)


def component(even, odd, gx_ref, gy_ref, comp):
    halves = []
    for half, first, second, third in zip(
        (even, odd), x_factors(gx_ref), spread(gy_ref), xx_factors(gx_ref)
    ):
        met = jnp.where(comp == 1, swap_x(half), jnp.where(comp == 2, swap_y(half), half))
        factor = jnp.where(comp == 1, first, jnp.where(comp == 2, second, third))
        halves.append(met * jnp.where(comp == 0, 1.0, factor))
    return halves


def comp_index():
    return lax.axis_index("l") * 2 + lax.axis_index("k")


KEPT = HX + 8


def wave_grid():
    row = lax.broadcasted_iota(jnp.int32, (KEPT, NY), 0)
    col = lax.broadcasted_iota(jnp.int32, (KEPT, NY), 1)
    wave_x = jnp.where(row >= HX, HX, 2 * (row % QX) + (row >= QX).astype(jnp.int32))
    nyquist_y = col == HY
    wave_y = jnp.where(nyquist_y, HY, col % HY)
    kx = wave_x.astype(F32) * (TWO_PI / NX)
    ky = wave_y.astype(F32) * (TWO_PI / NY)
    return kx, ky, col >= HY, nyquist_y


def prepare_kernel(
    top_ref, fx_in, ty_in, dens_in, fx, bx, ty, dens_ref, decay_ref, gx_ref, gy_ref, sems
):
    copies = [
        pltpu.make_async_copy(source, target, sems.at[place])
        for place, (source, target) in enumerate(
            ((fx_in, fx), (ty_in, ty), (dens_in.at[0], dens_ref))
        )
    ]
    for copy in copies:
        copy.start()
    kx, ky, sine_y, nyquist_y = wave_grid()
    kabs = jnp.sqrt(kx * kx + ky * ky)
    inverse = 1.0 / jnp.maximum(kabs, TWO_PI / max(NX, NY))
    decay_ref[...] = 4.0 * jnp.exp(-kabs * top_ref[0]) * (1.0 - jnp.exp(-kabs))
    gx_ref[...] = kx * inverse
    ry = ky * inverse
    gy_ref[...] = jnp.where(nyquist_y, 0.0, jnp.where(sine_y, -ry, ry))
    for copy in copies:
        copy.wait()
    for place in range(4):
        bx[place] = fx[place].astype(F32).T.astype(BF16)


def gather_rows(pieces, full_ref):
    comp = comp_index()
    for step, piece in enumerate(pieces):
        full_ref[pl.ds(pl.multiple_of(jnp.bitwise_xor(comp, step) * QX, QX), QX), :] = piece[...]


def forward_plane(field, decay_ref, gx_ref, gy_ref, fx, bx, ty):
    even, odd = to_waves(field, fx, ty)
    decay = spread(decay_ref)
    even, odd = component(even * decay[0], odd * decay[1], gx_ref, gy_ref, comp_index())
    return from_waves(even, odd, bx, ty)


def start_kernel(
    nxy, m0, m1, m2, m3, top_ref, decay_ref, gx_ref, gy_ref, fx, bx, ty, out_ref, far_ref, full_ref, pull_ref, sem
):
    rows = NX // nxy
    gather_rows((m0, m1, m2, m3), full_ref)
    copy = pltpu.make_async_copy(full_ref, far_ref, sem)
    copy.start()
    dens = full_ref[...]
    pull_ref[...] = 0.5 * (dens * (1.0 / (dens * dens + 0.25)))
    for place, field in enumerate((full_ref, pull_ref)):
        plane = forward_plane(field[...], decay_ref, gx_ref, gy_ref, fx, bx, ty)
        for target in range(nxy):
            out_ref[target, place * rows : (place + 1) * rows, :] = plane[
                target * rows : (target + 1) * rows
            ]
    for target in range(nxy):
        out_ref[target, 2 * rows : 2 * rows + 8, :] = jnp.full((8, NY), top_ref[0], F32)
    copy.wait()


def collect_kernel(nxy, got_ref, weight_ref, obs_ref, sum_ref):
    rows = NX // nxy
    total = got_ref[0, : 2 * rows, :]
    for source in range(1, nxy):
        total = total + got_ref[source, : 2 * rows, :]
    sum_ref[: 2 * rows] = total
    part = weight_ref.shape[0]
    place = pl.ds(pl.multiple_of(lax.axis_index("h") * part, part), part)
    sum_ref[place, :] = sum_ref[place, :] - obs_ref[...]
    left = lax.broadcasted_iota(jnp.int32, (1, NY), 1) < HY
    for pair in range(nxy // 2):
        first, second = (got_ref[2 * pair + i, 2 * rows : 2 * rows + 1, :] for i in (0, 1))
        sum_ref[2 * rows + pair : 2 * rows + pair + 1, :] = jnp.where(left, first, second)
    sum_ref[2 * rows + nxy // 2 :] = weight_ref[...]


def send_all(block_ref, far_ref, sems):
    copies = [
        pltpu.make_async_copy(block_ref, far_ref.at[place], sems.at[place])
        for place in range(far_ref.shape[0])
    ]
    for copy in copies:
        copy.start()
    return copies


def residual_kernel(nxy, nh, *refs):
    rows = NX // nxy
    part = rows // nh
    pairs = nxy // 2
    start = 2 * rows + pairs
    sums = refs[:nh]
    error_ref, pull_ref, weight_ref, tops_ref, far_ref, block_ref, sems = refs[nh:]
    chip = lax.axis_index("h")
    total = sums[0][: 2 * rows]
    for step in range(1, nh):
        total = total + sums[step][: 2 * rows]
    for step in range(nh):
        tops_ref[step * pairs : (step + 1) * pairs] = sums[step][2 * rows : start]
        place = pl.ds(pl.multiple_of(lax.rem(chip + (nh - step), nh) * part, part), part)
        weight_ref[place, :] = sums[step][start:]
    weight = weight_ref[...]
    error = total[:rows]
    block_ref[...] = weight * (weight * error)
    copies = send_all(block_ref, far_ref, sems)
    error_ref[...] = error
    pull_ref[...] = total[rows:]
    for copy in copies:
        copy.wait()


def power_kernel(layers, tops_ref, power_ref):
    kx, ky, *_ = wave_grid()
    for start in range(0, KEPT, 64):
        stop = min(start + 64, KEPT)
        ks = jnp.sqrt(kx[start:stop] ** 2 + ky[start:stop] ** 2)
        double = -2.0 * ks

        def add(step, total):
            for pair in range(2):
                tops = tops_ref[pl.ds(2 * step + pair, 1), :]
                for top in (tops[:, :HY], tops[:, HY:]):
                    total = total + jnp.exp(double * jnp.concatenate([top, top], axis=1))
            return total

        total = lax.fori_loop(0, layers // 4, add, jnp.zeros_like(ks))
        rise = 1.0 - jnp.exp(-ks)
        power_ref[start:stop] = (16.0 * (rise * rise)) * total


def adjoint_kernel(
    nxy, res_ref, decay_ref, gx_ref, gy_ref, power_ref, fx, bx, ty, own_out, other_out, z_ref, i_ref
):
    rows = NX // nxy
    comp = comp_index()
    even, odd = to_waves(res_ref[...], fx, ty)
    even, odd = component(even, odd, gx_ref, gy_ref, comp)
    sign = jnp.where((comp == 1) | (comp == 2), -1.0, 1.0)
    even = even * sign
    odd = odd * sign
    decay = spread(decay_ref)
    z_ref[...] = from_waves(even * decay[0], odd * decay[1], bx, ty)
    power = spread(power_ref)
    even = even * power[0]
    odd = odd * power[1]
    block = lax.axis_index("x") * lax.axis_size("y") + lax.axis_index("y")
    upper = block * rows < HX
    near = pl.ds(pl.multiple_of(lax.rem(block * rows, HX), rows), rows)
    flip = jnp.where(upper, 1.0, -1.0)
    for target in range(4):
        if target == 0:
            e, o = even, odd
        elif target == 1:
            first = x_factors(gx_ref)
            e, o = swap_x(even) * first[0], swap_x(odd) * first[1]
        elif target == 2:
            second = spread(gy_ref)
            e, o = swap_y(even) * second[0], swap_y(odd) * second[1]
        else:
            third = xx_factors(gx_ref)
            e, o = even * third[0], odd * third[1]
        line = table_times(bx[0, near, :], bx[1, near, :], e)
        line = line + flip * table_times(bx[2, near, :], bx[3, near, :], o)
        i_ref[target * rows : (target + 1) * rows, :] = line
    i_ref[...] = times_turned(i_ref[...], ty[0], ty[1])
    for step in range(4):
        out = (own_out, other_out)[step % 2]
        begin = (step // 2) * (QX + rows)
        other = jnp.bitwise_xor(comp, step)
        out[begin : begin + QX] = z_ref[pl.ds(pl.multiple_of(other * QX, QX), QX), :]
        out[begin + QX : begin + QX + rows] = i_ref[
            pl.ds(pl.multiple_of(other * rows, rows), rows), :
        ]


def pair_kernel(own_ref, got_ref, near_ref, far_ref):
    half = near_ref.shape[0]
    near_ref[...] = own_ref[:half] + got_ref[:half]
    far_ref[...] = own_ref[half:] + got_ref[half:]


def share(grad, quad, image, weight, scratch, part):
    scratch[...] = weight * image
    place = pl.ds(pl.multiple_of(lax.axis_index("h") * part, part), part)
    mine = scratch[place, :]
    lane = lax.broadcasted_iota(jnp.int32, (1, NY), 1)
    square = grad * grad
    gg = jnp.sum(square)
    qgg = jnp.sum(quad * square)
    curv = jnp.sum(mine * mine)
    return jnp.where(lane == 0, gg, jnp.where(lane == 1, qgg, jnp.where(lane == 2, curv, 0.0)))


def step_length(shares):
    total = jnp.sum(shares, axis=0, keepdims=True)
    lane = lax.broadcasted_iota(jnp.int32, total.shape, 1)
    pick = lambda place: jnp.sum(jnp.where(lane == place, total, 0.0), keepdims=True)
    return pick(0) / (pick(2) + 0.5 * pick(1))


def gradient_kernel(nxy, nh, *refs):
    rows = NX // nxy
    part = rows // nh
    pieces = refs[:2]
    pull_ref, dens_ref, weight_ref = refs[2:5]
    far_ref, grad_ref, line_ref, image_ref, scratch, block_ref, sems = refs[5:]
    total = pieces[0][...] + pieces[1][...]
    data = total[:QX]
    line = total[QX:]
    dens = dens_ref[...]
    quad = 1.0 / (dens * dens + 0.25)
    grad = data + 0.5 * (quad * dens)
    image = line + pull_ref[...]
    weight = weight_ref[...]
    block_ref[:rows] = weight * (weight * image)
    block_ref[rows:] = jnp.broadcast_to(share(grad, quad, image, weight, scratch, part), (8, NY))
    copies = send_all(block_ref, far_ref, sems)
    grad_ref[...] = grad
    line_ref[...] = line
    image_ref[...] = image
    for copy in copies:
        copy.wait()


def part_kernel(nxy, got_ref, plane_ref, share_ref):
    rows = NX // nxy
    total = got_ref[0, rows:, :]
    for source in range(1, nxy):
        total = total + got_ref[source, rows:, :]
    share_ref[...] = total
    for source in range(nxy):
        plane_ref[source * rows : (source + 1) * rows] = got_ref[source, :rows, :]


def add_kernel(*refs):
    total = refs[0][...]
    for part in refs[1:-1]:
        total = total + part[...]
    refs[-1][...] = total


def second_kernel(
    s0, s1, s2, s3, dens_ref, full_ref, g0, g1, g2, g3, decay_ref, gx_ref, gy_ref, fx, bx, ty,
    out_ref, dens_out, base_out, alpha_ref, all_ref,
):
    gather_rows((g0, g1, g2, g3), all_ref)
    alpha = step_length(s0[:1] + s1[:1] + (s2[:1] + s3[:1]))
    alpha_ref[...] = jnp.broadcast_to(alpha, alpha_ref.shape)
    old = dens_ref[...]
    grad = g0[...]
    dens = old - alpha * grad
    dens_out[...] = dens
    data = grad - 0.5 * ((1.0 / (old * old + 0.25)) * old)
    base_out[...] = data + 0.5 * (dens * (1.0 / (dens * dens + 0.25)))
    dens = full_ref[...] - alpha * all_ref[...]
    all_ref[...] = 0.5 * (dens * (1.0 / (dens * dens + 0.25)))
    plane = forward_plane(all_ref[...], decay_ref, gx_ref, gy_ref, fx, bx, ty)
    out_ref[...] = plane.reshape(out_ref.shape)


def sum_kernel(nxy, got_ref, half_ref, sum_ref):
    rows = NX // nxy
    total = got_ref[0]
    for source in range(1, nxy):
        total = total + got_ref[source]
    sum_ref[:rows] = total
    sum_ref[rows:] = half_ref[...]


def second_gradient_kernel(
    u0, u1, alpha_ref, base_ref, dens_ref, line_ref, grad_ref, image_ref, share_ref
):
    alpha = alpha_ref[:1, :1]
    total = u0[...] + u1[...]
    dens = dens_ref[...]
    grad = base_ref[...] - alpha * total[:QX]
    quad = 1.0 / (dens * dens + 0.25)
    grad_ref[...] = grad
    image_ref[...] = line_ref[...] - alpha * total[QX:]
    square = grad * grad
    lane = lax.broadcasted_iota(jnp.int32, (8, NY), 1)
    share_ref[...] = jnp.where(
        lane == 0, jnp.sum(square), jnp.where(lane == 1, jnp.sum(quad * square), 0.0)
    )


def curvature_kernel(nh, part, *refs):
    parts = refs[:nh]
    image_ref, weight_ref, share_ref, out_ref, scratch = refs[nh:]
    rows = image_ref.shape[0]
    total = parts[0][...]
    for piece in parts[1:]:
        total = total + piece[...]
    image = image_ref[...] + total[:rows]
    scratch[...] = image
    out_ref[...] = scratch[pl.ds(pl.multiple_of(lax.axis_index("h") * part, part), part), :]
    mine = weight_ref[...] * image
    lane = lax.broadcasted_iota(jnp.int32, (1, 128), 1)
    share_ref[...] = jnp.broadcast_to(
        jnp.where(lane == 2, jnp.sum(mine * mine), total[rows : rows + 1, :128]), share_ref.shape
    )


def finish_kernel(
    shares_ref, dens_ref, grad_ref, alpha_ref, error_ref, first_ref, second_ref, w_ref, dens_out, err_out
):
    part = w_ref.shape[0]
    alpha = step_length(shares_ref[...])
    dens_out[0] = dens_ref[...] - alpha * grad_ref[...]
    place = pl.ds(pl.multiple_of(lax.axis_index("h") * part, part), part)
    error = error_ref[place, :] - alpha_ref[:1, :1] * first_ref[place, :]
    err_out[0] = w_ref[...] * (error - alpha * second_ref[...])


VMEM = pl.BlockSpec(memory_space=pltpu.VMEM)
SMEM = pl.BlockSpec(memory_space=pltpu.SMEM)
ANY = pl.BlockSpec(memory_space=pl.ANY)
FAR = pl.BlockSpec(memory_space=pltpu.HBM)


class Program:
    def __init__(self):
        self.alive = []

    def hold(self, *values):
        self.alive += values

    def drop(self, *values):
        self.alive = [item for item in self.alive if all(item is not value for value in values)]

    def call(self, kernel, outs, *args, scratch=(), scalars=(), far=(), far_out=(), sems=0, mib=8):
        used = len(args)
        keep = [item for item in self.alive if all(item is not value for value in args)]
        kept = len(keep)

        def inner(*refs):
            kernel(*refs[:used], *refs[used + kept :])

        args = [
            pltpu.with_memory_space_constraint(item, pltpu.HBM) if place in far else item
            for place, item in enumerate(args)
        ]
        kinds = [(item, F32) if isinstance(item, tuple) else (item.shape, item.dtype) for item in outs]
        return pl.pallas_call(
            inner,
            out_shape=[
                (pltpu.HBM if place in far_out else jax.ShapeDtypeStruct)(*kind)
                for place, kind in enumerate(kinds)
            ],
            in_specs=[
                SMEM if place in scalars else FAR if place in far else VMEM
                for place in range(used)
            ]
            + [ANY] * kept,
            out_specs=[FAR if place in far_out else VMEM for place in range(len(outs))],
            scratch_shapes=[pltpu.VMEM(shape, F32) for shape in scratch]
            + [pltpu.SemaphoreType.DMA((sems,) if sems > 1 else ())] * (sems > 0),
            compiler_params=pltpu.CompilerParams(vmem_limit_bytes=mib << 20),
        )(*args, *keep)


def from_comps(values):
    return [values[0]] + [
        lax.ppermute(values[step], COMP, [(i, i ^ step) for i in range(4)]) for step in (1, 2, 3)
    ]


def flip(value, axis):
    return lax.ppermute(value, axis, [(0, 1), (1, 0)])


def gather_comps(value):
    across = flip(value, "l")
    return [value, flip(value, "k"), across, flip(across, "k")]


def from_axis(values, axis):
    size = len(values)
    got = {0: values[0]}
    for step in sorted(range(1, size), key=lambda step: min(step, size - step)):
        got[step] = lax.ppermute(values[step], axis, [(i, (i + step) % size) for i in range(size)])
    return [got[step] for step in range(size)]


def exchange(value, axes):
    return lax.all_to_all(value, axes, 0, 0, tiled=True)


def after(values, *others):
    if isinstance(values, (list, tuple)):
        return list(lax.optimization_barrier((tuple(values), others))[0])
    return lax.optimization_barrier((values, others))[0]


def body(density, observed, data_weight, layer_top):
    nx, ny, nh = (lax.axis_size(axis) for axis in DEPTH)
    nxy = nx * ny
    rows = NX // nxy
    part = rows // nh
    fx, ty = (jnp.asarray(table) for table in make_tables())
    bind = functools.partial
    program = Program()
    call = program.call

    near, across = flip(density[0], "k"), flip(density[0], "l")
    *tables, dens, decay, gx, gy = call(
        prepare_kernel,
        [fx, fx, ty, (QX, NY), (KEPT, NY), (KEPT, NY), (KEPT, NY)],
        layer_top, fx, ty, density, scalars=(0,), far=(1, 2, 3), sems=3,
    )
    layers = [near, across, flip(after(across, dens), "k")]
    factors = (decay, gx, gy)
    weight_own, obs_own = data_weight[0], observed[0]
    program.hold(*tables, *factors, dens)
    message, full = call(
        bind(start_kernel, nxy), [(nxy, 2 * rows + 8, NY), (NX, NY)],
        dens, *layers, layer_top, *factors, *tables,
        scratch=[(NX, NY)] * 2, scalars=(4,), far_out=(1,), sems=1,
    )
    got = exchange(message, XY)
    (sums,) = call(
        bind(collect_kernel, nxy), [(2 * rows + nxy // 2 + part, NY)], got, weight_own, obs_own
    )
    sums = from_axis([sums] * nh, "h")
    error, pulled, weight, tops, message = call(
        bind(residual_kernel, nxy, nh),
        [(rows, NY), (rows, NY), (rows, NY), (nxy * nh // 2, NY), (nxy, rows, NY)],
        *sums, scratch=[(rows, NY)], far_out=(4,), sems=nxy,
    )
    program.hold(error, pulled, weight)
    got = exchange(message, XY)
    (power,) = call(bind(power_kernel, nxy * nh), [(KEPT, NY)], tops)
    program.hold(power)
    adjoint = lambda plane: call(
        bind(adjoint_kernel, nxy), [(2 * (QX + rows), NY)] * 2,
        plane.reshape(NX, NY), *factors, power, *tables,
        scratch=[(NX, NY), (4 * rows, NY)],
    )

    def reduce_comps(own, other):
        near, far = call(pair_kernel, [(QX + rows, NY)] * 2, own, flip(other, "k"))
        return near, flip(far, "l")

    pieces = reduce_comps(*adjoint(got))
    message, grad, line, image = call(
        bind(gradient_kernel, nxy, nh),
        [(nxy, rows + 8, NY), (QX, NY), (rows, NY), (rows, NY)],
        *pieces, pulled, dens, weight,
        scratch=[(rows, NY), (rows + 8, NY)], far_out=(0,), sems=nxy,
    )
    program.drop(pulled)
    program.hold(line, image)
    grads = gather_comps(grad)
    got = after(exchange(message, XY), *grads)
    plane, shares = call(bind(part_kernel, nxy), [(NX, NY), (8, NY)], got)
    pieces = adjoint(plane)
    shares = after(from_axis([shares] * nh, "h"), *pieces)
    (shares,) = call(add_kernel, [(8, NY)], *shares)
    shares = gather_comps(shares)
    message, dens, base, alpha = call(
        second_kernel, [(nxy, rows, NY), (QX, NY), (QX, NY), (8, 128)],
        *shares, dens, full, *grads, *factors, *tables, scratch=[(NX, NY)],
    )
    program.alive = [weight, error, line, image, dens, base, alpha]
    got = exchange(message, XY)
    pieces = reduce_comps(*after(pieces, message))
    grad2, image2, half = call(
        second_gradient_kernel, [(QX, NY), (rows, NY), (8, NY)],
        *pieces, alpha, base, dens, line,
    )
    (parts,) = call(bind(sum_kernel, nxy), [(rows + 8, NY)], got, half)
    program.alive = [error, image, dens, alpha, grad2]
    shares, image2 = call(
        bind(curvature_kernel, nh, part), [(nxy * 4, 128), (part, NY)],
        *from_axis([parts] * nh, "h"), image2, weight, scratch=[(rows, NY)],
    )
    shares = exchange(shares, (*XY, *COMP))
    program.alive = []
    return tuple(
        call(
            finish_kernel, [density.shape, observed.shape],
            shares, dens, grad2, alpha, error, image, image2, weight_own,
        )
    )


def solution(mesh):
    depth = mesh.shape["depth"]
    sizes = {64: (4, 4, 4), 4: (2, 1, 2)}[depth]
    fine = Mesh(mesh.devices.reshape(*sizes, 2, 2), ALL)
    data = P(COMP, DEPTH, None)
    layer = P(DEPTH, COMP, None)
    return jax.shard_map(
        body,
        mesh=fine,
        in_specs=(layer, data, data, P(DEPTH)),
        out_specs=(layer, data),
        check_vma=False,
    )
```
